512 devices in a mesh: dp: 32 (over z, core), shard: 16 (over y, x).
Axes of the slice: x: 4, y: 4, z: 16, core: 2. Of those that a mesh axis runs over, the one named last changes fastest.
Arguments:
- tokens: bfloat16 [196608, 512], P(('dp', 'shard')), may hold values from -24 to 24
- w_proj: bfloat16 [512, 2048], P(None, 'shard'), may hold values from -0.25 to 0.25
- w_out: bfloat16 [512, 512], replicated, may hold values from -0.25 to 0.25
- item_rows: bfloat16 [16384, 512], P('shard'), may hold values from -1.5 to 1.5
- lengths: int32 [512, 4], P(('dp', 'shard')), may hold values from 1 to 192, 384 in all within a row
- target_owner: int32 [196608, 1], P(('dp', 'shard')), may hold values from 0 to 15; in each aligned block of 384 rows (0 to 383, 384 to 767, ...) at most 48 rows name the same one
- target_row: int32 [196608], P(('dp', 'shard')), may hold values from 0 to 1023
- negative_rows: int32 [1024], P('shard'), may hold values from 0 to 1023
Outputs:
- grad_tokens: bfloat16 [196608, 512], P(('dp', 'shard'))
- weight_grads: float32 [512, 512], replicated
- item_grads: float32 [16384, 512], P('shard')
The draws below stay inside these ranges and needn't reach their ends.
Inputs may be any that keep to these rules, and one draw needn't show every extreme that they name: `target_owner`: in the rows of one device no owner is named more than 48 times, a bound that some block reaches.
All inputs are finite; a program needn't handle non-finite values.
Results may differ from the reference program's by a relative error of at most 0.02.
Values may be sent and summed in bfloat16 or wider, within the bound.
No kernel may reach another device: no remote copies, remote signals or barrier semaphores. Data moves between devices by JAX's collectives and lax.ppermute only.
A program may use at most 64 MiB of HBM per device.

```python
import math
import jax
import jax.numpy as jnp
import numpy as np
from jax import lax

D = 512
HEADS = 4
DH = 128
TOK_DEV = 384
HIST_DEV = 4
MAXLEN = 192
ROWS_DEV = 1024
NEG_DEV = 64
CAP = 48
TOKENS = 196608
ITEMS = 16384
NEGS = 1024
N_DP = 32
N_SHARD = 16
DEVICES = 512


def scaled_draw(key, rows_count, factor):
    base_key, row_key, col_key = jax.random.split(key, 3)
    row_scale = jnp.exp(jax.random.uniform(row_key, (rows_count, 1), minval=math.log(0.3), maxval=math.log(3.0)))
    col_scale = jnp.exp(jax.random.uniform(col_key, (1, D), minval=math.log(0.5), maxval=math.log(2.0)))
    base_values = jnp.clip(jax.random.normal(base_key, (rows_count, D)), -4.0, 4.0)
    return (base_values * row_scale * col_scale * factor).astype(jnp.float32)


def draw_tokens(key, part):
    return scaled_draw(jax.random.fold_in(key, 11), TOKENS, 1.0).astype(jnp.bfloat16)


def draw_item_rows(key, part):
    return scaled_draw(jax.random.fold_in(key, 23), ITEMS, 0.0625).astype(jnp.bfloat16)


def with_ends(drawn, own_key, least, largest):
    longest = drawn.shape.index(max(drawn.shape))
    spots = []
    for shift in (0, 1):
        where = [jax.random.randint(jax.random.fold_in(own_key, axis), (), 0, length) for axis, length in enumerate(drawn.shape)]
        where[longest] = (where[longest] + shift) % drawn.shape[longest]
        spots.append(tuple(where))
    return drawn.at[spots[0]].set(least).at[spots[1]].set(largest)


def levels(rng, shape, pieces, smallest, top_value):
    level, own = 1.0, jax.random.fold_in(rng, 6)
    for dim, shards_of in pieces:
        steps = jnp.exp(jax.random.uniform(jax.random.fold_in(own, dim), (shards_of,), jnp.float32, smallest / len(pieces), top_value / len(pieces)))
        level = level * jnp.repeat(steps, shape[dim] // shards_of).reshape([-1 if axis == dim else 1 for axis in range(len(shape))])
    return level


def profile(number_of, total, reach, skew):
    weights = [(1 << 20) // math.isqrt(rank ** skew) + 1 for rank in range(2, number_of + 1)]
    spare, given = total - reach - (number_of - 1), [1] * (number_of - 1)
    while spare > 0:
        free = [i for i in range(number_of - 1) if given[i] < reach]
        whole, remaining = sum([weights[i] for i in free]), spare
        for i in free:
            more = min(reach - given[i], max(1, remaining * weights[i] // whole), spare)
            given[i] = given[i] + more
            spare = spare - more
    return np.array([reach] + given)


def ragged_sizes(stream_key, number_of, total, bound, slope):
    if number_of == 2:
        one = jax.random.randint(stream_key, (), max(1, total - bound), min(bound, total - 1) + 1)
        return jnp.stack([one, total - one])
    tallies = jnp.asarray(profile(number_of, total, bound, slope), jnp.int32)
    couples = (number_of - 1) // 2
    giver, sink = tallies[1:1 + 2 * couples:2], tallies[2:2 + 2 * couples:2]
    margin = jnp.minimum(giver - 1, bound - sink)
    passed = jax.random.randint(jax.random.fold_in(stream_key, 1), (couples,), 0, 1 << 20) % (margin + 1)
    tallies = tallies.at[1:1 + 2 * couples:2].set(giver - passed).at[2:2 + 2 * couples:2].set(sink + passed)
    return tallies[jax.random.permutation(jax.random.fold_in(stream_key, 2), number_of)]


def shared_out(own_key, own, number, rows, count, top, most, skew):
    ranking = jax.random.permutation(own_key, count)
    heavy_load, usual = load_shares(count, rows * top, most, skew, True), load_shares(count, rows * top, most, skew, False)
    places = jnp.arange(count)

    def named(sizes, offset_by):
        used = int((sizes > 0).sum())
        fixed = max(1, used // 4)
        passed = fixed + (places - fixed + offset_by * (used - fixed)) % max(1, count - fixed)
        return jnp.zeros((count,), jnp.int32).at[ranking[jnp.where(places < fixed, places, passed)]].set(jnp.asarray(sizes, jnp.int32))

    sizes = jnp.where(number % 4 == 0, named(heavy_load, number // 4), named(usual, number - number // 4 - 1))
    mixed = jax.random.permutation(jax.random.fold_in(own, 3), count)
    giver, sink = mixed[0:count // 2 * 2:2], mixed[1:count // 2 * 2:2]
    margin = jnp.minimum(sizes[giver] - 1, most - sizes[sink]) // 2
    margin = jnp.where((giver == ranking[0]) | (sink == ranking[0]) | (sizes[sink] == 0), 0, jnp.maximum(margin, 0))
    passed = jax.random.randint(jax.random.fold_in(own, 4), (count // 2,), 0, 1 << 20) % (margin + 1)
    sizes = sizes.at[giver].add(-passed).at[sink].add(passed)
    items = jnp.searchsorted(jnp.cumsum(sizes), jnp.arange(rows * top), side="right").astype(jnp.int32)
    table = items.reshape(top, rows).T
    table = table[jax.random.permutation(jax.random.fold_in(own, 1), rows)]
    offset_by = jax.random.randint(jax.random.fold_in(own, 2), (rows, 1), 0, top)
    return jnp.take_along_axis(table, (jnp.arange(top)[None, :] + offset_by) % top, axis=1)


def load_shares(number_of, total, reach, slope, full):
    portions = [(1 << 20) // math.isqrt(standing ** slope) + 1 for standing in range(1, number_of + 1)]
    largest = reach if full else min(reach, max(-(-total // number_of), total * portions[0] // sum(portions)))
    least = 1 if total - largest >= number_of - 1 else 0
    counts, rest = [largest] + [least] * (number_of - 1), total - largest - least * (number_of - 1)
    while rest > 0:
        movable = [i for i in range(1, number_of) if counts[i] < largest] or [i for i in range(1, number_of) if counts[i] < reach]
        pool, remaining = sum([portions[i] for i in movable]), rest
        for i in movable:
            more = min(reach - counts[i], max(1, remaining * portions[i] // pool), rest)
            counts[i] = counts[i] + more
            rest = rest - more
    return np.array(counts)


def noise(own_key, dims, deviation, bound, cuts=(), kind=jnp.bfloat16):
    values = jax.random.normal(own_key, dims, jnp.float32) * deviation
    if len(cuts) > 0:
        values = levels(own_key, dims, cuts, -0.22, 0.18) * values
    return jnp.clip(values, min=-bound, max=bound).astype(kind)


def setup_inputs(seed: int = 0) -> dict:
    arg_keys = jax.random.split(jax.random.key(seed), 9)
    tokens = draw_tokens(jax.random.fold_in(arg_keys[8], 71), 0)
    w_proj = noise(arg_keys[1], (D, 4 * D), D ** -0.5, 0.25, ((1, 16),))
    w_out = noise(arg_keys[2], (D, D), D ** -0.5, 0.25)
    item_rows = draw_item_rows(jax.random.fold_in(arg_keys[8], 71), 0)
    lengths = jax.vmap(lambda own: ragged_sizes(own, HIST_DEV, TOK_DEV, MAXLEN, 2))(jax.random.split(arg_keys[4], DEVICES)).reshape((DEVICES, HIST_DEV)).astype(jnp.int32)
    target_owner_keys = jax.random.split(jax.random.fold_in(arg_keys[5], 1), TOKENS // TOK_DEV)
    target_owner_turns = jax.random.permutation(jax.random.fold_in(arg_keys[5], 3), TOKENS // TOK_DEV)
    target_owner = jax.vmap(lambda own, number: shared_out(jax.random.fold_in(arg_keys[5], 2), own, number, TOK_DEV, N_SHARD, 1, CAP, 1))(target_owner_keys, target_owner_turns).reshape((TOKENS, 1))
    target_row = with_ends(jax.random.randint(arg_keys[6], (TOKENS,), 0, ROWS_DEV), jax.random.fold_in(arg_keys[6], 1), 0, ROWS_DEV - 1).astype(jnp.int32)
    negative_rows = with_ends(jax.random.randint(arg_keys[7], (NEGS,), 0, ROWS_DEV), jax.random.fold_in(arg_keys[7], 1), 0, ROWS_DEV - 1).astype(jnp.int32)
    return dict(tokens=tokens, w_proj=w_proj, w_out=w_out, item_rows=item_rows, lengths=lengths, target_owner=target_owner, target_row=target_row, negative_rows=negative_rows)


epsilon = 1e-06
logit_divisor = 0.015625
loss_scale = 512.0

def reduce_last_dimension(operand, other_side):
    return lax.dot_general(operand, other_side, (((1,), (1,)), ((), ())), preferred_element_type=jnp.float32)

def contract_first(operand, other_side):
    return lax.dot_general(operand, other_side, (((0,), (0,)), ((), ())), preferred_element_type=jnp.float32)

def silu_slope(values):
    sigmoid = jax.nn.sigmoid(values)
    return sigmoid * (1.0 + values * (1.0 - sigmoid))

def history_mask(lengths_row, rows_count):
    history_ends = jnp.cumsum(lengths_row).astype(jnp.int32)
    positions = jnp.arange(rows_count, dtype=jnp.int32)
    history_ids = lax.optimization_barrier(jnp.sum((positions[:, None] >= history_ends[None, :-1]).astype(jnp.int32), axis=1))
    visible = (history_ids[:, None] == history_ids[None, :]) & (positions[None, :] <= positions[:, None])
    return jnp.where(visible, 1.0, 0.0).astype(jnp.float32)

def head_columns(activated, section, head_index):
    first_col = section * D + head_index * DH
    return activated[:, first_col:first_col + DH]

def head_scores(queries, key_rows):
    return reduce_last_dimension(queries, key_rows) * DH ** (-0.5)

def head_weights(scores, visible):
    return (jax.nn.silu(scores) * visible * (1.0 / MAXLEN)).astype(jnp.bfloat16)

def forward_layer(tokens, project, w_out, visible):
    wide_tokens = tokens.astype(jnp.float32)
    input_scale = lax.rsqrt(lax.optimization_barrier(jnp.mean(wide_tokens * wide_tokens, axis=1, keepdims=True)) + epsilon)
    normed = (wide_tokens * input_scale).astype(jnp.bfloat16)
    pre_act = project(normed)
    activated = lax.optimization_barrier(jax.nn.silu(pre_act).astype(jnp.bfloat16))
    heads_out = []
    for head_index in range(HEADS):
        queries = head_columns(activated, 2, head_index)
        key_rows = head_columns(activated, 3, head_index)
        value_rows = head_columns(activated, 1, head_index)
        weights = head_weights(head_scores(queries, key_rows), visible)
        heads_out.append(jnp.dot(weights, value_rows, preferred_element_type=jnp.float32))
    joined = lax.optimization_barrier(jnp.concatenate(heads_out, axis=1).astype(jnp.bfloat16))
    joined_wide = joined.astype(jnp.float32)
    middle_scale = lax.rsqrt(lax.optimization_barrier(jnp.mean(joined_wide * joined_wide, axis=1, keepdims=True)) + epsilon)
    gate_wide = activated[:, :D].astype(jnp.float32)
    gated = (joined_wide * middle_scale * gate_wide).astype(jnp.bfloat16)
    layer_out = wide_tokens + jnp.dot(gated, w_out, preferred_element_type=jnp.float32)
    return (layer_out, (wide_tokens, input_scale, pre_act, activated, joined, middle_scale, gated))

def loss_head(layer_out, clicked_product_vectors, sampled_decoys):
    out_scale = lax.rsqrt(lax.optimization_barrier(jnp.sum(layer_out * layer_out, axis=1, keepdims=True)) + epsilon)
    normalized_example_vectors = lax.optimization_barrier((layer_out * out_scale).astype(jnp.bfloat16))
    normalized_complete_embedding = normalized_example_vectors.astype(jnp.float32)
    correct_logit_entry = lax.optimization_barrier(jnp.sum(normalized_complete_embedding * clicked_product_vectors.astype(jnp.float32), axis=1)) / logit_divisor
    decoy_logit_entries = reduce_last_dimension(normalized_example_vectors, sampled_decoys) / logit_divisor
    target_exp = jnp.exp(correct_logit_entry)
    negative_exp = jnp.exp(decoy_logit_entries)
    totals = target_exp + lax.optimization_barrier(jnp.sum(negative_exp, axis=1))
    target_prob = target_exp / totals
    negative_probs = (loss_scale * negative_exp / totals[:, None]).astype(jnp.bfloat16)
    target_coef = (loss_scale * (target_prob - 1.0))[:, None]
    grad_unit = target_coef * clicked_product_vectors.astype(jnp.float32) + jnp.dot(negative_probs, sampled_decoys, preferred_element_type=jnp.float32)
    grad_out = out_scale * grad_unit - layer_out * out_scale ** 3 * lax.optimization_barrier(jnp.sum(layer_out * grad_unit, axis=1, keepdims=True))
    grad_target = target_coef * normalized_complete_embedding
    return (grad_out, grad_target, negative_probs, normalized_example_vectors)

def backward_layer(grad_out, saved_state, project_back, w_out, visible):
    wide_tokens, input_scale, pre_act, activated, joined, middle_scale, gated = saved_state
    grad_out_b = grad_out.astype(jnp.bfloat16)
    weight_part = contract_first(gated, grad_out_b)
    grad_gated = reduce_last_dimension(grad_out_b, w_out)
    joined_wide = joined.astype(jnp.float32)
    gate_wide = activated[:, :D].astype(jnp.float32)
    grad_gate = grad_gated * joined_wide * middle_scale
    grad_norm = grad_gated * gate_wide
    grad_joined = middle_scale * grad_norm - joined_wide * middle_scale ** 3 * lax.optimization_barrier(jnp.mean(joined_wide * grad_norm, axis=1, keepdims=True))
    grad_joined_b = grad_joined.astype(jnp.bfloat16)
    grad_values = []
    grad_queries = []
    grad_keys = []
    for head_index in range(HEADS):
        queries = head_columns(activated, 2, head_index)
        key_rows = head_columns(activated, 3, head_index)
        value_rows = head_columns(activated, 1, head_index)
        scores = head_scores(queries, key_rows)
        weights = head_weights(scores, visible)
        grad_head = grad_joined_b[:, head_index * DH:(head_index + 1) * DH]
        grad_weights = reduce_last_dimension(grad_head, value_rows)
        grad_values.append(contract_first(weights, grad_head))
        grad_scores = (grad_weights * visible * (1.0 / MAXLEN) * silu_slope(scores) * DH ** (-0.5)).astype(jnp.bfloat16)
        grad_queries.append(jnp.dot(grad_scores, key_rows, preferred_element_type=jnp.float32))
        grad_keys.append(contract_first(grad_scores, queries))
    grad_act = jnp.concatenate([grad_gate] + grad_values + grad_queries + grad_keys, axis=1)
    grad_pre = (grad_act * silu_slope(pre_act)).astype(jnp.bfloat16)
    grad_normed = project_back(grad_pre)
    grad_input = input_scale * grad_normed - wide_tokens * input_scale ** 3 * lax.optimization_barrier(jnp.mean(wide_tokens * grad_normed, axis=1, keepdims=True))
    return ((grad_out + grad_input).astype(jnp.bfloat16), weight_part)

def reference(tokens, w_proj, w_out, item_rows, lengths, target_owner, target_row, negative_rows):
    block_count = N_DP * N_SHARD
    block_rows = TOK_DEV
    rows_wide = item_rows.astype(jnp.float32)
    item_scale = lax.rsqrt(lax.optimization_barrier(jnp.sum(rows_wide * rows_wide, axis=1, keepdims=True)) + epsilon)
    unit_items = (rows_wide * item_scale).astype(jnp.bfloat16)
    negative_ids = (jnp.arange(NEGS, dtype=jnp.int32) // NEG_DEV * ROWS_DEV + negative_rows).astype(jnp.int32)
    sampled_decoys = jnp.take(unit_items, negative_ids, axis=0)
    target_ids = (target_owner[:, 0] * ROWS_DEV + target_row).astype(jnp.int32)

    def project(normed):
        return jnp.dot(normed, w_proj, preferred_element_type=jnp.float32)

    def project_back(grad_pre):
        return reduce_last_dimension(grad_pre, w_proj)

    def block_step(running, block_data):
        weight_sum, item_sum, negative_sum = running
        block_tokens, block_lengths, block_ids = block_data
        visible = history_mask(block_lengths, block_rows)
        layer_out, saved_state = forward_layer(block_tokens, project, w_out, visible)
        clicked_product_vectors = jnp.take(unit_items, block_ids, axis=0)
        grad_out, grad_target, negative_probs, normalized_example_vectors = loss_head(layer_out, clicked_product_vectors, sampled_decoys)
        grad_tokens, weight_part = backward_layer(grad_out, saved_state, project_back, w_out, visible)
        item_sum = item_sum.at[block_ids].add(grad_target)
        negative_sum = negative_sum + contract_first(negative_probs, normalized_example_vectors)
        return ((weight_sum + weight_part, item_sum, negative_sum), grad_tokens)
    initial = (jnp.zeros((D, D), jnp.float32), jnp.zeros((ITEMS, D), jnp.float32), jnp.zeros((NEGS, D), jnp.float32))
    block_data = (tokens.reshape(block_count, block_rows, D), lengths, target_ids.reshape(block_count, block_rows))
    finals, grad_tokens = lax.scan(block_step, initial, block_data)
    weight_sum, item_sum, negative_sum = finals
    grad_items = item_sum.at[negative_ids].add(negative_sum)
    item_grads = (item_scale * grad_items - rows_wide * item_scale ** 3 * lax.optimization_barrier(jnp.sum(rows_wide * grad_items, axis=1, keepdims=True))) / loss_scale
    return (grad_tokens.reshape(TOKENS, D), weight_sum / loss_scale, item_grads)
```

```python
import jax
import jax.numpy as jnp
from jax import lax
from jax.sharding import PartitionSpec as P

D = 512
HEADS = 4
DH = 128
MAXLEN = 192
SECTIONS = 4 * HEADS

epsilon = 1e-06
logit_divisor = 0.015625
loss_scale = 512.0

F32 = jnp.float32
BF16 = jnp.bfloat16


def dot(a, b, contract, batch=((), ())):
    return lax.dot_general(a, b, (contract, batch), preferred_element_type=F32)


def silu_slope(values):
    sigmoid = jax.nn.sigmoid(values)
    return sigmoid * (1.0 + values * (1.0 - sigmoid))


def history_mask(lengths_row, rows_count):
    history_ends = jnp.cumsum(lengths_row)
    positions = jnp.arange(rows_count, dtype=jnp.int32)
    history_ids = jnp.sum((positions[:, None] >= history_ends[None, :-1]).astype(jnp.int32), axis=1)
    return (history_ids[:, None] == history_ids[None, :]) & (
        positions[None, :] <= positions[:, None]
    )


def exchange(pieces, axis, groups=None):
    return lax.all_to_all(
        pieces, axis, split_axis=0, concat_axis=0, tiled=True, axis_index_groups=groups
    )


def gather_from(piece, axis, count, groups=None):
    return exchange(jnp.broadcast_to(piece[None], (count,) + piece.shape), axis, groups)


def add_up(received):
    return jnp.sum(received.astype(F32), axis=0)


def shards(tokens, w_proj, w_out, item_rows, lengths, target_owner, target_row, negative_rows):
    tok_rows = tokens.shape[0]
    width = tokens.shape[1]
    item_count = item_rows.shape[0]
    dp = lax.axis_size("dp")
    owners_count = lax.axis_size("shard")
    capacity = 2 * tok_rows // owners_count
    slots = owners_count * capacity
    own_negs = negative_rows.shape[0]
    negs = owners_count * own_negs
    zs = dp // 2
    lo = 4
    hi = zs // lo
    pair = [[2 * z, 2 * z + 1] for z in range(zs)]
    near = [[2 * (lo * h + l) + c for l in range(lo)] for h in range(hi) for c in range(2)]
    far = [[2 * (lo * h + l) + c for h in range(hi)] for l in range(lo) for c in range(2)]

    owners = target_owner
    hits = owners == lax.broadcasted_iota(jnp.int32, (tok_rows, owners_count), 1)
    t_row = lax.broadcasted_iota(jnp.int32, (tok_rows, tok_rows), 0)
    t_col = lax.broadcasted_iota(jnp.int32, (tok_rows, tok_rows), 1)
    before = dot((t_col < t_row).astype(BF16), hits.astype(BF16), ((1,), (0,)))
    slot_index = jnp.sum(jnp.where(hits, before, 0.0), axis=1, keepdims=True).astype(jnp.int32)
    position = owners * capacity + slot_index
    placed = position == lax.broadcasted_iota(jnp.int32, (tok_rows, slots), 1)
    requests = jnp.sum(jnp.where(placed, target_row[:, None], 0), axis=0)
    placed = placed.astype(BF16)
    asked = exchange(requests.reshape(owners_count, capacity), "shard").reshape(slots, 1)

    w_all = gather_from(w_proj, "shard", owners_count)

    rows_wide = item_rows.astype(F32)
    item_scale = lax.rsqrt(jnp.sum(rows_wide * rows_wide, axis=1, keepdims=True) + epsilon)
    unit_items = (rows_wide * item_scale).astype(BF16)
    own_pick = (
        negative_rows[:, None] == lax.broadcasted_iota(jnp.int32, (own_negs, item_count), 1)
    ).astype(BF16)
    decoys = gather_from(
        dot(own_pick, unit_items, ((1,), (0,))).astype(BF16), "shard", owners_count
    ).reshape(negs, width)
    asked_pick = (asked == lax.broadcasted_iota(jnp.int32, (slots, item_count), 1)).astype(BF16)
    served = dot(asked_pick, unit_items, ((1,), (0,))).astype(BF16)
    fetched = exchange(served.reshape(owners_count, capacity, width), "shard").reshape(slots, width)

    visible = history_mask(lengths[0], tok_rows)[None]
    wide_tokens = tokens.astype(F32)
    input_scale = lax.rsqrt(jnp.mean(wide_tokens * wide_tokens, axis=1, keepdims=True) + epsilon)
    normed = (wide_tokens * input_scale).astype(BF16)
    normed_s = jnp.broadcast_to(normed[None], (SECTIONS, tok_rows, width))
    pre_act = dot(normed_s, w_all, ((2,), (1,)), ((0,), (0,)))
    activated = jax.nn.silu(pre_act).astype(BF16)
    gate, values, queries, keys = (activated[i * HEADS : (i + 1) * HEADS] for i in range(4))
    scores = dot(queries, keys, ((2,), (2,)), ((0,), (0,))) * DH ** (-0.5)
    score_sig = jax.nn.sigmoid(scores)
    weights = jnp.where(visible, scores * score_sig * (1.0 / MAXLEN), 0.0).astype(BF16)
    joined = dot(weights, values, ((2,), (1,)), ((0,), (0,))).astype(BF16)
    joined_wide = joined.astype(F32)
    middle_scale = lax.rsqrt(
        jnp.sum(joined_wide * joined_wide, axis=(0, 2), keepdims=True) / width + epsilon
    )
    gate_wide = gate.astype(F32)
    gated = (joined_wide * middle_scale * gate_wide).astype(BF16)
    w_out_h = w_out.reshape(HEADS, DH, width)
    layer_out = wide_tokens + jnp.sum(dot(gated, w_out_h, ((2,), (1,)), ((0,), (0,))), axis=0)

    clicked = dot(placed, fetched, ((1,), (0,)))
    out_scale = lax.rsqrt(jnp.sum(layer_out * layer_out, axis=1, keepdims=True) + epsilon)
    unit_b = (layer_out * out_scale).astype(BF16)
    unit_wide = unit_b.astype(F32)
    target_logit = jnp.sum(unit_wide * clicked, axis=1, keepdims=True) / logit_divisor
    negative_logits = dot(unit_b, decoys, ((1,), (1,))) / logit_divisor
    target_exp = jnp.exp(target_logit)
    negative_exp = jnp.exp(negative_logits)
    totals = target_exp + jnp.sum(negative_exp, axis=1, keepdims=True)
    negative_probs = (negative_exp * (loss_scale / totals)).astype(BF16)
    target_coef = loss_scale * (target_exp / totals - 1.0)
    grad_target = (target_coef * unit_wide).astype(BF16)
    outgoing = dot(placed, grad_target, ((0,), (0,))).astype(BF16)
    grad_negs = dot(negative_probs, unit_b, ((0,), (0,))).astype(BF16)
    grad_unit = target_coef * clicked + dot(negative_probs, decoys, ((1,), (0,)))
    grad_out = out_scale * grad_unit - layer_out * out_scale**3 * jnp.sum(
        layer_out * grad_unit, axis=1, keepdims=True
    )
    grad_out_b = grad_out.astype(BF16)
    weight_part = dot(gated, grad_out_b, ((1,), (0,))).astype(BF16).reshape(width, width)

    halves = jnp.concatenate(
        [
            grad_negs.reshape(owners_count, 2, own_negs // 2, width),
            weight_part.reshape(owners_count, 2, width // owners_count // 2, width),
        ],
        axis=2,
    ).transpose(1, 0, 2, 3)
    of_pair = add_up(exchange(halves, "dp", pair)).astype(BF16)
    back = exchange(
        jnp.concatenate([outgoing.reshape(owners_count, capacity, width), of_pair], axis=1), "shard"
    )
    half_negs = own_negs // 2
    returned = back[:, :capacity].reshape(slots, width)
    neg_and_w = add_up(back[:, capacity:])
    neg_half = neg_and_w[:half_negs].astype(BF16)
    w_part = neg_and_w[half_negs:].astype(BF16)
    core = lax.rem(lax.axis_index("dp"), 2)
    half_rows = lax.dynamic_slice_in_dim(negative_rows, core * half_negs, half_negs)
    half_pick = (
        lax.broadcasted_iota(jnp.int32, (item_count, half_negs), 0) == half_rows[None, :]
    ).astype(BF16)
    dense = dot(asked_pick, returned, ((0,), (0,))) + dot(half_pick, neg_half, ((1,), (0,)))
    part = add_up(exchange(dense.astype(BF16).reshape(2, item_count // 2, width), "dp", pair))

    def with_w(rows, w_rows, count):
        pieces = rows.astype(BF16).reshape(count, -1, width)
        shared = jnp.broadcast_to(w_rows.astype(BF16)[None], (count,) + w_rows.shape)
        got = add_up(exchange(jnp.concatenate([pieces, shared], axis=1), "dp", near if count == lo and rows.shape[0] == item_count // 2 else far))
        own = pieces.shape[1]
        return got[:own], got[own:]

    part, w_part = with_w(part, w_part, lo)
    part, w_part = with_w(part, w_part, hi)
    part = gather_from(part.astype(BF16), "dp", hi, far).reshape(-1, width)
    part = gather_from(part, "dp", lo, near).reshape(-1, width)
    w_half = gather_from(w_part.astype(BF16), "shard", owners_count)
    both = gather_from(
        jnp.concatenate([part, w_half.reshape(-1, width)], axis=0), "dp", 2, pair
    )
    grad_items = both[:, : item_count // 2].reshape(item_count, width).astype(F32)
    w_sum = both[:, item_count // 2 :].reshape(2, owners_count, -1, width)
    weight_grads = w_sum.transpose(1, 0, 2, 3).reshape(width, width).astype(F32) / loss_scale
    item_grads = (
        item_scale * grad_items
        - rows_wide * item_scale**3 * jnp.sum(rows_wide * grad_items, axis=1, keepdims=True)
    ) / loss_scale

    grad_gated = dot(
        jnp.broadcast_to(grad_out_b[None], (HEADS, tok_rows, width)),
        w_out_h,
        ((2,), (2,)),
        ((0,), (0,)),
    )
    grad_gate = grad_gated * joined_wide * middle_scale
    grad_norm = grad_gated * gate_wide
    grad_joined = middle_scale * grad_norm - joined_wide * middle_scale**3 * (
        jnp.sum(joined_wide * grad_norm, axis=(0, 2), keepdims=True) / width
    )
    grad_joined_b = grad_joined.astype(BF16)
    grad_weights = dot(grad_joined_b, values, ((2,), (2,)), ((0,), (0,)))
    grad_values = dot(weights, grad_joined_b, ((1,), (1,)), ((0,), (0,)))
    slope = score_sig * (1.0 + scores * (1.0 - score_sig))
    grad_scores = jnp.where(
        visible, grad_weights * (1.0 / MAXLEN) * slope * DH ** (-0.5), 0.0
    ).astype(BF16)
    grad_queries = dot(grad_scores, keys, ((2,), (1,)), ((0,), (0,)))
    grad_keys = dot(grad_scores, queries, ((1,), (1,)), ((0,), (0,)))
    grad_act = jnp.concatenate([grad_gate, grad_values, grad_queries, grad_keys], axis=0)
    grad_pre = (grad_act * silu_slope(pre_act)).astype(BF16)
    grad_normed = jnp.sum(dot(grad_pre, w_all, ((2,), (2,)), ((0,), (0,))), axis=0)
    grad_input = input_scale * grad_normed - wide_tokens * input_scale**3 * jnp.mean(
        wide_tokens * grad_normed, axis=1, keepdims=True
    )
    grad_tokens = (grad_out + grad_input).astype(BF16)
    return (grad_tokens, weight_grads, item_grads)


def solution(mesh):
    in_specs = (
        P(("dp", "shard"), None),
        P(None, "shard"),
        P(),
        P("shard", None),
        P(("dp", "shard"), None),
        P(("dp", "shard"), None),
        P(("dp", "shard")),
        P("shard"),
    )
    out_specs = (P(("dp", "shard"), None), P(), P("shard", None))
    return jax.shard_map(shards, mesh=mesh, in_specs=in_specs, out_specs=out_specs, check_vma=False)
```

```python
import functools

import jax
import jax.numpy as jnp
from jax import lax
from jax.experimental import pallas as pl
from jax.experimental.pallas import tpu as pltpu
from jax.sharding import PartitionSpec as P

D = 512
HEADS = 4
DH = 128
MAXLEN = 192
SECTIONS = 4 * HEADS
PLANE = 16
CAP = 48
NEG = 64
WROWS = 32
CHIPS = 16
HALF = 512
PIECE = 32
LANES = 128

epsilon = 1e-06
logit_scale = 64.0
loss_scale = 512.0

F32 = jnp.float32
BF16 = jnp.bfloat16
I32 = jnp.int32


def dot(a, b, contract, batch=((), ())):
    return lax.dot_general(a, b, (contract, batch), preferred_element_type=F32)


def iota(shape, axis):
    return lax.broadcasted_iota(I32, shape, axis)


def one_hot(mask):
    return jnp.where(mask, 1.0, 0.0).astype(BF16)


def silu_slope(values):
    sigmoid = jax.nn.sigmoid(values)
    return sigmoid * (1.0 + values * (1.0 - sigmoid))


def history_mask(lengths_row, rows_count):
    history_ends = jnp.cumsum(lengths_row)
    positions = jnp.arange(rows_count, dtype=jnp.int32)
    history_ids = jnp.sum((positions[:, None] >= history_ends[None, :-1]).astype(jnp.int32), axis=1)
    return (history_ids[:, None] == history_ids[None, :]) & (
        positions[None, :] <= positions[:, None]
    )


def exchange(pieces, axis, groups=None):
    return lax.all_to_all(
        pieces, axis, split_axis=0, concat_axis=0, tiled=True, axis_index_groups=groups
    )


def route_kernel(core_ref, owner_ref, row_ref, w_ref, out_ref, pos_ref):
    tok = owner_ref.shape[0]
    owners = owner_ref[...]
    hits = owners == iota((tok, LANES), 1)
    earlier = one_hot(iota((tok, tok), 1) < iota((tok, tok), 0))
    before = dot(earlier, one_hot(hits), ((1,), (0,)))
    slot = jnp.sum(jnp.where(hits, before, 0.0), axis=1, keepdims=True).astype(I32)
    pos_ref[...] = owners * CAP + slot
    spread = one_hot(owners * LANES + slot == iota((tok, PLANE * LANES), 1))
    asked = jnp.broadcast_to(row_ref[...], (16, tok))
    which = iota((16, tok), 0)
    digits = jnp.where(which == 0, asked >> 5, jnp.where(which == 1, asked & 31, 0))
    requests = dot(digits.astype(F32).astype(BF16), spread, ((1,), (0,))).astype(BF16)
    rows = w_ref.shape[0] // 2
    own = w_ref[pl.ds(pl.multiple_of(core_ref[0] * rows, rows), rows), :]
    for j in range(PLANE):
        out_ref[j, 0:rows, :] = own
        out_ref[j, rows : rows + 16, :] = requests[:, j * LANES : (j + 1) * LANES]


def serve_kernel(recv_ref, items_ref, negs_ref, out_ref, pick_ref):
    rows = recv_ref.shape[1] - 16
    count = items_ref.shape[0]
    diagonal = iota((CAP, LANES), 0) == iota((CAP, LANES), 1)
    for j in range(PLANE):
        digits = recv_ref[j, rows : rows + 16, :].astype(F32)
        asked = 32.0 * digits[0:1] + digits[1:2]
        column = jnp.sum(
            jnp.where(diagonal, jnp.broadcast_to(asked, (CAP, LANES)), 0.0), axis=1, keepdims=True
        ).astype(I32)
        pick_ref[j * CAP : (j + 1) * CAP, :] = one_hot(column == iota((CAP, count), 1))
    negs = negs_ref[...]
    step = 4
    for j in range(0, PLANE, step):
        served = dot(pick_ref[j * CAP : (j + step) * CAP, :], items_ref[...], ((1,), (0,)))
        served = served.astype(BF16)
        for i in range(step):
            out_ref[j + i, 0:CAP, :] = served[i * CAP : (i + 1) * CAP]
            out_ref[j + i, CAP : CAP + NEG, :] = negs


def loss_kernel(
    layer_ref,
    gated_ref,
    recv_ref,
    pos_ref,
    out_ref,
    grad_ref,
    grad_b_ref,
    fetched,
    decoys,
    probs,
    unit,
    back,
):
    tok = layer_ref.shape[0]
    for j in range(PLANE):
        fetched[j * CAP : (j + 1) * CAP, :] = recv_ref[j, 0:CAP, :]
        decoys[j * NEG : (j + 1) * NEG, :] = recv_ref[j, CAP : CAP + NEG, :]
    step = 128
    for c in range(0, tok, step):
        layer_out = layer_ref[c : c + step, :]
        placed = one_hot(pos_ref[c : c + step, :] == iota((step, PLANE * CAP), 1))
        clicked = dot(placed, fetched[...], ((1,), (0,)))
        out_scale = lax.rsqrt(jnp.sum(layer_out * layer_out, axis=1, keepdims=True) + epsilon)
        unit_b = (layer_out * out_scale).astype(BF16)
        unit[c : c + step, :] = unit_b
        unit_wide = unit_b.astype(F32)
        target_exp = jnp.exp(jnp.sum(unit_wide * clicked, axis=1, keepdims=True) * logit_scale)
        negative_exp = jnp.exp(dot(unit_b, decoys[...], ((1,), (1,))) * logit_scale)
        totals = target_exp + jnp.sum(negative_exp, axis=1, keepdims=True)
        negative_probs = (negative_exp * (loss_scale / totals)).astype(BF16)
        probs[c : c + step, :] = negative_probs
        target_coef = loss_scale * (target_exp / totals - 1.0)
        back[c : c + step, :] = (target_coef * unit_wide).astype(BF16)
        grad_unit = target_coef * clicked + dot(negative_probs, decoys[...], ((1,), (0,)))
        along = jnp.sum(layer_out * grad_unit, axis=1, keepdims=True)
        grad_out = out_scale * grad_unit - layer_out * (out_scale**3 * along)
        grad_ref[c : c + step, :] = grad_out
        grad_b_ref[c : c + step, :] = grad_out.astype(BF16)
    across = jnp.broadcast_to(pos_ref[...].astype(F32), (tok, LANES)).T[0:1, :].astype(I32)
    group = 4
    for j in range(0, PLANE, group):
        slots = group * CAP
        placed_t = one_hot(iota((slots, tok), 0) + j * CAP == across)
        sent = dot(placed_t, back[...], ((1,), (0,))).astype(BF16)
        negs = dot(probs[:, j * NEG : (j + group) * NEG], unit[...], ((0,), (0,))).astype(BF16)
        weights = dot(gated_ref[j // group], grad_b_ref[...], ((0,), (0,))).astype(BF16)
        for i in range(group):
            out_ref[j + i, 0:CAP, :] = sent[i * CAP : (i + 1) * CAP]
            out_ref[j + i, CAP : CAP + NEG, :] = negs[i * NEG : (i + 1) * NEG]
            out_ref[j + i, CAP + NEG :, :] = weights[i * WROWS : (i + 1) * WROWS]


def collect_kernel(core_ref, recv_ref, pick_ref, neg_row_ref, keep_ref, send_ref, returned):
    core = core_ref[0]
    negs = jnp.zeros((NEG, D), F32)
    weights = jnp.zeros((WROWS, D), F32)
    for j in range(PLANE):
        returned[j * CAP : (j + 1) * CAP, :] = recv_ref[j, 0:CAP, :]
        negs = negs + recv_ref[j, CAP : CAP + NEG, :].astype(F32)
        weights = weights + recv_ref[j, CAP + NEG :, :].astype(F32)
    negs = negs.astype(BF16)
    step = 256
    for ref, half in ((keep_ref, core), (send_ref, 1 - core)):
        for b in range(0, HALF, step):
            first = pl.multiple_of(half * HALF + b, step)
            here = one_hot(iota((step, NEG), 0) + first == neg_row_ref[...])
            total = dot(pick_ref[:, pl.ds(first, step)], returned[...], ((0,), (0,)))
            total = total + dot(here, negs, ((1,), (0,)))
            ref[b : b + step, :] = total.astype(BF16)
        part = jnp.where(half == 0, weights[0 : WROWS // 2], weights[WROWS // 2 :])
        ref[HALF:, :] = part.astype(BF16)


def pack_kernel(keep_ref, other_ref, out_ref):
    for i in range(CHIPS):
        rows = slice(i * PIECE, (i + 1) * PIECE)
        total = keep_ref[rows, :].astype(F32) + other_ref[rows, :].astype(F32)
        total = total.astype(BF16)
        for q in range(D // LANES):
            out_ref[i, q * PIECE : (q + 1) * PIECE, :] = total[:, q * LANES : (q + 1) * LANES]
    weights = keep_ref[HALF:, :].astype(F32) + other_ref[HALF:, :].astype(F32)
    for i in range(CHIPS):
        row = weights[i : i + 1, :]
        parts = [row[:, q * LANES : (q + 1) * LANES] for q in range(D // LANES)]
        parts.append(jnp.zeros((8 - D // LANES, LANES), F32))
        out_ref[i, D // LANES * PIECE :, :] = jnp.concatenate(parts, axis=0).astype(BF16)


def total_kernel(recv_ref, out_ref):
    total = recv_ref[0].astype(F32)
    for i in range(1, CHIPS):
        total = total + recv_ref[i].astype(F32)
    total = total.astype(BF16)
    for i in range(CHIPS):
        out_ref[i] = total


def weight_kernel(core_ref, mine_ref, other_ref, out_ref):
    first = core_ref[0] == 0
    rows = []
    for half in range(2):
        for i in range(CHIPS):
            mine = mine_ref[i, D // LANES * PIECE :, :].astype(F32)
            other = other_ref[i, D // LANES * PIECE :, :].astype(F32)
            block = jnp.where(first, mine, other) if half == 0 else jnp.where(first, other, mine)
            rows.append(
                jnp.concatenate([block[q : q + 1, :] for q in range(D // LANES)], axis=1)
            )
    gathered = jnp.concatenate(rows, axis=0).astype(BF16)
    for j in range(PLANE):
        out_ref[j] = gathered


def finish_kernel(core_ref, mine_ref, other_ref, items_ref, out_ref):
    def half_rows(source_ref, half):
        for i in range(CHIPS):
            first = pl.multiple_of(half * HALF + i * PIECE, PIECE)
            rows = items_ref[pl.ds(first, PIECE), :].astype(F32)
            grads = jnp.concatenate(
                [source_ref[i, q * PIECE : (q + 1) * PIECE, :] for q in range(D // LANES)], axis=1
            ).astype(F32)
            scale = lax.rsqrt(jnp.sum(rows * rows, axis=1, keepdims=True) + epsilon)
            along = jnp.sum(rows * grads, axis=1, keepdims=True)
            out_ref[pl.ds(first, PIECE), :] = (
                scale * grads - rows * (scale**3 * along)
            ) * (1.0 / loss_scale)

    half_rows(mine_ref, core_ref[0])
    half_rows(other_ref, 1 - core_ref[0])


def local(kernel, outs, operands, scalars=0, scratch=(), flops=0, name=None):
    spaces = [pltpu.SMEM] * scalars + [pltpu.VMEM] * (len(operands) - scalars)
    moved = sum(v.size * v.dtype.itemsize for v in operands) + sum(
        v.size * v.dtype.itemsize for v in outs
    )
    return pl.pallas_call(
        kernel,
        out_shape=tuple(outs),
        in_specs=[pl.BlockSpec(memory_space=s) for s in spaces],
        out_specs=tuple(pl.BlockSpec(memory_space=pltpu.VMEM) for _ in outs),
        scratch_shapes=list(scratch),
        compiler_params=pltpu.CompilerParams(vmem_limit_bytes=56 * 1024 * 1024),
        cost_estimate=pl.CostEstimate(flops=flops, bytes_accessed=moved, transcendentals=0),
        name=name,
    )(*operands)


def shaped(shape, dtype=BF16):
    return jax.ShapeDtypeStruct(shape, dtype)


def shards(tokens, w_proj, w_out, item_rows, lengths, target_owner, target_row, negative_rows):
    tok_rows = tokens.shape[0]
    width = tokens.shape[1]
    item_count = item_rows.shape[0]
    dp = lax.axis_size("dp")
    slots = PLANE * CAP
    negs = PLANE * NEG
    partners = [(i, i ^ 1) for i in range(dp)]
    columns = [[2 * z + c for z in range(CHIPS)] for c in range(2)]
    core = lax.rem(lax.axis_index("dp"), 2).astype(I32)
    core_s = core.reshape(1)

    half_w = width // 2
    first_out, position = local(
        route_kernel,
        [shaped((PLANE, half_w + 16, DH)), shaped((tok_rows, 1), I32)],
        [core_s, target_owner, target_row.reshape(1, tok_rows), w_proj],
        scalars=1,
        name="route",
    )
    first_in = exchange(first_out, "shard")
    w_mine = first_in[:, :half_w]
    w_other = lax.ppermute(w_mine, "dp", partners)

    rows_wide = item_rows.astype(F32)
    item_scale = lax.rsqrt(jnp.sum(rows_wide * rows_wide, axis=1, keepdims=True) + epsilon)
    unit_items = (rows_wide * item_scale).astype(BF16)
    own_pick = (negative_rows[:, None] == iota((NEG, item_count), 1)).astype(BF16)
    own_negs = dot(own_pick, unit_items, ((1,), (0,))).astype(BF16)
    served, asked_pick = local(
        serve_kernel,
        [shaped((PLANE, CAP + NEG, width)), shaped((slots, item_count))],
        [first_in, unit_items, own_negs],
        name="serve",
    )
    looked_up = exchange(served, "shard")

    w_all = jnp.where(
        core == 0,
        jnp.concatenate([w_mine, w_other], axis=1),
        jnp.concatenate([w_other, w_mine], axis=1),
    )
    visible = history_mask(lengths[0], tok_rows)[None]
    wide_tokens = tokens.astype(F32)
    input_scale = lax.rsqrt(jnp.mean(wide_tokens * wide_tokens, axis=1, keepdims=True) + epsilon)
    normed = (wide_tokens * input_scale).astype(BF16)
    normed_s = jnp.broadcast_to(normed[None], (SECTIONS, tok_rows, width))
    pre_act = dot(normed_s, w_all, ((2,), (1,)), ((0,), (0,)))
    activated = jax.nn.silu(pre_act).astype(BF16)
    gate, values, queries, keys = (activated[i * HEADS : (i + 1) * HEADS] for i in range(4))
    scores = dot(queries, keys, ((2,), (2,)), ((0,), (0,))) * DH ** (-0.5)
    score_sig = jax.nn.sigmoid(scores)
    weights = jnp.where(visible, scores * score_sig * (1.0 / MAXLEN), 0.0).astype(BF16)
    joined = dot(weights, values, ((2,), (1,)), ((0,), (0,))).astype(BF16)
    joined_wide = joined.astype(F32)
    middle_scale = lax.rsqrt(
        jnp.sum(joined_wide * joined_wide, axis=(0, 2), keepdims=True) / width + epsilon
    )
    gate_wide = gate.astype(F32)
    gated = (joined_wide * middle_scale * gate_wide).astype(BF16)
    w_out_h = w_out.reshape(HEADS, DH, width)
    layer_out = wide_tokens + jnp.sum(dot(gated, w_out_h, ((2,), (1,)), ((0,), (0,))), axis=0)

    third_out, grad_out, grad_out_b = local(
        loss_kernel,
        [
            shaped((PLANE, CAP + NEG + WROWS, width)),
            shaped((tok_rows, width), F32),
            shaped((tok_rows, width)),
        ],
        [layer_out, gated, looked_up, position],
        scratch=[
            pltpu.VMEM((slots, width), BF16),
            pltpu.VMEM((negs, width), BF16),
            pltpu.VMEM((tok_rows, negs), BF16),
            pltpu.VMEM((tok_rows, width), BF16),
            pltpu.VMEM((tok_rows, width), BF16),
        ],
        name="loss",
    )
    third_in = exchange(third_out, "shard")
    kept, sent = local(
        collect_kernel,
        [shaped((HALF + WROWS // 2, width))] * 2,
        [core_s, third_in, asked_pick, negative_rows.reshape(1, NEG)],
        scalars=1,
        scratch=[pltpu.VMEM((slots, width), BF16)],
        name="collect",
    )
    arrived = lax.ppermute(sent, "dp", partners)
    pieces = (CHIPS, width // LANES * PIECE + 8, LANES)
    (packed,) = local(pack_kernel, [shaped(pieces)], [kept, arrived], name="pack")
    (summed,) = local(
        total_kernel, [shaped(pieces)], [exchange(packed, "dp", columns)], name="total"
    )
    mine = exchange(summed, "dp", columns)
    other = lax.ppermute(mine, "dp", partners)
    (weight_rows,) = local(
        weight_kernel,
        [shaped((PLANE, WROWS, width))],
        [core_s, mine, other],
        scalars=1,
        name="weight",
    )
    weight_grads = exchange(weight_rows, "shard").reshape(width, width).astype(F32) / loss_scale
    (item_grads,) = local(
        finish_kernel,
        [shaped((item_count, width), F32)],
        [core_s, mine, other, item_rows],
        scalars=1,
        name="finish",
    )

    grad_gated = dot(
        jnp.broadcast_to(grad_out_b[None], (HEADS, tok_rows, width)),
        w_out_h,
        ((2,), (2,)),
        ((0,), (0,)),
    )
    grad_gate = grad_gated * joined_wide * middle_scale
    grad_norm = grad_gated * gate_wide
    grad_joined = middle_scale * grad_norm - joined_wide * middle_scale**3 * (
        jnp.sum(joined_wide * grad_norm, axis=(0, 2), keepdims=True) / width
    )
    grad_joined_b = grad_joined.astype(BF16)
    grad_weights = dot(grad_joined_b, values, ((2,), (2,)), ((0,), (0,)))
    grad_values = dot(weights, grad_joined_b, ((1,), (1,)), ((0,), (0,)))
    slope = score_sig * (1.0 + scores * (1.0 - score_sig))
    grad_scores = jnp.where(
        visible, grad_weights * (1.0 / MAXLEN) * slope * DH ** (-0.5), 0.0
    ).astype(BF16)
    grad_queries = dot(grad_scores, keys, ((2,), (1,)), ((0,), (0,)))
    grad_keys = dot(grad_scores, queries, ((1,), (1,)), ((0,), (0,)))
    grad_act = jnp.concatenate([grad_gate, grad_values, grad_queries, grad_keys], axis=0)
    grad_pre = (grad_act * silu_slope(pre_act)).astype(BF16)
    grad_normed = jnp.sum(dot(grad_pre, w_all, ((2,), (2,)), ((0,), (0,))), axis=0)
    grad_input = input_scale * grad_normed - wide_tokens * input_scale**3 * jnp.mean(
        wide_tokens * grad_normed, axis=1, keepdims=True
    )
    grad_tokens = (grad_out + grad_input).astype(BF16)
    return (grad_tokens, weight_grads, item_grads)


def solution(mesh):
    in_specs = (
        P(("dp", "shard"), None),
        P(None, "shard"),
        P(),
        P("shard", None),
        P(("dp", "shard"), None),
        P(("dp", "shard"), None),
        P(("dp", "shard")),
        P("shard"),
    )
    out_specs = (P(("dp", "shard"), None), P(), P("shard", None))
    return jax.shard_map(shards, mesh=mesh, in_specs=in_specs, out_specs=out_specs, check_vma=False)
```

```python
import jax
import jax.numpy as jnp
from jax import lax
from jax.experimental import pallas as pl
from jax.experimental.pallas import tpu as pltpu
from jax.sharding import PartitionSpec as P

D = 512
HEADS = 4
DH = 128
MAXLEN = 192
SECTIONS = 4 * HEADS
PLANE = 16
CAP = 48
NEG = 64
WROWS = 32
CHIPS = 16
NEAR = 4
FAR = 4
HALF = 512
PIECE = 32
SHARED = 16
LANES = 128
BLOCKS = D // LANES

epsilon = 1e-06
logit_scale = 64.0
loss_scale = 512.0

F32 = jnp.float32
BF16 = jnp.bfloat16
I32 = jnp.int32


def dot(a, b, contract, batch=((), ())):
    return lax.dot_general(a, b, (contract, batch), preferred_element_type=F32)


def iota(shape, axis):
    return lax.broadcasted_iota(I32, shape, axis)


def one_hot(mask):
    return jnp.where(mask, 1.0, 0.0).astype(BF16)


def silu_slope(values):
    sigmoid = jax.nn.sigmoid(values)
    return sigmoid * (1.0 + values * (1.0 - sigmoid))


def history_mask(lengths_row, rows_count):
    history_ends = jnp.cumsum(lengths_row)
    positions = jnp.arange(rows_count, dtype=jnp.int32)
    history_ids = jnp.sum((positions[:, None] >= history_ends[None, :-1]).astype(jnp.int32), axis=1)
    return (history_ids[:, None] == history_ids[None, :]) & (
        positions[None, :] <= positions[:, None]
    )


def exchange(pieces, axis, groups=None):
    return lax.all_to_all(
        pieces, axis, split_axis=0, concat_axis=0, tiled=True, axis_index_groups=groups
    )


def route_kernel(core_ref, index_ref, w_ref, items_ref, out_ref, pos_ref):
    tok = pos_ref.shape[0]
    first = core_ref[0] == 0
    owners = jnp.broadcast_to(index_ref[0:1, 0:tok].astype(F32), (LANES, tok)).T.astype(I32)
    hits = owners == iota((tok, LANES), 1)
    earlier = one_hot(iota((tok, tok), 1) < iota((tok, tok), 0))
    before = dot(earlier, one_hot(hits), ((1,), (0,)))
    slot = jnp.sum(jnp.where(hits, before, 0.0), axis=1, keepdims=True).astype(I32)
    owners = owners[:, 0:1]
    pos_ref[...] = owners * CAP + slot
    spread = one_hot(owners * LANES + slot == iota((tok, PLANE * LANES), 1))
    asked = jnp.broadcast_to(index_ref[0:1, tok : 2 * tok], (16, tok))
    which = iota((16, tok), 0)
    digits = jnp.where(which == 0, asked >> 5, jnp.where(which == 1, asked & 31, 0))
    requests = dot(digits.astype(F32).astype(BF16), spread, ((1,), (0,))).astype(BF16)
    here = one_hot(iota((items_ref.shape[0], NEG), 0) == index_ref[0:1, 2 * tok :])
    negs = dot(here, items_ref[...], ((0,), (0,)))
    negs = jnp.where(first, negs[0 : NEG // 2], negs[NEG // 2 :])
    scale = lax.rsqrt(jnp.sum(negs * negs, axis=1, keepdims=True) + epsilon)
    negs = (negs * scale).astype(BF16)
    rows = w_ref.shape[0] // 2
    own = w_ref[pl.ds(pl.multiple_of(core_ref[0] * rows, rows), rows), :]
    for j in range(PLANE):
        out_ref[j, 0:rows, :] = own
        for q in range(BLOCKS):
            at = rows + q * (NEG // 2)
            out_ref[j, at : at + NEG // 2, :] = negs[:, q * LANES : (q + 1) * LANES]
        at = rows + BLOCKS * (NEG // 2)
        out_ref[j, at : at + 16, :] = requests[:, j * LANES : (j + 1) * LANES]


def serve_kernel(recv_ref, items_ref, out_ref, pick_ref):
    rows = recv_ref.shape[1] - 16
    count = items_ref.shape[0]
    diagonal = iota((CAP, LANES), 0) == iota((CAP, LANES), 1)
    for j in range(PLANE):
        digits = recv_ref[j, rows : rows + 16, :].astype(F32)
        asked = 32.0 * digits[0:1] + digits[1:2]
        column = jnp.sum(
            jnp.where(diagonal, jnp.broadcast_to(asked, (CAP, LANES)), 0.0), axis=1, keepdims=True
        ).astype(I32)
        pick_ref[j * CAP : (j + 1) * CAP, :] = one_hot(column == iota((CAP, count), 1))
    step = 4
    for j in range(0, PLANE, step):
        served = dot(pick_ref[j * CAP : (j + step) * CAP, :], items_ref[...], ((1,), (0,)))
        served = served.astype(BF16)
        for i in range(step):
            out_ref[j + i] = served[i * CAP : (i + 1) * CAP]


def loss_kernel(
    core_ref,
    layer_ref,
    gated_ref,
    recv_ref,
    mine_ref,
    other_ref,
    pos_ref,
    out_ref,
    grad_ref,
    grad_b_ref,
    fetched,
    decoys,
    probs,
    unit,
    back,
):
    tok = layer_ref.shape[0]
    part = NEG // 2
    rows = mine_ref.shape[1] - 16 - BLOCKS * part
    for j in range(PLANE):
        fetched[j * CAP : (j + 1) * CAP, :] = recv_ref[j]
        for ref, half in ((mine_ref, core_ref[0]), (other_ref, 1 - core_ref[0])):
            at = pl.multiple_of(j * NEG + half * part, part)
            for q in range(BLOCKS):
                block = ref[j, rows + q * part : rows + (q + 1) * part, :]
                decoys[pl.ds(at, part), q * LANES : (q + 1) * LANES] = block
    step = 128
    for c in range(0, tok, step):
        layer_out = layer_ref[c : c + step, :]
        placed = one_hot(pos_ref[c : c + step, :] == iota((step, PLANE * CAP), 1))
        clicked = dot(placed, fetched[...], ((1,), (0,)))
        out_scale = lax.rsqrt(jnp.sum(layer_out * layer_out, axis=1, keepdims=True) + epsilon)
        unit_b = (layer_out * out_scale).astype(BF16)
        unit[c : c + step, :] = unit_b
        unit_wide = unit_b.astype(F32)
        target_exp = jnp.exp(jnp.sum(unit_wide * clicked, axis=1, keepdims=True) * logit_scale)
        negative_exp = jnp.exp(dot(unit_b, decoys[...], ((1,), (1,))) * logit_scale)
        totals = target_exp + jnp.sum(negative_exp, axis=1, keepdims=True)
        negative_probs = (negative_exp * (loss_scale / totals)).astype(BF16)
        probs[c : c + step, :] = negative_probs
        target_coef = loss_scale * (target_exp / totals - 1.0)
        back[c : c + step, :] = (target_coef * unit_wide).astype(BF16)
        grad_unit = target_coef * clicked + dot(negative_probs, decoys[...], ((1,), (0,)))
        along = jnp.sum(layer_out * grad_unit, axis=1, keepdims=True)
        grad_out = out_scale * grad_unit - layer_out * (out_scale**3 * along)
        grad_ref[c : c + step, :] = grad_out
        grad_b_ref[c : c + step, :] = grad_out.astype(BF16)
    across = jnp.broadcast_to(pos_ref[...].astype(F32), (tok, LANES)).T[0:1, :].astype(I32)
    group = 4
    for j in range(0, PLANE, group):
        slots = group * CAP
        placed_t = one_hot(iota((slots, tok), 0) + j * CAP == across)
        sent = dot(placed_t, back[...], ((1,), (0,))).astype(BF16)
        negs = dot(probs[:, j * NEG : (j + group) * NEG], unit[...], ((0,), (0,))).astype(BF16)
        weights = dot(gated_ref[j // group], grad_b_ref[...], ((0,), (0,))).astype(BF16)
        for i in range(group):
            out_ref[j + i, 0:CAP, :] = sent[i * CAP : (i + 1) * CAP]
            out_ref[j + i, CAP : CAP + NEG, :] = negs[i * NEG : (i + 1) * NEG]
            out_ref[j + i, CAP + NEG :, :] = weights[i * WROWS : (i + 1) * WROWS]


def collect_kernel(core_ref, recv_ref, pick_ref, neg_row_ref, keep_ref, send_ref, returned):
    core = core_ref[0]
    negs = jnp.zeros((NEG, D), F32)
    weights = jnp.zeros((WROWS, D), F32)
    for j in range(PLANE):
        returned[j * CAP : (j + 1) * CAP, :] = recv_ref[j, 0:CAP, :]
        negs = negs + recv_ref[j, CAP : CAP + NEG, :].astype(F32)
        weights = weights + recv_ref[j, CAP + NEG :, :].astype(F32)
    negs = negs.astype(BF16)
    step = 256
    for ref, half in ((keep_ref, core), (send_ref, 1 - core)):
        for b in range(0, HALF, step):
            first = pl.multiple_of(half * HALF + b, step)
            here = one_hot(iota((step, NEG), 0) + first == neg_row_ref[...])
            total = dot(pick_ref[:, pl.ds(first, step)], returned[...], ((0,), (0,)))
            total = total + dot(here, negs, ((1,), (0,)))
            ref[b : b + step, :] = total.astype(BF16)
        part = jnp.where(half == 0, weights[0 : WROWS // 2], weights[WROWS // 2 :])
        ref[HALF:, :] = part.astype(BF16)


def near_kernel(keep_ref, other_ref, out_ref):
    rows = HALF // NEAR
    weights = (keep_ref[HALF:, :].astype(F32) + other_ref[HALF:, :].astype(F32)).astype(BF16)
    for i in range(NEAR):
        at = slice(i * rows, (i + 1) * rows)
        total = keep_ref[at, :].astype(F32) + other_ref[at, :].astype(F32)
        out_ref[i, 0:rows, :] = total.astype(BF16)
        out_ref[i, rows:, :] = weights


def far_kernel(recv_ref, out_ref):
    rows = recv_ref.shape[1] - SHARED
    total = recv_ref[0].astype(F32)
    for i in range(1, NEAR):
        total = total + recv_ref[i].astype(F32)
    total = total.astype(BF16)
    for i in range(FAR):
        out_ref[i, 0:PIECE, :] = total[i * PIECE : (i + 1) * PIECE]
        out_ref[i, PIECE:, :] = total[rows:]


def total_kernel(recv_ref, out_ref, weights_ref):
    total = recv_ref[0].astype(F32)
    for i in range(1, FAR):
        total = total + recv_ref[i].astype(F32)
    total = total.astype(BF16)
    for i in range(CHIPS):
        out_ref[i] = total[0:PIECE]
    weights_ref[...] = total[PIECE:]


def weight_kernel(place_ref, mine_ref, other_ref, out_ref):
    core, plane_y, plane_x = place_ref[0], place_ref[1], place_ref[2]
    for ref, half in ((mine_ref, core), (other_ref, 1 - core)):
        for ky in range(4):
            for kx in range(4):
                owner = ((plane_y - ky) & 3) * 4 + ((plane_x - kx) & 3)
                at = pl.multiple_of(owner * WROWS + half * SHARED, SHARED)
                first = (ky * 4 + kx) * SHARED
                rows = ref[first : first + SHARED, :].astype(F32)
                out_ref[pl.ds(at, SHARED), :] = rows * (1.0 / loss_scale)


def finish_kernel(core_ref, mine_ref, other_ref, items_ref, out_ref):
    for ref, half in ((mine_ref, core_ref[0]), (other_ref, 1 - core_ref[0])):
        for i in range(CHIPS):
            start = (i % NEAR) * (HALF // NEAR) + (i // NEAR) * PIECE
            first = pl.multiple_of(half * HALF + start, PIECE)
            rows = items_ref[pl.ds(first, PIECE), :].astype(F32)
            grads = ref[i].astype(F32)
            scale = lax.rsqrt(jnp.sum(rows * rows, axis=1, keepdims=True) + epsilon)
            along = jnp.sum(rows * grads, axis=1, keepdims=True)
            out_ref[pl.ds(first, PIECE), :] = (
                scale * grads - rows * (scale**3 * along)
            ) * (1.0 / loss_scale)


def local(kernel, outs, operands, scalars=0, scratch=(), flops=0, name=None):
    spaces = [pltpu.SMEM] * scalars + [pltpu.VMEM] * (len(operands) - scalars)
    moved = sum(v.size * v.dtype.itemsize for v in operands) + sum(
        v.size * v.dtype.itemsize for v in outs
    )
    return pl.pallas_call(
        kernel,
        out_shape=tuple(outs),
        in_specs=[pl.BlockSpec(memory_space=s) for s in spaces],
        out_specs=tuple(pl.BlockSpec(memory_space=pltpu.VMEM) for _ in outs),
        scratch_shapes=list(scratch),
        compiler_params=pltpu.CompilerParams(vmem_limit_bytes=56 * 1024 * 1024),
        cost_estimate=pl.CostEstimate(flops=flops, bytes_accessed=moved, transcendentals=0),
        name=name,
    )(*operands)


def shaped(shape, dtype=BF16):
    return jax.ShapeDtypeStruct(shape, dtype)


def shards(tokens, w_proj, w_out, item_rows, lengths, target_owner, target_row, negative_rows):
    tok_rows = tokens.shape[0]
    width = tokens.shape[1]
    item_count = item_rows.shape[0]
    dp = lax.axis_size("dp")
    slots = PLANE * CAP
    negs = PLANE * NEG
    partners = [(i, i ^ 1) for i in range(dp)]
    columns = [[2 * z + c for z in range(CHIPS)] for c in range(2)]
    near = [[2 * (NEAR * h + l) + c for l in range(NEAR)] for h in range(FAR) for c in range(2)]
    far = [[2 * (NEAR * h + l) + c for h in range(FAR)] for l in range(NEAR) for c in range(2)]
    core = lax.rem(lax.axis_index("dp"), 2).astype(I32)
    core_s = core.reshape(1)
    plane = lax.axis_index("shard").astype(I32)

    half_w = width // 2
    index = jnp.concatenate([target_owner[:, 0], target_row, negative_rows]).reshape(1, -1)
    first_out, position = local(
        route_kernel,
        [
            shaped((PLANE, half_w + BLOCKS * NEG // 2 + 16, DH)),
            shaped((tok_rows, 1), I32),
        ],
        [core_s, index, w_proj, item_rows],
        scalars=1,
        name="route",
    )
    first_in = exchange(first_out, "shard")
    first_other = lax.ppermute(first_in, "dp", partners)
    w_mine = first_in[:, :half_w]
    w_other = first_other[:, :half_w]

    rows_wide = item_rows.astype(F32)
    item_scale = lax.rsqrt(jnp.sum(rows_wide * rows_wide, axis=1, keepdims=True) + epsilon)
    unit_items = (rows_wide * item_scale).astype(BF16)
    served, asked_pick = local(
        serve_kernel,
        [shaped((PLANE, CAP, width)), shaped((slots, item_count))],
        [first_in, unit_items],
        name="serve",
    )
    looked_up = exchange(served, "shard")
    w_all = jnp.where(
        core == 0,
        jnp.concatenate([w_mine, w_other], axis=1),
        jnp.concatenate([w_other, w_mine], axis=1),
    )

    w_all = jnp.where(
        core == 0,
        jnp.concatenate([w_mine, w_other], axis=1),
        jnp.concatenate([w_other, w_mine], axis=1),
    )
    visible = history_mask(lengths[0], tok_rows)[None]
    wide_tokens = tokens.astype(F32)
    input_scale = lax.rsqrt(jnp.mean(wide_tokens * wide_tokens, axis=1, keepdims=True) + epsilon)
    normed = (wide_tokens * input_scale).astype(BF16)
    normed_s = jnp.broadcast_to(normed[None], (SECTIONS, tok_rows, width))
    pre_act = dot(normed_s, w_all, ((2,), (1,)), ((0,), (0,)))
    activated = jax.nn.silu(pre_act).astype(BF16)
    gate, values, queries, keys = (activated[i * HEADS : (i + 1) * HEADS] for i in range(4))
    scores = dot(queries, keys, ((2,), (2,)), ((0,), (0,))) * DH ** (-0.5)
    score_sig = jax.nn.sigmoid(scores)
    weights = jnp.where(visible, scores * score_sig * (1.0 / MAXLEN), 0.0).astype(BF16)
    joined = dot(weights, values, ((2,), (1,)), ((0,), (0,))).astype(BF16)
    joined_wide = joined.astype(F32)
    middle_scale = lax.rsqrt(
        jnp.sum(joined_wide * joined_wide, axis=(0, 2), keepdims=True) / width + epsilon
    )
    gate_wide = gate.astype(F32)
    gated = (joined_wide * middle_scale * gate_wide).astype(BF16)
    w_out_h = w_out.reshape(HEADS, DH, width)
    layer_out = wide_tokens + jnp.sum(dot(gated, w_out_h, ((2,), (1,)), ((0,), (0,))), axis=0)

    third_out, grad_out, grad_out_b = local(
        loss_kernel,
        [
            shaped((PLANE, CAP + NEG + WROWS, width)),
            shaped((tok_rows, width), F32),
            shaped((tok_rows, width)),
        ],
        [core_s, layer_out, gated, looked_up, first_in, first_other, position],
        scalars=1,
        scratch=[
            pltpu.VMEM((slots, width), BF16),
            pltpu.VMEM((negs, width), BF16),
            pltpu.VMEM((tok_rows, negs), BF16),
            pltpu.VMEM((tok_rows, width), BF16),
            pltpu.VMEM((tok_rows, width), BF16),
        ],
        name="loss",
    )
    third_in = exchange(third_out, "shard")

    grad_gated = dot(
        jnp.broadcast_to(grad_out_b[None], (HEADS, tok_rows, width)),
        w_out_h,
        ((2,), (2,)),
        ((0,), (0,)),
    )
    grad_gate = grad_gated * joined_wide * middle_scale
    grad_norm = grad_gated * gate_wide
    grad_joined = middle_scale * grad_norm - joined_wide * middle_scale**3 * (
        jnp.sum(joined_wide * grad_norm, axis=(0, 2), keepdims=True) / width
    )
    grad_joined_b = grad_joined.astype(BF16)
    grad_weights = dot(grad_joined_b, values, ((2,), (2,)), ((0,), (0,)))
    grad_values = dot(weights, grad_joined_b, ((1,), (1,)), ((0,), (0,)))
    slope = score_sig * (1.0 + scores * (1.0 - score_sig))
    grad_scores = jnp.where(
        visible, grad_weights * (1.0 / MAXLEN) * slope * DH ** (-0.5), 0.0
    ).astype(BF16)
    grad_queries = dot(grad_scores, keys, ((2,), (1,)), ((0,), (0,)))
    grad_keys = dot(grad_scores, queries, ((1,), (1,)), ((0,), (0,)))
    grad_act = jnp.concatenate([grad_gate, grad_values, grad_queries, grad_keys], axis=0)
    grad_pre = (grad_act * silu_slope(pre_act)).astype(BF16)
    grad_normed = jnp.sum(dot(grad_pre, w_all, ((2,), (2,)), ((0,), (0,))), axis=0)
    grad_input = input_scale * grad_normed - wide_tokens * input_scale**3 * jnp.mean(
        wide_tokens * grad_normed, axis=1, keepdims=True
    )
    grad_tokens = (grad_out + grad_input).astype(BF16)
    third_in, grad_tokens = lax.optimization_barrier((third_in, grad_tokens))

    kept, sent = local(
        collect_kernel,
        [shaped((HALF + WROWS // 2, width))] * 2,
        [core_s, third_in, asked_pick, negative_rows.reshape(1, NEG)],
        scalars=1,
        scratch=[pltpu.VMEM((slots, width), BF16)],
        name="collect",
    )
    arrived = lax.ppermute(sent, "dp", partners)
    (near_out,) = local(
        near_kernel,
        [shaped((NEAR, HALF // NEAR + SHARED, width))],
        [kept, arrived],
        name="near",
    )
    (far_out,) = local(
        far_kernel,
        [shaped((FAR, PIECE + SHARED, width))],
        [exchange(near_out, "dp", near)],
        name="far",
    )
    summed, w_rows = local(
        total_kernel,
        [shaped((CHIPS, PIECE, width)), shaped((SHARED, width))],
        [exchange(far_out, "dp", far)],
        name="total",
    )
    mine = exchange(summed, "dp", columns)

    def turned(rows, step_y, step_x):
        moves = [
            (y * 4 + x, (y + step_y) % 4 * 4 + (x + step_x) % 4) for y in range(4) for x in range(4)
        ]
        return lax.ppermute(rows, "shard", moves)

    w_rows = jnp.concatenate([w_rows] + [turned(w_rows, 0, k) for k in (1, 2, 3)], axis=0)
    w_rows = jnp.concatenate([w_rows] + [turned(w_rows, k, 0) for k in (1, 2, 3)], axis=0)
    w_other_rows = lax.ppermute(w_rows, "dp", partners)
    mine, w_other_rows = lax.optimization_barrier((mine, w_other_rows))
    (weight_grads,) = local(
        weight_kernel,
        [shaped((width, width), F32)],
        [jnp.stack([core, plane >> 2, plane & 3]), w_rows, w_other_rows],
        scalars=1,
        name="weight",
    )
    other = lax.ppermute(mine, "dp", partners)
    (item_grads,) = local(
        finish_kernel,
        [shaped((item_count, width), F32)],
        [core_s, mine, other, item_rows],
        scalars=1,
        name="finish",
    )
    return (grad_tokens, weight_grads, item_grads)


def solution(mesh):
    in_specs = (
        P(("dp", "shard"), None),
        P(None, "shard"),
        P(),
        P("shard", None),
        P(("dp", "shard"), None),
        P(("dp", "shard"), None),
        P(("dp", "shard")),
        P("shard"),
    )
    out_specs = (P(("dp", "shard"), None), P(), P("shard", None))
    return jax.shard_map(shards, mesh=mesh, in_specs=in_specs, out_specs=out_specs, check_vma=False)
```

```python
import jax
import jax.numpy as jnp
from jax import lax
from jax.experimental import pallas as pl
from jax.experimental.pallas import tpu as pltpu
from jax.sharding import PartitionSpec as P

D = 512
HEADS = 4
DH = 128
MAXLEN = 192
SECTIONS = 4 * HEADS
PLANE = 16
CAP = 48
NEG = 64
WROWS = 32
CHIPS = 16
NEAR = 4
FAR = 4
HALF = 512
PIECE = 32
SHARED = 16
LANES = 128
BLOCKS = D // LANES

epsilon = 1e-06
logit_scale = 64.0
loss_scale = 512.0

F32 = jnp.float32
BF16 = jnp.bfloat16
I32 = jnp.int32


def dot(a, b, contract, batch=((), ())):
    return lax.dot_general(a, b, (contract, batch), preferred_element_type=F32)


def iota(shape, axis):
    return lax.broadcasted_iota(I32, shape, axis)


def one_hot(mask):
    return jnp.where(mask, 1.0, 0.0).astype(BF16)


def silu_slope(values):
    sigmoid = jax.nn.sigmoid(values)
    return sigmoid * (1.0 + values * (1.0 - sigmoid))


def history_mask(lengths_row, rows_count):
    history_ends = jnp.cumsum(lengths_row)
    positions = jnp.arange(rows_count, dtype=jnp.int32)
    history_ids = jnp.sum((positions[:, None] >= history_ends[None, :-1]).astype(jnp.int32), axis=1)
    return (history_ids[:, None] == history_ids[None, :]) & (
        positions[None, :] <= positions[:, None]
    )


def exchange(pieces, axis, groups=None):
    return lax.all_to_all(
        pieces, axis, split_axis=0, concat_axis=0, tiled=True, axis_index_groups=groups
    )


def route_kernel(core_ref, index_ref, w_ref, items_ref, out_ref, pos_ref):
    tok = pos_ref.shape[0]
    first = core_ref[0] == 0
    owners = jnp.broadcast_to(index_ref[0:1, 0:tok].astype(F32), (LANES, tok)).T.astype(I32)
    hits = owners == iota((tok, LANES), 1)
    earlier = one_hot(iota((tok, tok), 1) < iota((tok, tok), 0))
    before = dot(earlier, one_hot(hits), ((1,), (0,)))
    slot = jnp.sum(jnp.where(hits, before, 0.0), axis=1, keepdims=True).astype(I32)
    owners = owners[:, 0:1]
    pos_ref[...] = owners * CAP + slot
    spread = one_hot(owners * LANES + slot == iota((tok, PLANE * LANES), 1))
    asked = jnp.broadcast_to(index_ref[0:1, tok : 2 * tok], (16, tok))
    which = iota((16, tok), 0)
    digits = jnp.where(which == 0, asked >> 5, jnp.where(which == 1, asked & 31, 0))
    requests = dot(digits.astype(F32).astype(BF16), spread, ((1,), (0,))).astype(BF16)
    here = one_hot(iota((items_ref.shape[0], NEG), 0) == index_ref[0:1, 2 * tok :])
    negs = dot(here, items_ref[...], ((0,), (0,)))
    negs = jnp.where(first, negs[0 : NEG // 2], negs[NEG // 2 :])
    scale = lax.rsqrt(jnp.sum(negs * negs, axis=1, keepdims=True) + epsilon)
    negs = (negs * scale).astype(BF16)
    rows = w_ref.shape[0] // 2
    own = w_ref[pl.ds(pl.multiple_of(core_ref[0] * rows, rows), rows), :]
    for j in range(PLANE):
        out_ref[j, 0:rows, :] = own
        for q in range(BLOCKS):
            at = rows + q * (NEG // 2)
            out_ref[j, at : at + NEG // 2, :] = negs[:, q * LANES : (q + 1) * LANES]
        at = rows + BLOCKS * (NEG // 2)
        out_ref[j, at : at + 16, :] = requests[:, j * LANES : (j + 1) * LANES]


def serve_kernel(recv_ref, items_ref, out_ref, pick_ref):
    rows = recv_ref.shape[1] - 16
    count = items_ref.shape[0]
    diagonal = iota((CAP, LANES), 0) == iota((CAP, LANES), 1)
    for j in range(PLANE):
        digits = recv_ref[j, rows : rows + 16, :].astype(F32)
        asked = 32.0 * digits[0:1] + digits[1:2]
        column = jnp.sum(
            jnp.where(diagonal, jnp.broadcast_to(asked, (CAP, LANES)), 0.0), axis=1, keepdims=True
        ).astype(I32)
        pick_ref[j * CAP : (j + 1) * CAP, :] = one_hot(column == iota((CAP, count), 1))
    step = 4
    for j in range(0, PLANE, step):
        served = dot(pick_ref[j * CAP : (j + step) * CAP, :], items_ref[...], ((1,), (0,)))
        served = served.astype(BF16)
        for i in range(step):
            out_ref[j + i] = served[i * CAP : (i + 1) * CAP]


def normalize(tokens_ref, normed_ref):
    step = 128
    for c in range(0, tokens_ref.shape[0], step):
        wide = tokens_ref[c : c + step, :].astype(F32)
        scale = lax.rsqrt(jnp.mean(wide * wide, axis=1, keepdims=True) + epsilon)
        normed_ref[c : c + step, :] = (wide * scale).astype(BF16)


def norm_kernel(tokens_ref, after_ref, normed_ref):
    normalize(tokens_ref, normed_ref)


def forward_kernel(
    core_ref,
    lengths_ref,
    tokens_ref,
    mine_ref,
    other_ref,
    w_out_ref,
    layer_ref,
    gated_ref,
    w_all_ref,
    normed,
    act,
):
    tok, width = tokens_ref.shape
    core = core_ref[0]
    half = width // 2
    step = 128
    normalize(tokens_ref, normed)
    left = normed[:, pl.ds(pl.multiple_of(core * half, half), half)]
    right = normed[:, pl.ds(pl.multiple_of((1 - core) * half, half), half)]
    for ref, part in ((mine_ref, core), (other_ref, 1 - core)):
        at = pl.multiple_of(part * half, half)
        for j in range(SECTIONS):
            w_all_ref[j, pl.ds(at, half), :] = ref[j, 0:half, :]
    for j in range(0, SECTIONS, 2):
        w_left = jnp.concatenate([mine_ref[j, 0:half, :], mine_ref[j + 1, 0:half, :]], axis=1)
        w_right = jnp.concatenate([other_ref[j, 0:half, :], other_ref[j + 1, 0:half, :]], axis=1)
        pre = dot(left, w_left, ((1,), (0,))) + dot(right, w_right, ((1,), (0,)))
        pair = (pre * jax.nn.sigmoid(pre)).astype(BF16)
        act[j] = pair[:, 0:DH]
        act[j + 1] = pair[:, DH:]
    end_0 = lengths_ref[0, 0]
    end_1 = end_0 + lengths_ref[0, 1]
    end_2 = end_1 + lengths_ref[0, 2]
    for c in range(0, tok, step):
        seen = c + step
        row = iota((step, 1), 0) + c
        start = jnp.where(row >= end_0, end_0, 0)
        start = jnp.where(row >= end_1, end_1, start)
        start = jnp.where(row >= end_2, end_2, start)
        col = iota((step, seen), 1)
        visible = (col <= row) & (col >= start)
        heads = []
        total = jnp.zeros((step, 1), F32)
        for h in range(HEADS):
            values = act[HEADS + h, 0:seen, :]
            queries = act[2 * HEADS + h, c:seen, :]
            keys = act[3 * HEADS + h, 0:seen, :]
            scores = dot(queries, keys, ((1,), (1,))) * DH ** (-0.5)
            silu = scores * jax.nn.sigmoid(scores) * (1.0 / MAXLEN)
            weights = jnp.where(visible, silu, 0.0).astype(BF16)
            joined = dot(weights, values, ((1,), (0,))).astype(BF16).astype(F32)
            total = total + jnp.sum(joined * joined, axis=1, keepdims=True)
            heads.append(joined)
        scale = lax.rsqrt(total * (1.0 / width) + epsilon)
        out = tokens_ref[c:seen, :].astype(F32)
        for h in range(HEADS):
            gated = (heads[h] * scale * act[h, c:seen, :].astype(F32)).astype(BF16)
            gated_ref[h, c:seen, :] = gated
            out = out + dot(gated, w_out_ref[h * DH : (h + 1) * DH, :], ((1,), (0,)))
        layer_ref[c:seen, :] = out


def loss_kernel(
    core_ref,
    layer_ref,
    gated_ref,
    recv_ref,
    mine_ref,
    other_ref,
    pos_ref,
    out_ref,
    grad_ref,
    grad_b_ref,
    fetched,
    decoys,
    probs,
    unit,
    back,
):
    tok = layer_ref.shape[0]
    part = NEG // 2
    rows = mine_ref.shape[1] - 16 - BLOCKS * part
    for j in range(PLANE):
        fetched[j * CAP : (j + 1) * CAP, :] = recv_ref[j]
        for ref, half in ((mine_ref, core_ref[0]), (other_ref, 1 - core_ref[0])):
            at = pl.multiple_of(j * NEG + half * part, part)
            for q in range(BLOCKS):
                block = ref[j, rows + q * part : rows + (q + 1) * part, :]
                decoys[pl.ds(at, part), q * LANES : (q + 1) * LANES] = block
    step = 128
    for c in range(0, tok, step):
        layer_out = layer_ref[c : c + step, :]
        placed = one_hot(pos_ref[c : c + step, :] == iota((step, PLANE * CAP), 1))
        clicked = dot(placed, fetched[...], ((1,), (0,)))
        out_scale = lax.rsqrt(jnp.sum(layer_out * layer_out, axis=1, keepdims=True) + epsilon)
        unit_b = (layer_out * out_scale).astype(BF16)
        unit[c : c + step, :] = unit_b
        unit_wide = unit_b.astype(F32)
        target_exp = jnp.exp(jnp.sum(unit_wide * clicked, axis=1, keepdims=True) * logit_scale)
        negative_exp = jnp.exp(dot(unit_b, decoys[...], ((1,), (1,))) * logit_scale)
        totals = target_exp + jnp.sum(negative_exp, axis=1, keepdims=True)
        negative_probs = (negative_exp * (loss_scale / totals)).astype(BF16)
        probs[c : c + step, :] = negative_probs
        target_coef = loss_scale * (target_exp / totals - 1.0)
        back[c : c + step, :] = (target_coef * unit_wide).astype(BF16)
        grad_unit = target_coef * clicked + dot(negative_probs, decoys[...], ((1,), (0,)))
        along = jnp.sum(layer_out * grad_unit, axis=1, keepdims=True)
        grad_out = out_scale * grad_unit - layer_out * (out_scale**3 * along)
        grad_ref[c : c + step, :] = grad_out
        grad_b_ref[c : c + step, :] = grad_out.astype(BF16)
    across = jnp.broadcast_to(pos_ref[...].astype(F32), (tok, LANES)).T[0:1, :].astype(I32)
    group = 4
    for j in range(0, PLANE, group):
        slots = group * CAP
        placed_t = one_hot(iota((slots, tok), 0) + j * CAP == across)
        sent = dot(placed_t, back[...], ((1,), (0,))).astype(BF16)
        negs = dot(probs[:, j * NEG : (j + group) * NEG], unit[...], ((0,), (0,))).astype(BF16)
        weights = dot(gated_ref[j // group], grad_b_ref[...], ((0,), (0,))).astype(BF16)
        for i in range(group):
            out_ref[j + i, 0:CAP, :] = sent[i * CAP : (i + 1) * CAP]
            out_ref[j + i, CAP : CAP + NEG, :] = negs[i * NEG : (i + 1) * NEG]
            out_ref[j + i, CAP + NEG :, :] = weights[i * WROWS : (i + 1) * WROWS]


def half_sums(half, pick_ref, neg_row_ref, returned, negs, weights, ref):
    step = 256
    for b in range(0, HALF, step):
        first = pl.multiple_of(half * HALF + b, step)
        here = one_hot(iota((step, NEG), 0) + first == neg_row_ref[...])
        total = dot(pick_ref[:, pl.ds(first, step)], returned[...], ((0,), (0,)))
        total = total + dot(here, negs, ((1,), (0,)))
        ref[b : b + step, :] = total.astype(BF16)
    part = jnp.where(half == 0, weights[0:SHARED], weights[SHARED:])
    ref[HALF:, :] = part.astype(BF16)


def send_kernel(
    core_ref, recv_ref, pick_ref, neg_row_ref, send_ref, returned, negs_ref, weights_ref
):
    negs = jnp.zeros((NEG, D), F32)
    weights = jnp.zeros((WROWS, D), F32)
    for j in range(PLANE):
        returned[j * CAP : (j + 1) * CAP, :] = recv_ref[j, 0:CAP, :]
        negs = negs + recv_ref[j, CAP : CAP + NEG, :].astype(F32)
        weights = weights + recv_ref[j, CAP + NEG :, :].astype(F32)
    negs = negs.astype(BF16)
    negs_ref[...] = negs
    weights_ref[...] = weights
    half_sums(1 - core_ref[0], pick_ref, neg_row_ref, returned, negs, weights, send_ref)


def keep_kernel(
    core_ref, pick_ref, neg_row_ref, returned, negs_ref, weights_ref, keep_ref
):
    negs, weights = negs_ref[...], weights_ref[...]
    half_sums(core_ref[0], pick_ref, neg_row_ref, returned, negs, weights, keep_ref)


def near_kernel(keep_ref, other_ref, out_ref):
    rows = HALF // NEAR
    weights = (keep_ref[HALF:, :].astype(F32) + other_ref[HALF:, :].astype(F32)).astype(BF16)
    for i in range(NEAR):
        at = slice(i * rows, (i + 1) * rows)
        total = keep_ref[at, :].astype(F32) + other_ref[at, :].astype(F32)
        out_ref[i, 0:rows, :] = total.astype(BF16)
        out_ref[i, rows:, :] = weights


def far_kernel(recv_ref, out_ref):
    rows = recv_ref.shape[1] - SHARED
    total = recv_ref[0].astype(F32)
    for i in range(1, NEAR):
        total = total + recv_ref[i].astype(F32)
    total = total.astype(BF16)
    for i in range(FAR):
        out_ref[i, 0:PIECE, :] = total[i * PIECE : (i + 1) * PIECE]
        out_ref[i, PIECE:, :] = total[rows:]


def total_kernel(recv_ref, out_ref, weights_ref):
    total = recv_ref[0].astype(F32)
    for i in range(1, FAR):
        total = total + recv_ref[i].astype(F32)
    total = total.astype(BF16)
    for i in range(CHIPS):
        out_ref[i] = total[0:PIECE]
    weights_ref[...] = total[PIECE:]


def weight_kernel(place_ref, mine_ref, other_ref, out_ref):
    core, plane_y, plane_x = place_ref[0], place_ref[1], place_ref[2]
    for ref, half in ((mine_ref, core), (other_ref, 1 - core)):
        for ky in range(4):
            for kx in range(4):
                owner = ((plane_y - ky) & 3) * 4 + ((plane_x - kx) & 3)
                at = pl.multiple_of(owner * WROWS + half * SHARED, SHARED)
                first = (ky * 4 + kx) * SHARED
                rows = ref[first : first + SHARED, :].astype(F32)
                out_ref[pl.ds(at, SHARED), :] = rows * (1.0 / loss_scale)


def finish_kernel(half_ref, grads_ref, items_ref, *rest):
    out_ref = rest[-1]
    for i in range(CHIPS):
        first = (i % NEAR) * (HALF // NEAR) + (i // NEAR) * PIECE
        rows = items_ref[first : first + PIECE, :].astype(F32)
        grads = grads_ref[i].astype(F32)
        scale = lax.rsqrt(jnp.sum(rows * rows, axis=1, keepdims=True) + epsilon)
        along = jnp.sum(rows * grads, axis=1, keepdims=True)
        out_ref[first : first + PIECE, :] = (scale * grads - rows * (scale**3 * along)) * (
            1.0 / loss_scale
        )


def finish(half, grads, items, earlier=None):
    count, width = items.shape
    half_block = pl.BlockSpec((HALF, width), lambda i, half_ref: (half_ref[0], 0))
    operands = [half.reshape(1), grads, items]
    in_specs = [pl.BlockSpec((CHIPS, PIECE, width), lambda i, half_ref: (0, 0, 0)), half_block]
    aliases = {}
    if earlier is not None:
        operands.append(earlier)
        in_specs.append(pl.BlockSpec(memory_space=pl.ANY))
        aliases = {3: 0}
    return pl.pallas_call(
        finish_kernel,
        out_shape=jax.ShapeDtypeStruct((count, width), F32),
        grid_spec=pltpu.PrefetchScalarGridSpec(
            num_scalar_prefetch=1, grid=(1,), in_specs=in_specs, out_specs=half_block
        ),
        input_output_aliases=aliases,
        cost_estimate=pl.CostEstimate(flops=0, bytes_accessed=1 << 21, transcendentals=0),
        name="finish",
    )(*operands)


def local(kernel, outs, operands, scalars=0, scratch=(), flops=0):
    spaces = [pltpu.SMEM] * scalars + [pltpu.VMEM] * (len(operands) - scalars)
    moved = sum(v.size * v.dtype.itemsize for v in operands) + sum(
        v.size * v.dtype.itemsize for v in outs
    )
    return pl.pallas_call(
        kernel,
        out_shape=tuple(outs),
        in_specs=[pl.BlockSpec(memory_space=s) for s in spaces],
        out_specs=tuple(pl.BlockSpec(memory_space=pltpu.VMEM) for _ in outs),
        scratch_shapes=list(scratch),
        compiler_params=pltpu.CompilerParams(vmem_limit_bytes=56 * 1024 * 1024),
        cost_estimate=pl.CostEstimate(flops=flops, bytes_accessed=moved, transcendentals=0),
    )(*operands)


def shaped(shape, dtype=BF16):
    return jax.ShapeDtypeStruct(shape, dtype)


def shards(tokens, w_proj, w_out, item_rows, lengths, target_owner, target_row, negative_rows):
    tok_rows = tokens.shape[0]
    width = tokens.shape[1]
    item_count = item_rows.shape[0]
    dp = lax.axis_size("dp")
    slots = PLANE * CAP
    negs = PLANE * NEG
    partners = [(i, i ^ 1) for i in range(dp)]
    columns = [[2 * z + c for z in range(CHIPS)] for c in range(2)]
    near = [[2 * (NEAR * h + l) + c for l in range(NEAR)] for h in range(FAR) for c in range(2)]
    far = [[2 * (NEAR * h + l) + c for h in range(FAR)] for l in range(NEAR) for c in range(2)]
    core = lax.rem(lax.axis_index("dp"), 2).astype(I32)
    core_s = core.reshape(1)
    plane = lax.axis_index("shard").astype(I32)

    half_w = width // 2
    index = jnp.concatenate([target_owner[:, 0], target_row, negative_rows]).reshape(1, -1)
    first_out, position = local(
        route_kernel,
        [
            shaped((PLANE, half_w + BLOCKS * NEG // 2 + 16, DH)),
            shaped((tok_rows, 1), I32),
        ],
        [core_s, index, w_proj, item_rows],
        scalars=1,
    )
    first_in = exchange(first_out, "shard")

    rows_wide = item_rows.astype(F32)
    item_scale = lax.rsqrt(jnp.sum(rows_wide * rows_wide, axis=1, keepdims=True) + epsilon)
    unit_items = (rows_wide * item_scale).astype(BF16)
    first_in, unit_items = lax.optimization_barrier((first_in, unit_items))
    served, asked_pick = local(
        serve_kernel,
        [shaped((PLANE, CAP, width)), shaped((slots, item_count))],
        [first_in, unit_items],
    )
    served, first_mine = lax.optimization_barrier((served, first_in))
    looked_up = exchange(served, "shard")
    first_other = lax.ppermute(first_mine, "dp", partners)
    layer_out, gated, w_all = local(
        forward_kernel,
        [
            shaped((tok_rows, width), F32),
            shaped((HEADS, tok_rows, DH)),
            shaped((SECTIONS, width, DH)),
        ],
        [core_s, lengths, tokens, first_mine, first_other, w_out],
        scalars=2,
        scratch=[
            pltpu.VMEM((tok_rows, width), BF16),
            pltpu.VMEM((SECTIONS, tok_rows, DH), BF16),
        ],
    )

    third_out, grad_out, grad_out_b = local(
        loss_kernel,
        [
            shaped((PLANE, CAP + NEG + WROWS, width)),
            shaped((tok_rows, width), F32),
            shaped((tok_rows, width)),
        ],
        [core_s, layer_out, gated, looked_up, first_mine, first_other, position],
        scalars=1,
        scratch=[
            pltpu.VMEM((slots, width), BF16),
            pltpu.VMEM((negs, width), BF16),
            pltpu.VMEM((tok_rows, negs), BF16),
            pltpu.VMEM((tok_rows, width), BF16),
            pltpu.VMEM((tok_rows, width), BF16),
        ],
    )
    third_in = exchange(third_out, "shard")

    (normed,) = local(norm_kernel, [shaped((tok_rows, width))], [tokens, grad_out_b])
    grad_out_b, w_all, normed, tokens = lax.optimization_barrier(
        (grad_out_b, w_all, normed, tokens)
    )
    visible = history_mask(lengths[0], tok_rows)[None]
    wide_tokens = tokens.astype(F32)
    input_scale = lax.rsqrt(jnp.mean(wide_tokens * wide_tokens, axis=1, keepdims=True) + epsilon)
    normed_s = jnp.broadcast_to(normed[None], (SECTIONS, tok_rows, width))
    pre_act = dot(normed_s, w_all, ((2,), (1,)), ((0,), (0,)))
    activated = jax.nn.silu(pre_act).astype(BF16)
    gate, values, queries, keys = (activated[i * HEADS : (i + 1) * HEADS] for i in range(4))
    scores = dot(queries, keys, ((2,), (2,)), ((0,), (0,))) * DH ** (-0.5)
    score_sig = jax.nn.sigmoid(scores)
    weights = jnp.where(visible, scores * score_sig * (1.0 / MAXLEN), 0.0).astype(BF16)
    joined = dot(weights, values, ((2,), (1,)), ((0,), (0,))).astype(BF16)
    joined_wide = joined.astype(F32)
    middle_scale = lax.rsqrt(
        jnp.sum(joined_wide * joined_wide, axis=(0, 2), keepdims=True) / width + epsilon
    )
    gate_wide = gate.astype(F32)
    w_out_h = w_out.reshape(HEADS, DH, width)
    grad_gated = dot(
        jnp.broadcast_to(grad_out_b[None], (HEADS, tok_rows, width)),
        w_out_h,
        ((2,), (2,)),
        ((0,), (0,)),
    )
    grad_gate = grad_gated * joined_wide * middle_scale
    grad_norm = grad_gated * gate_wide
    grad_joined = middle_scale * grad_norm - joined_wide * middle_scale**3 * (
        jnp.sum(joined_wide * grad_norm, axis=(0, 2), keepdims=True) / width
    )
    grad_joined_b = grad_joined.astype(BF16)
    grad_weights = dot(grad_joined_b, values, ((2,), (2,)), ((0,), (0,)))
    grad_values = dot(weights, grad_joined_b, ((1,), (1,)), ((0,), (0,)))
    slope = score_sig * (1.0 + scores * (1.0 - score_sig))
    grad_scores = jnp.where(
        visible, grad_weights * (1.0 / MAXLEN) * slope * DH ** (-0.5), 0.0
    ).astype(BF16)
    grad_queries = dot(grad_scores, keys, ((2,), (1,)), ((0,), (0,)))
    grad_keys = dot(grad_scores, queries, ((1,), (1,)), ((0,), (0,)))
    grad_act = jnp.concatenate([grad_gate, grad_values, grad_queries, grad_keys], axis=0)
    grad_pre = (grad_act * silu_slope(pre_act)).astype(BF16)
    grad_normed = jnp.sum(dot(grad_pre, w_all, ((2,), (2,)), ((0,), (0,))), axis=0)
    grad_input = input_scale * grad_normed - wide_tokens * input_scale**3 * jnp.mean(
        wide_tokens * grad_normed, axis=1, keepdims=True
    )
    grad_tokens = (grad_out + grad_input).astype(BF16)
    third_in, grad_tokens = lax.optimization_barrier((third_in, grad_tokens))

    neg_row = negative_rows.reshape(1, NEG)
    sent, returned, neg_sum, w_sum = local(
        send_kernel,
        [
            shaped((HALF + SHARED, width)),
            shaped((slots, width)),
            shaped((NEG, width)),
            shaped((WROWS, width), F32),
        ],
        [core_s, third_in, asked_pick, neg_row],
        scalars=1,
    )
    arrived = lax.ppermute(sent, "dp", partners)
    (kept,) = local(
        keep_kernel,
        [shaped((HALF + SHARED, width))],
        [core_s, asked_pick, neg_row, returned, neg_sum, w_sum],
        scalars=1,
    )
    (near_out,) = local(
        near_kernel, [shaped((NEAR, HALF // NEAR + SHARED, width))], [kept, arrived]
    )
    (far_out,) = local(
        far_kernel, [shaped((FAR, PIECE + SHARED, width))], [exchange(near_out, "dp", near)]
    )
    summed, w_rows = local(
        total_kernel,
        [shaped((CHIPS, PIECE, width)), shaped((SHARED, width))],
        [exchange(far_out, "dp", far)],
    )
    mine = exchange(summed, "dp", columns)

    def turned(rows, step_y, step_x):
        moves = [
            (y * 4 + x, (y + step_y) % 4 * 4 + (x + step_x) % 4) for y in range(4) for x in range(4)
        ]
        return lax.ppermute(rows, "shard", moves)

    w_rows = jnp.concatenate([w_rows] + [turned(w_rows, 0, k) for k in (1, 2, 3)], axis=0)
    w_rows = jnp.concatenate([w_rows] + [turned(w_rows, k, 0) for k in (1, 2, 3)], axis=0)
    w_other_rows = lax.ppermute(w_rows, "dp", partners)
    other = lax.ppermute(mine, "dp", partners)
    item_grads = finish(1 - core, other, item_rows, finish(core, mine, item_rows))
    w_rows, w_other_rows, item_grads = lax.optimization_barrier((w_rows, w_other_rows, item_grads))
    (weight_grads,) = local(
        weight_kernel,
        [shaped((width, width), F32)],
        [jnp.stack([core, plane >> 2, plane & 3]), w_rows, w_other_rows],
        scalars=1,
    )
    return (grad_tokens, weight_grads, item_grads)


def solution(mesh):
    in_specs = (
        P(("dp", "shard"), None),
        P(None, "shard"),
        P(),
        P("shard", None),
        P(("dp", "shard"), None),
        P(("dp", "shard"), None),
        P(("dp", "shard")),
        P("shard"),
    )
    out_specs = (P(("dp", "shard"), None), P(), P("shard", None))
    return jax.shard_map(
        shards, mesh=mesh, in_specs=in_specs, out_specs=out_specs, check_vma=False
    )
```

```python
import jax
import jax.numpy as jnp
from jax import lax
from jax.experimental import pallas as pl
from jax.experimental.pallas import tpu as pltpu
from jax.sharding import PartitionSpec as P

D = 512
HEADS = 4
DH = 128
MAXLEN = 192
SECTIONS = 4 * HEADS
PLANE = 16
CAP = 48
NEG = 64
WROWS = 32
CHIPS = 16
HALF = 512
PIECE = 32
SHARED = 16
LANES = 128
BLOCKS = D // LANES
GRANT = 24 * 1024 * 1024
WIDE_GRANT = 56 * 1024 * 1024

epsilon = 1e-06
logit_scale = 64.0
loss_scale = 512.0

F32 = jnp.float32
BF16 = jnp.bfloat16
I32 = jnp.int32


def dot(a, b, contract, batch=((), ())):
    return lax.dot_general(a, b, (contract, batch), preferred_element_type=F32)


def iota(shape, axis):
    return lax.broadcasted_iota(I32, shape, axis)


def one_hot(mask):
    return jnp.where(mask, 1.0, 0.0).astype(BF16)


def silu_slope(values):
    sigmoid = jax.nn.sigmoid(values)
    return sigmoid * (1.0 + values * (1.0 - sigmoid))


def history_mask(lengths_row, rows_count):
    history_ends = jnp.cumsum(lengths_row)
    positions = jnp.arange(rows_count, dtype=jnp.int32)
    history_ids = jnp.sum((positions[:, None] >= history_ends[None, :-1]).astype(jnp.int32), axis=1)
    return (history_ids[:, None] == history_ids[None, :]) & (
        positions[None, :] <= positions[:, None]
    )


def exchange(pieces, axis, groups=None):
    return lax.all_to_all(
        pieces, axis, split_axis=0, concat_axis=0, tiled=True, axis_index_groups=groups
    )


def route_kernel(core_ref, index_ref, w_ref, items_ref, out_ref, pos_ref):
    tok = pos_ref.shape[0]
    first = core_ref[0] == 0
    owners = jnp.broadcast_to(index_ref[0:1, 0:tok].astype(F32), (LANES, tok)).T.astype(I32)
    hits = owners == iota((tok, LANES), 1)
    earlier = one_hot(iota((tok, tok), 1) < iota((tok, tok), 0))
    before = dot(earlier, one_hot(hits), ((1,), (0,)))
    slot = jnp.sum(jnp.where(hits, before, 0.0), axis=1, keepdims=True).astype(I32)
    owners = owners[:, 0:1]
    pos_ref[...] = owners * CAP + slot
    spread = one_hot(owners * LANES + slot == iota((tok, PLANE * LANES), 1))
    asked = jnp.broadcast_to(index_ref[0:1, tok : 2 * tok], (16, tok))
    which = iota((16, tok), 0)
    digits = jnp.where(which == 0, asked >> 5, jnp.where(which == 1, asked & 31, 0))
    requests = dot(digits.astype(F32).astype(BF16), spread, ((1,), (0,))).astype(BF16)
    here = one_hot(iota((items_ref.shape[0], NEG), 0) == index_ref[0:1, 2 * tok :])
    negs = dot(here, items_ref[...], ((0,), (0,)))
    negs = jnp.where(first, negs[0 : NEG // 2], negs[NEG // 2 :])
    scale = lax.rsqrt(jnp.sum(negs * negs, axis=1, keepdims=True) + epsilon)
    negs = (negs * scale).astype(BF16)
    rows = w_ref.shape[0] // 2
    own = w_ref[pl.ds(pl.multiple_of(core_ref[0] * rows, rows), rows), :]
    for j in range(PLANE):
        out_ref[j, 0:rows, :] = own
        for q in range(BLOCKS):
            at = rows + q * (NEG // 2)
            out_ref[j, at : at + NEG // 2, :] = negs[:, q * LANES : (q + 1) * LANES]
        at = rows + BLOCKS * (NEG // 2)
        out_ref[j, at : at + 16, :] = requests[:, j * LANES : (j + 1) * LANES]


def serve_kernel(recv_ref, items_ref, out_ref, pick_ref):
    rows = recv_ref.shape[1] - 16
    count = items_ref.shape[0]
    diagonal = iota((CAP, LANES), 0) == iota((CAP, LANES), 1)
    for j in range(PLANE):
        digits = recv_ref[j, rows : rows + 16, :].astype(F32)
        asked = 32.0 * digits[0:1] + digits[1:2]
        column = jnp.sum(
            jnp.where(diagonal, jnp.broadcast_to(asked, (CAP, LANES)), 0.0), axis=1, keepdims=True
        ).astype(I32)
        pick_ref[j * CAP : (j + 1) * CAP, :] = one_hot(column == iota((CAP, count), 1))
    step = 4
    for j in range(0, PLANE, step):
        served = dot(pick_ref[j * CAP : (j + step) * CAP, :], items_ref[...], ((1,), (0,)))
        served = served.astype(BF16)
        for i in range(step):
            out_ref[j + i] = served[i * CAP : (i + 1) * CAP]


def normalize(tokens_ref, normed_ref):
    step = 128
    for c in range(0, tokens_ref.shape[0], step):
        wide = tokens_ref[c : c + step, :].astype(F32)
        scale = lax.rsqrt(jnp.mean(wide * wide, axis=1, keepdims=True) + epsilon)
        normed_ref[c : c + step, :] = (wide * scale).astype(BF16)


def norm_kernel(tokens_ref, after_ref, normed_ref):
    normalize(tokens_ref, normed_ref)


def forward_kernel(
    core_ref,
    lengths_ref,
    tokens_ref,
    mine_ref,
    other_ref,
    w_out_ref,
    layer_ref,
    gated_ref,
    w_all_ref,
    normed,
    act,
):
    tok, width = tokens_ref.shape
    core = core_ref[0]
    half = width // 2
    step = 128
    normalize(tokens_ref, normed)
    left = normed[:, pl.ds(pl.multiple_of(core * half, half), half)]
    right = normed[:, pl.ds(pl.multiple_of((1 - core) * half, half), half)]
    for ref, part in ((mine_ref, core), (other_ref, 1 - core)):
        at = pl.multiple_of(part * half, half)
        for j in range(SECTIONS):
            w_all_ref[j, pl.ds(at, half), :] = ref[j, 0:half, :]
    for j in range(0, SECTIONS, 2):
        w_left = jnp.concatenate([mine_ref[j, 0:half, :], mine_ref[j + 1, 0:half, :]], axis=1)
        w_right = jnp.concatenate([other_ref[j, 0:half, :], other_ref[j + 1, 0:half, :]], axis=1)
        pre = dot(left, w_left, ((1,), (0,))) + dot(right, w_right, ((1,), (0,)))
        pair = (pre * jax.nn.sigmoid(pre)).astype(BF16)
        act[j] = pair[:, 0:DH]
        act[j + 1] = pair[:, DH:]
    end_0 = lengths_ref[0, 0]
    end_1 = end_0 + lengths_ref[0, 1]
    end_2 = end_1 + lengths_ref[0, 2]
    for c in range(0, tok, step):
        seen = c + step
        row = iota((step, 1), 0) + c
        start = jnp.where(row >= end_0, end_0, 0)
        start = jnp.where(row >= end_1, end_1, start)
        start = jnp.where(row >= end_2, end_2, start)
        col = iota((step, seen), 1)
        visible = (col <= row) & (col >= start)
        heads = []
        total = jnp.zeros((step, 1), F32)
        for h in range(HEADS):
            values = act[HEADS + h, 0:seen, :]
            queries = act[2 * HEADS + h, c:seen, :]
            keys = act[3 * HEADS + h, 0:seen, :]
            scores = dot(queries, keys, ((1,), (1,))) * DH ** (-0.5)
            silu = scores * jax.nn.sigmoid(scores) * (1.0 / MAXLEN)
            weights = jnp.where(visible, silu, 0.0).astype(BF16)
            joined = dot(weights, values, ((1,), (0,))).astype(BF16).astype(F32)
            total = total + jnp.sum(joined * joined, axis=1, keepdims=True)
            heads.append(joined)
        scale = lax.rsqrt(total * (1.0 / width) + epsilon)
        out = tokens_ref[c:seen, :].astype(F32)
        for h in range(HEADS):
            gated = (heads[h] * scale * act[h, c:seen, :].astype(F32)).astype(BF16)
            gated_ref[h, c:seen, :] = gated
            out = out + dot(gated, w_out_ref[h * DH : (h + 1) * DH, :], ((1,), (0,)))
        layer_ref[c:seen, :] = out


def loss_kernel(
    core_ref,
    layer_ref,
    gated_ref,
    recv_ref,
    mine_ref,
    other_ref,
    pos_ref,
    out_ref,
    grad_ref,
    grad_b_ref,
    fetched,
    decoys,
    probs,
    unit,
    back,
):
    tok = layer_ref.shape[0]
    part = NEG // 2
    rows = mine_ref.shape[1] - 16 - BLOCKS * part
    for j in range(PLANE):
        fetched[j * CAP : (j + 1) * CAP, :] = recv_ref[j]
        for ref, half in ((mine_ref, core_ref[0]), (other_ref, 1 - core_ref[0])):
            at = pl.multiple_of(j * NEG + half * part, part)
            for q in range(BLOCKS):
                block = ref[j, rows + q * part : rows + (q + 1) * part, :]
                decoys[pl.ds(at, part), q * LANES : (q + 1) * LANES] = block
    step = 128
    for c in range(0, tok, step):
        layer_out = layer_ref[c : c + step, :]
        placed = one_hot(pos_ref[c : c + step, :] == iota((step, PLANE * CAP), 1))
        clicked = dot(placed, fetched[...], ((1,), (0,)))
        out_scale = lax.rsqrt(jnp.sum(layer_out * layer_out, axis=1, keepdims=True) + epsilon)
        unit_b = (layer_out * out_scale).astype(BF16)
        unit[c : c + step, :] = unit_b
        unit_wide = unit_b.astype(F32)
        target_exp = jnp.exp(jnp.sum(unit_wide * clicked, axis=1, keepdims=True) * logit_scale)
        negative_exp = jnp.exp(dot(unit_b, decoys[...], ((1,), (1,))) * logit_scale)
        totals = target_exp + jnp.sum(negative_exp, axis=1, keepdims=True)
        negative_probs = (negative_exp * (loss_scale / totals)).astype(BF16)
        probs[c : c + step, :] = negative_probs
        target_coef = loss_scale * (target_exp / totals - 1.0)
        back[c : c + step, :] = (target_coef * unit_wide).astype(BF16)
        grad_unit = target_coef * clicked + dot(negative_probs, decoys[...], ((1,), (0,)))
        along = jnp.sum(layer_out * grad_unit, axis=1, keepdims=True)
        grad_out = out_scale * grad_unit - layer_out * (out_scale**3 * along)
        grad_ref[c : c + step, :] = grad_out
        grad_b_ref[c : c + step, :] = grad_out.astype(BF16)
    across = jnp.broadcast_to(pos_ref[...].astype(F32), (tok, LANES)).T[0:1, :].astype(I32)
    group = 4
    for j in range(0, PLANE, group):
        slots = group * CAP
        placed_t = one_hot(iota((slots, tok), 0) + j * CAP == across)
        sent = dot(placed_t, back[...], ((1,), (0,))).astype(BF16)
        negs = dot(probs[:, j * NEG : (j + group) * NEG], unit[...], ((0,), (0,))).astype(BF16)
        weights = dot(gated_ref[j // group], grad_b_ref[...], ((0,), (0,))).astype(BF16)
        for i in range(group):
            out_ref[j + i, 0:CAP, :] = sent[i * CAP : (i + 1) * CAP]
            out_ref[j + i, CAP : CAP + NEG, :] = negs[i * NEG : (i + 1) * NEG]
            out_ref[j + i, CAP + NEG :, :] = weights[i * WROWS : (i + 1) * WROWS]


def half_sums(half, pick_ref, neg_row_ref, returned, negs, weights, ref):
    step = 256
    for b in range(0, HALF, step):
        first = pl.multiple_of(half * HALF + b, step)
        here = one_hot(iota((step, NEG), 0) + first == neg_row_ref[...])
        total = dot(pick_ref[:, pl.ds(first, step)], returned[...], ((0,), (0,)))
        total = total + dot(here, negs, ((1,), (0,)))
        ref[b : b + step, :] = total.astype(BF16)
    part = jnp.where(half == 0, weights[0:SHARED], weights[SHARED:])
    ref[HALF:, :] = part.astype(BF16)


def send_kernel(
    core_ref, recv_ref, pick_ref, neg_row_ref, send_ref, returned, negs_ref, weights_ref
):
    negs = jnp.zeros((NEG, D), F32)
    weights = jnp.zeros((WROWS, D), F32)
    for j in range(PLANE):
        returned[j * CAP : (j + 1) * CAP, :] = recv_ref[j, 0:CAP, :]
        negs = negs + recv_ref[j, CAP : CAP + NEG, :].astype(F32)
        weights = weights + recv_ref[j, CAP + NEG :, :].astype(F32)
    negs = negs.astype(BF16)
    negs_ref[...] = negs
    weights_ref[...] = weights
    half_sums(1 - core_ref[0], pick_ref, neg_row_ref, returned, negs, weights, send_ref)


def keep_kernel(
    core_ref, pick_ref, neg_row_ref, returned, negs_ref, weights_ref, keep_ref
):
    negs, weights = negs_ref[...], weights_ref[...]
    half_sums(core_ref[0], pick_ref, neg_row_ref, returned, negs, weights, keep_ref)


def pair_kernel(keep_ref, other_ref, out_ref, weights_ref):
    for i in range(CHIPS):
        at = slice(i * PIECE, (i + 1) * PIECE)
        out_ref[i] = (keep_ref[at, :].astype(F32) + other_ref[at, :].astype(F32)).astype(BF16)
    weights_ref[...] = (keep_ref[HALF:, :].astype(F32) + other_ref[HALF:, :].astype(F32)).astype(
        BF16
    )


def total_kernel(recv_ref, out_ref):
    total = recv_ref[0].astype(F32)
    for i in range(1, CHIPS):
        total = total + recv_ref[i].astype(F32)
    total = total.astype(BF16)
    for i in range(CHIPS):
        out_ref[i] = total


def weight_kernel(place_ref, mine_ref, other_ref, out_ref):
    core, plane_y, plane_x = place_ref[0], place_ref[1], place_ref[2]
    for ref, half in ((mine_ref, core), (other_ref, 1 - core)):
        for ky in range(4):
            for kx in range(4):
                owner = ((plane_y - ky) & 3) * 4 + ((plane_x - kx) & 3)
                at = pl.multiple_of(owner * WROWS + half * SHARED, SHARED)
                first = (ky * 4 + kx) * SHARED
                rows = ref[first : first + SHARED, :].astype(F32)
                out_ref[pl.ds(at, SHARED), :] = rows * (1.0 / loss_scale)


def finish_kernel(half_ref, grads_ref, items_ref, *rest):
    out_ref = rest[-1]
    for i in range(CHIPS):
        first = i * PIECE
        rows = items_ref[first : first + PIECE, :].astype(F32)
        grads = grads_ref[i].astype(F32)
        scale = lax.rsqrt(jnp.sum(rows * rows, axis=1, keepdims=True) + epsilon)
        along = jnp.sum(rows * grads, axis=1, keepdims=True)
        out_ref[first : first + PIECE, :] = (scale * grads - rows * (scale**3 * along)) * (
            1.0 / loss_scale
        )


def finish(half, grads, items, earlier=None):
    count, width = items.shape
    half_block = pl.BlockSpec((HALF, width), lambda i, half_ref: (half_ref[0], 0))
    operands = [half.reshape(1), grads, items]
    in_specs = [pl.BlockSpec(memory_space=pltpu.VMEM), half_block]
    aliases = {}
    if earlier is not None:
        operands.append(earlier)
        in_specs.append(pl.BlockSpec(memory_space=pl.ANY))
        aliases = {3: 0}
    return pl.pallas_call(
        finish_kernel,
        out_shape=jax.ShapeDtypeStruct((count, width), F32),
        grid_spec=pltpu.PrefetchScalarGridSpec(
            num_scalar_prefetch=1, grid=(1,), in_specs=in_specs, out_specs=half_block
        ),
        input_output_aliases=aliases,
        compiler_params=pltpu.CompilerParams(vmem_limit_bytes=GRANT),
        cost_estimate=pl.CostEstimate(flops=0, bytes_accessed=1 << 21, transcendentals=0),
        name="finish",
    )(*operands)


def local(kernel, outs, operands, scalars=0, scratch=(), grant=GRANT):
    spaces = [pltpu.SMEM] * scalars + [pltpu.VMEM] * (len(operands) - scalars)
    moved = sum(v.size * v.dtype.itemsize for v in operands) + sum(
        v.size * v.dtype.itemsize for v in outs
    )
    return pl.pallas_call(
        kernel,
        out_shape=tuple(outs),
        in_specs=[pl.BlockSpec(memory_space=s) for s in spaces],
        out_specs=tuple(pl.BlockSpec(memory_space=pltpu.VMEM) for _ in outs),
        scratch_shapes=list(scratch),
        compiler_params=pltpu.CompilerParams(vmem_limit_bytes=grant),
        cost_estimate=pl.CostEstimate(flops=0, bytes_accessed=moved, transcendentals=0),
    )(*operands)


def shaped(shape, dtype=BF16):
    return jax.ShapeDtypeStruct(shape, dtype)


def shards(tokens, w_proj, w_out, item_rows, lengths, target_owner, target_row, negative_rows):
    tok_rows = tokens.shape[0]
    width = tokens.shape[1]
    item_count = item_rows.shape[0]
    dp = lax.axis_size("dp")
    slots = PLANE * CAP
    negs = PLANE * NEG
    partners = [(i, i ^ 1) for i in range(dp)]
    columns = [[2 * z + c for z in range(CHIPS)] for c in range(2)]
    core = lax.rem(lax.axis_index("dp"), 2).astype(I32)
    core_s = core.reshape(1)
    plane = lax.axis_index("shard").astype(I32)

    half_w = width // 2
    index = jnp.concatenate([target_owner[:, 0], target_row, negative_rows]).reshape(1, -1)
    first_out, position = local(
        route_kernel,
        [
            shaped((PLANE, half_w + BLOCKS * NEG // 2 + 16, DH)),
            shaped((tok_rows, 1), I32),
        ],
        [core_s, index, w_proj, item_rows],
        scalars=1,
        grant=WIDE_GRANT,
    )
    first_in = exchange(first_out, "shard")

    rows_wide = item_rows.astype(F32)
    item_scale = lax.rsqrt(jnp.sum(rows_wide * rows_wide, axis=1, keepdims=True) + epsilon)
    unit_items = (rows_wide * item_scale).astype(BF16)
    first_in, unit_items = lax.optimization_barrier((first_in, unit_items))
    served, asked_pick = local(
        serve_kernel,
        [shaped((PLANE, CAP, width)), shaped((slots, item_count))],
        [first_in, unit_items],
        grant=WIDE_GRANT,
    )
    served, first_mine = lax.optimization_barrier((served, first_in))
    looked_up = exchange(served, "shard")
    first_other = lax.ppermute(first_mine, "dp", partners)
    layer_out, gated, w_all = local(
        forward_kernel,
        [
            shaped((tok_rows, width), F32),
            shaped((HEADS, tok_rows, DH)),
            shaped((SECTIONS, width, DH)),
        ],
        [core_s, lengths, tokens, first_mine, first_other, w_out],
        scalars=2,
        scratch=[
            pltpu.VMEM((tok_rows, width), BF16),
            pltpu.VMEM((SECTIONS, tok_rows, DH), BF16),
        ],
    )

    third_out, grad_out, grad_out_b = local(
        loss_kernel,
        [
            shaped((PLANE, CAP + NEG + WROWS, width)),
            shaped((tok_rows, width), F32),
            shaped((tok_rows, width)),
        ],
        [core_s, layer_out, gated, looked_up, first_mine, first_other, position],
        scalars=1,
        scratch=[
            pltpu.VMEM((slots, width), BF16),
            pltpu.VMEM((negs, width), BF16),
            pltpu.VMEM((tok_rows, negs), BF16),
            pltpu.VMEM((tok_rows, width), BF16),
            pltpu.VMEM((tok_rows, width), BF16),
        ],
        grant=WIDE_GRANT,
    )
    third_in = exchange(third_out, "shard")

    (normed,) = local(norm_kernel, [shaped((tok_rows, width))], [tokens, grad_out_b])
    grad_out_b, w_all, normed, tokens = lax.optimization_barrier(
        (grad_out_b, w_all, normed, tokens)
    )
    visible = history_mask(lengths[0], tok_rows)[None]
    wide_tokens = tokens.astype(F32)
    input_scale = lax.rsqrt(jnp.mean(wide_tokens * wide_tokens, axis=1, keepdims=True) + epsilon)
    normed_s = jnp.broadcast_to(normed[None], (SECTIONS, tok_rows, width))
    pre_act = dot(normed_s, w_all, ((2,), (1,)), ((0,), (0,)))
    activated = jax.nn.silu(pre_act).astype(BF16)
    gate, values, queries, keys = (activated[i * HEADS : (i + 1) * HEADS] for i in range(4))
    scores = dot(queries, keys, ((2,), (2,)), ((0,), (0,))) * DH ** (-0.5)
    score_sig = jax.nn.sigmoid(scores)
    weights = jnp.where(visible, scores * score_sig * (1.0 / MAXLEN), 0.0).astype(BF16)
    joined = dot(weights, values, ((2,), (1,)), ((0,), (0,))).astype(BF16)
    joined_wide = joined.astype(F32)
    middle_scale = lax.rsqrt(
        jnp.sum(joined_wide * joined_wide, axis=(0, 2), keepdims=True) / width + epsilon
    )
    gate_wide = gate.astype(F32)
    w_out_h = w_out.reshape(HEADS, DH, width)
    grad_gated = dot(
        jnp.broadcast_to(grad_out_b[None], (HEADS, tok_rows, width)),
        w_out_h,
        ((2,), (2,)),
        ((0,), (0,)),
    )
    grad_gate = grad_gated * joined_wide * middle_scale
    grad_norm = grad_gated * gate_wide
    grad_joined = middle_scale * grad_norm - joined_wide * middle_scale**3 * (
        jnp.sum(joined_wide * grad_norm, axis=(0, 2), keepdims=True) / width
    )
    grad_joined_b = grad_joined.astype(BF16)
    grad_weights = dot(grad_joined_b, values, ((2,), (2,)), ((0,), (0,)))
    grad_values = dot(weights, grad_joined_b, ((1,), (1,)), ((0,), (0,)))
    slope = score_sig * (1.0 + scores * (1.0 - score_sig))
    grad_scores = jnp.where(
        visible, grad_weights * (1.0 / MAXLEN) * slope * DH ** (-0.5), 0.0
    ).astype(BF16)
    grad_queries = dot(grad_scores, keys, ((2,), (1,)), ((0,), (0,)))
    grad_keys = dot(grad_scores, queries, ((1,), (1,)), ((0,), (0,)))
    grad_act = jnp.concatenate([grad_gate, grad_values, grad_queries, grad_keys], axis=0)
    grad_pre = (grad_act * silu_slope(pre_act)).astype(BF16)
    grad_normed = jnp.sum(dot(grad_pre, w_all, ((2,), (2,)), ((0,), (0,))), axis=0)
    grad_input = input_scale * grad_normed - wide_tokens * input_scale**3 * jnp.mean(
        wide_tokens * grad_normed, axis=1, keepdims=True
    )
    grad_tokens = (grad_out + grad_input).astype(BF16)
    third_in, grad_tokens = lax.optimization_barrier((third_in, grad_tokens))

    neg_row = negative_rows.reshape(1, NEG)
    sent, returned, neg_sum, w_sum = local(
        send_kernel,
        [
            shaped((HALF + SHARED, width)),
            shaped((slots, width)),
            shaped((NEG, width)),
            shaped((WROWS, width), F32),
        ],
        [core_s, third_in, asked_pick, neg_row],
        scalars=1,
    )
    arrived = lax.ppermute(sent, "dp", partners)
    (kept,) = local(
        keep_kernel,
        [shaped((HALF + SHARED, width))],
        [core_s, asked_pick, neg_row, returned, neg_sum, w_sum],
        scalars=1,
    )
    pieces, w_rows = local(
        pair_kernel, [shaped((CHIPS, PIECE, width)), shaped((SHARED, width))], [kept, arrived]
    )
    pieces = exchange(pieces, "dp", columns)
    for k in range(4):
        crossed = lax.ppermute(w_rows, "dp", [(i, i ^ (2 << k)) for i in range(dp)])
        w_rows = (w_rows.astype(F32) + crossed.astype(F32)).astype(BF16)
    pieces, w_rows = lax.optimization_barrier((pieces, w_rows))
    (summed,) = local(total_kernel, [shaped((CHIPS, PIECE, width))], [pieces])
    mine = exchange(summed, "dp", columns)

    def turned(rows, step_y, step_x):
        moves = [
            (y * 4 + x, (y + step_y) % 4 * 4 + (x + step_x) % 4) for y in range(4) for x in range(4)
        ]
        return lax.ppermute(rows, "shard", moves)

    w_rows = jnp.concatenate([w_rows] + [turned(w_rows, 0, k) for k in (1, 2, 3)], axis=0)
    w_rows = jnp.concatenate([w_rows] + [turned(w_rows, k, 0) for k in (1, 2, 3)], axis=0)
    w_other_rows = lax.ppermute(w_rows, "dp", partners)
    (weight_grads,) = local(
        weight_kernel,
        [shaped((width, width), F32)],
        [jnp.stack([core, plane >> 2, plane & 3]), w_rows, w_other_rows],
        scalars=1,
    )
    mine, weight_grads = lax.optimization_barrier((mine, weight_grads))
    other = lax.ppermute(mine, "dp", partners)
    item_grads = finish(1 - core, other, item_rows, finish(core, mine, item_rows))
    return (grad_tokens, weight_grads, item_grads)


def solution(mesh):
    in_specs = (
        P(("dp", "shard"), None),
        P(None, "shard"),
        P(),
        P("shard", None),
        P(("dp", "shard"), None),
        P(("dp", "shard"), None),
        P(("dp", "shard")),
        P("shard"),
    )
    out_specs = (P(("dp", "shard"), None), P(), P("shard", None))
    return jax.shard_map(
        shards, mesh=mesh, in_specs=in_specs, out_specs=out_specs, check_vma=False
    )
```

```python
import jax
import jax.numpy as jnp
from jax import lax
from jax.experimental import pallas as pl
from jax.experimental.pallas import tpu as pltpu
from jax.sharding import PartitionSpec as P

D = 512
HEADS = 4
DH = 128
MAXLEN = 192
SECTIONS = 4 * HEADS
PLANE = 16
CAP = 48
NEG = 64
WROWS = 32
CHIPS = 16
NEAR = 4
FAR = 4
HALF = 512
PIECE = 32
SHARED = 16
LANES = 128
BLOCKS = D // LANES
GRANT = 24 * 1024 * 1024
WIDE_GRANT = 56 * 1024 * 1024

epsilon = 1e-06
logit_scale = 64.0
loss_scale = 512.0

F32 = jnp.float32
BF16 = jnp.bfloat16
I32 = jnp.int32


def dot(a, b, contract, batch=((), ())):
    return lax.dot_general(a, b, (contract, batch), preferred_element_type=F32)


def iota(shape, axis):
    return lax.broadcasted_iota(I32, shape, axis)


def one_hot(mask):
    return jnp.where(mask, 1.0, 0.0).astype(BF16)


def silu_slope(values):
    sigmoid = jax.nn.sigmoid(values)
    return sigmoid * (1.0 + values * (1.0 - sigmoid))


def history_mask(lengths_row, rows_count):
    history_ends = jnp.cumsum(lengths_row)
    positions = jnp.arange(rows_count, dtype=jnp.int32)
    history_ids = jnp.sum((positions[:, None] >= history_ends[None, :-1]).astype(jnp.int32), axis=1)
    return (history_ids[:, None] == history_ids[None, :]) & (
        positions[None, :] <= positions[:, None]
    )


def exchange(pieces, axis, groups=None):
    return lax.all_to_all(
        pieces, axis, split_axis=0, concat_axis=0, tiled=True, axis_index_groups=groups
    )


def route_kernel(core_ref, index_ref, w_ref, items_ref, out_ref, pos_ref):
    tok = pos_ref.shape[0]
    first = core_ref[0] == 0
    owners = jnp.broadcast_to(index_ref[0:1, 0:tok].astype(F32), (LANES, tok)).T.astype(I32)
    hits = owners == iota((tok, LANES), 1)
    earlier = one_hot(iota((tok, tok), 1) < iota((tok, tok), 0))
    before = dot(earlier, one_hot(hits), ((1,), (0,)))
    slot = jnp.sum(jnp.where(hits, before, 0.0), axis=1, keepdims=True).astype(I32)
    owners = owners[:, 0:1]
    pos_ref[...] = owners * CAP + slot
    spread = one_hot(owners * LANES + slot == iota((tok, PLANE * LANES), 1))
    asked = jnp.broadcast_to(index_ref[0:1, tok : 2 * tok], (16, tok))
    which = iota((16, tok), 0)
    digits = jnp.where(which == 0, asked >> 5, jnp.where(which == 1, asked & 31, 0))
    requests = dot(digits.astype(F32).astype(BF16), spread, ((1,), (0,))).astype(BF16)
    here = one_hot(iota((items_ref.shape[0], NEG), 0) == index_ref[0:1, 2 * tok :])
    negs = dot(here, items_ref[...], ((0,), (0,)))
    negs = jnp.where(first, negs[0 : NEG // 2], negs[NEG // 2 :])
    scale = lax.rsqrt(jnp.sum(negs * negs, axis=1, keepdims=True) + epsilon)
    negs = (negs * scale).astype(BF16)
    rows = w_ref.shape[0] // 2
    own = w_ref[pl.ds(pl.multiple_of(core_ref[0] * rows, rows), rows), :]
    for j in range(PLANE):
        out_ref[j, 0:rows, :] = own
        for q in range(BLOCKS):
            at = rows + q * (NEG // 2)
            out_ref[j, at : at + NEG // 2, :] = negs[:, q * LANES : (q + 1) * LANES]
        at = rows + BLOCKS * (NEG // 2)
        out_ref[j, at : at + 16, :] = requests[:, j * LANES : (j + 1) * LANES]


def serve_kernel(recv_ref, items_ref, out_ref, pick_ref):
    rows = recv_ref.shape[1] - 16
    count = items_ref.shape[0]
    diagonal = iota((CAP, LANES), 0) == iota((CAP, LANES), 1)
    for j in range(PLANE):
        digits = recv_ref[j, rows : rows + 16, :].astype(F32)
        asked = 32.0 * digits[0:1] + digits[1:2]
        column = jnp.sum(
            jnp.where(diagonal, jnp.broadcast_to(asked, (CAP, LANES)), 0.0), axis=1, keepdims=True
        ).astype(I32)
        pick_ref[j * CAP : (j + 1) * CAP, :] = one_hot(column == iota((CAP, count), 1))
    step = 4
    for j in range(0, PLANE, step):
        served = dot(pick_ref[j * CAP : (j + step) * CAP, :], items_ref[...], ((1,), (0,)))
        served = served.astype(BF16)
        for i in range(step):
            out_ref[j + i] = served[i * CAP : (i + 1) * CAP]


def normalize(tokens_ref, normed_ref):
    step = 128
    for c in range(0, tokens_ref.shape[0], step):
        wide = tokens_ref[c : c + step, :].astype(F32)
        scale = lax.rsqrt(jnp.mean(wide * wide, axis=1, keepdims=True) + epsilon)
        normed_ref[c : c + step, :] = (wide * scale).astype(BF16)


def norm_kernel(tokens_ref, after_ref, normed_ref):
    normalize(tokens_ref, normed_ref)


def forward_kernel(
    core_ref,
    lengths_ref,
    tokens_ref,
    mine_ref,
    other_ref,
    w_out_ref,
    layer_ref,
    gated_ref,
    w_all_ref,
    normed,
    act,
):
    tok, width = tokens_ref.shape
    core = core_ref[0]
    half = width // 2
    step = 128
    normalize(tokens_ref, normed)
    left = normed[:, pl.ds(pl.multiple_of(core * half, half), half)]
    right = normed[:, pl.ds(pl.multiple_of((1 - core) * half, half), half)]
    for ref, part in ((mine_ref, core), (other_ref, 1 - core)):
        at = pl.multiple_of(part * half, half)
        for j in range(SECTIONS):
            w_all_ref[j, pl.ds(at, half), :] = ref[j, 0:half, :]
    for j in range(0, SECTIONS, 2):
        w_left = jnp.concatenate([mine_ref[j, 0:half, :], mine_ref[j + 1, 0:half, :]], axis=1)
        w_right = jnp.concatenate([other_ref[j, 0:half, :], other_ref[j + 1, 0:half, :]], axis=1)
        pre = dot(left, w_left, ((1,), (0,))) + dot(right, w_right, ((1,), (0,)))
        pair = (pre * jax.nn.sigmoid(pre)).astype(BF16)
        act[j] = pair[:, 0:DH]
        act[j + 1] = pair[:, DH:]
    end_0 = lengths_ref[0, 0]
    end_1 = end_0 + lengths_ref[0, 1]
    end_2 = end_1 + lengths_ref[0, 2]
    for c in range(0, tok, step):
        seen = c + step
        row = iota((step, 1), 0) + c
        start = jnp.where(row >= end_0, end_0, 0)
        start = jnp.where(row >= end_1, end_1, start)
        start = jnp.where(row >= end_2, end_2, start)
        col = iota((step, seen), 1)
        visible = (col <= row) & (col >= start)
        heads = []
        total = jnp.zeros((step, 1), F32)
        for h in range(HEADS):
            values = act[HEADS + h, 0:seen, :]
            queries = act[2 * HEADS + h, c:seen, :]
            keys = act[3 * HEADS + h, 0:seen, :]
            scores = dot(queries, keys, ((1,), (1,))) * DH ** (-0.5)
            silu = scores * jax.nn.sigmoid(scores) * (1.0 / MAXLEN)
            weights = jnp.where(visible, silu, 0.0).astype(BF16)
            joined = dot(weights, values, ((1,), (0,))).astype(BF16).astype(F32)
            total = total + jnp.sum(joined * joined, axis=1, keepdims=True)
            heads.append(joined)
        scale = lax.rsqrt(total * (1.0 / width) + epsilon)
        out = tokens_ref[c:seen, :].astype(F32)
        for h in range(HEADS):
            gated = (heads[h] * scale * act[h, c:seen, :].astype(F32)).astype(BF16)
            gated_ref[h, c:seen, :] = gated
            out = out + dot(gated, w_out_ref[h * DH : (h + 1) * DH, :], ((1,), (0,)))
        layer_ref[c:seen, :] = out


def loss_kernel(
    core_ref,
    layer_ref,
    gated_ref,
    recv_ref,
    mine_ref,
    other_ref,
    pos_ref,
    out_ref,
    grad_ref,
    grad_b_ref,
    fetched,
    decoys,
    probs,
    unit,
    back,
):
    tok = layer_ref.shape[0]
    part = NEG // 2
    rows = mine_ref.shape[1] - 16 - BLOCKS * part
    for j in range(PLANE):
        fetched[j * CAP : (j + 1) * CAP, :] = recv_ref[j]
        for ref, half in ((mine_ref, core_ref[0]), (other_ref, 1 - core_ref[0])):
            at = pl.multiple_of(j * NEG + half * part, part)
            for q in range(BLOCKS):
                block = ref[j, rows + q * part : rows + (q + 1) * part, :]
                decoys[pl.ds(at, part), q * LANES : (q + 1) * LANES] = block
    step = 128
    for c in range(0, tok, step):
        layer_out = layer_ref[c : c + step, :]
        placed = one_hot(pos_ref[c : c + step, :] == iota((step, PLANE * CAP), 1))
        clicked = dot(placed, fetched[...], ((1,), (0,)))
        out_scale = lax.rsqrt(jnp.sum(layer_out * layer_out, axis=1, keepdims=True) + epsilon)
        unit_b = (layer_out * out_scale).astype(BF16)
        unit[c : c + step, :] = unit_b
        unit_wide = unit_b.astype(F32)
        target_exp = jnp.exp(jnp.sum(unit_wide * clicked, axis=1, keepdims=True) * logit_scale)
        negative_exp = jnp.exp(dot(unit_b, decoys[...], ((1,), (1,))) * logit_scale)
        totals = target_exp + jnp.sum(negative_exp, axis=1, keepdims=True)
        negative_probs = (negative_exp * (loss_scale / totals)).astype(BF16)
        probs[c : c + step, :] = negative_probs
        target_coef = loss_scale * (target_exp / totals - 1.0)
        back[c : c + step, :] = (target_coef * unit_wide).astype(BF16)
        grad_unit = target_coef * clicked + dot(negative_probs, decoys[...], ((1,), (0,)))
        along = jnp.sum(layer_out * grad_unit, axis=1, keepdims=True)
        grad_out = out_scale * grad_unit - layer_out * (out_scale**3 * along)
        grad_ref[c : c + step, :] = grad_out
        grad_b_ref[c : c + step, :] = grad_out.astype(BF16)
    across = jnp.broadcast_to(pos_ref[...].astype(F32), (tok, LANES)).T[0:1, :].astype(I32)
    group = 4
    for j in range(0, PLANE, group):
        slots = group * CAP
        placed_t = one_hot(iota((slots, tok), 0) + j * CAP == across)
        sent = dot(placed_t, back[...], ((1,), (0,))).astype(BF16)
        negs = dot(probs[:, j * NEG : (j + group) * NEG], unit[...], ((0,), (0,))).astype(BF16)
        weights = dot(gated_ref[j // group], grad_b_ref[...], ((0,), (0,))).astype(BF16)
        for i in range(group):
            out_ref[j + i, 0:CAP, :] = sent[i * CAP : (i + 1) * CAP]
            out_ref[j + i, CAP : CAP + NEG, :] = negs[i * NEG : (i + 1) * NEG]
            out_ref[j + i, CAP + NEG :, :] = weights[i * WROWS : (i + 1) * WROWS]


def half_sums(half, pick_ref, neg_row_ref, returned, negs, weights, ref):
    step = 256
    for b in range(0, HALF, step):
        first = pl.multiple_of(half * HALF + b, step)
        here = one_hot(iota((step, NEG), 0) + first == neg_row_ref[...])
        total = dot(pick_ref[:, pl.ds(first, step)], returned[...], ((0,), (0,)))
        total = total + dot(here, negs, ((1,), (0,)))
        ref[b : b + step, :] = total.astype(BF16)
    part = jnp.where(half == 0, weights[0:SHARED], weights[SHARED:])
    ref[HALF:, :] = part.astype(BF16)


def send_kernel(
    core_ref, recv_ref, pick_ref, neg_row_ref, send_ref, returned, negs_ref, weights_ref
):
    negs = jnp.zeros((NEG, D), F32)
    weights = jnp.zeros((WROWS, D), F32)
    for j in range(PLANE):
        returned[j * CAP : (j + 1) * CAP, :] = recv_ref[j, 0:CAP, :]
        negs = negs + recv_ref[j, CAP : CAP + NEG, :].astype(F32)
        weights = weights + recv_ref[j, CAP + NEG :, :].astype(F32)
    negs = negs.astype(BF16)
    negs_ref[...] = negs
    weights_ref[...] = weights
    half_sums(1 - core_ref[0], pick_ref, neg_row_ref, returned, negs, weights, send_ref)


def keep_kernel(
    core_ref, pick_ref, neg_row_ref, returned, negs_ref, weights_ref, keep_ref
):
    negs, weights = negs_ref[...], weights_ref[...]
    half_sums(core_ref[0], pick_ref, neg_row_ref, returned, negs, weights, keep_ref)


def near_kernel(keep_ref, other_ref, out_ref):
    rows = HALF // NEAR
    weights = (keep_ref[HALF:, :].astype(F32) + other_ref[HALF:, :].astype(F32)).astype(BF16)
    for i in range(NEAR):
        at = slice(i * rows, (i + 1) * rows)
        total = keep_ref[at, :].astype(F32) + other_ref[at, :].astype(F32)
        out_ref[i, 0:rows, :] = total.astype(BF16)
        out_ref[i, rows:, :] = weights


def far_kernel(recv_ref, out_ref):
    rows = recv_ref.shape[1] - SHARED
    total = recv_ref[0].astype(F32)
    for i in range(1, NEAR):
        total = total + recv_ref[i].astype(F32)
    total = total.astype(BF16)
    for i in range(FAR):
        out_ref[i, 0:PIECE, :] = total[i * PIECE : (i + 1) * PIECE]
        out_ref[i, PIECE:, :] = total[rows:]


def total_kernel(recv_ref, out_ref, weights_ref):
    total = recv_ref[0].astype(F32)
    for i in range(1, FAR):
        total = total + recv_ref[i].astype(F32)
    total = total.astype(BF16)
    for i in range(CHIPS):
        out_ref[i] = total[0:PIECE]
    weights_ref[...] = total[PIECE:]


def weight_kernel(place_ref, mine_ref, other_ref, out_ref):
    core, plane = place_ref[0], place_ref[1]
    for ref, half in ((mine_ref, core), (other_ref, 1 - core)):
        for p in range(PLANE):
            at = pl.multiple_of((plane ^ p) * WROWS + half * SHARED, SHARED)
            rows = ref[p * SHARED : (p + 1) * SHARED, :].astype(F32)
            out_ref[pl.ds(at, SHARED), :] = rows * (1.0 / loss_scale)


def finish_kernel(half_ref, grads_ref, items_ref, *rest):
    out_ref = rest[-1]
    for i in range(CHIPS):
        first = (i % NEAR) * (HALF // NEAR) + (i // NEAR) * PIECE
        rows = items_ref[first : first + PIECE, :].astype(F32)
        grads = grads_ref[i].astype(F32)
        scale = lax.rsqrt(jnp.sum(rows * rows, axis=1, keepdims=True) + epsilon)
        along = jnp.sum(rows * grads, axis=1, keepdims=True)
        out_ref[first : first + PIECE, :] = (scale * grads - rows * (scale**3 * along)) * (
            1.0 / loss_scale
        )


def finish(half, grads, items, earlier=None):
    count, width = items.shape
    half_block = pl.BlockSpec((HALF, width), lambda i, half_ref: (half_ref[0], 0))
    operands = [half.reshape(1), grads, items]
    in_specs = [pl.BlockSpec(memory_space=pltpu.VMEM), half_block]
    aliases = {}
    if earlier is not None:
        operands.append(earlier)
        in_specs.append(pl.BlockSpec(memory_space=pl.ANY))
        aliases = {3: 0}
    return pl.pallas_call(
        finish_kernel,
        out_shape=jax.ShapeDtypeStruct((count, width), F32),
        grid_spec=pltpu.PrefetchScalarGridSpec(
            num_scalar_prefetch=1, grid=(1,), in_specs=in_specs, out_specs=half_block
        ),
        input_output_aliases=aliases,
        compiler_params=pltpu.CompilerParams(vmem_limit_bytes=GRANT),
        cost_estimate=pl.CostEstimate(flops=0, bytes_accessed=1 << 21, transcendentals=0),
        name="finish",
    )(*operands)


def local(kernel, outs, operands, scalars=0, scratch=(), grant=GRANT):
    spaces = [pltpu.SMEM] * scalars + [pltpu.VMEM] * (len(operands) - scalars)
    moved = sum(v.size * v.dtype.itemsize for v in operands) + sum(
        v.size * v.dtype.itemsize for v in outs
    )
    return pl.pallas_call(
        kernel,
        out_shape=tuple(outs),
        in_specs=[pl.BlockSpec(memory_space=s) for s in spaces],
        out_specs=tuple(pl.BlockSpec(memory_space=pltpu.VMEM) for _ in outs),
        scratch_shapes=list(scratch),
        compiler_params=pltpu.CompilerParams(vmem_limit_bytes=grant),
        cost_estimate=pl.CostEstimate(flops=0, bytes_accessed=moved, transcendentals=0),
    )(*operands)


def shaped(shape, dtype=BF16):
    return jax.ShapeDtypeStruct(shape, dtype)


def shards(tokens, w_proj, w_out, item_rows, lengths, target_owner, target_row, negative_rows):
    tok_rows = tokens.shape[0]
    width = tokens.shape[1]
    item_count = item_rows.shape[0]
    dp = lax.axis_size("dp")
    slots = PLANE * CAP
    negs = PLANE * NEG
    partners = [(i, i ^ 1) for i in range(dp)]
    columns = [[2 * z + c for z in range(CHIPS)] for c in range(2)]
    near = [[2 * (NEAR * h + l) + c for l in range(NEAR)] for h in range(FAR) for c in range(2)]
    far = [[2 * (NEAR * h + l) + c for h in range(FAR)] for l in range(NEAR) for c in range(2)]
    core = lax.rem(lax.axis_index("dp"), 2).astype(I32)
    core_s = core.reshape(1)
    plane = lax.axis_index("shard").astype(I32)

    half_w = width // 2
    index = jnp.concatenate([target_owner[:, 0], target_row, negative_rows]).reshape(1, -1)
    first_out, position = local(
        route_kernel,
        [
            shaped((PLANE, half_w + BLOCKS * NEG // 2 + 16, DH)),
            shaped((tok_rows, 1), I32),
        ],
        [core_s, index, w_proj, item_rows],
        scalars=1,
        grant=WIDE_GRANT,
    )
    first_in = exchange(first_out, "shard")

    rows_wide = item_rows.astype(F32)
    item_scale = lax.rsqrt(jnp.sum(rows_wide * rows_wide, axis=1, keepdims=True) + epsilon)
    unit_items = (rows_wide * item_scale).astype(BF16)
    first_in, unit_items = lax.optimization_barrier((first_in, unit_items))
    served, asked_pick = local(
        serve_kernel,
        [shaped((PLANE, CAP, width)), shaped((slots, item_count))],
        [first_in, unit_items],
        grant=WIDE_GRANT,
    )
    served, first_mine = lax.optimization_barrier((served, first_in))
    looked_up = exchange(served, "shard")
    first_other = lax.ppermute(first_mine, "dp", partners)
    layer_out, gated, w_all = local(
        forward_kernel,
        [
            shaped((tok_rows, width), F32),
            shaped((HEADS, tok_rows, DH)),
            shaped((SECTIONS, width, DH)),
        ],
        [core_s, lengths, tokens, first_mine, first_other, w_out],
        scalars=2,
        scratch=[
            pltpu.VMEM((tok_rows, width), BF16),
            pltpu.VMEM((SECTIONS, tok_rows, DH), BF16),
        ],
        grant=56 * 1024 * 1024,
    )

    third_out, grad_out, grad_out_b = local(
        loss_kernel,
        [
            shaped((PLANE, CAP + NEG + WROWS, width)),
            shaped((tok_rows, width), F32),
            shaped((tok_rows, width)),
        ],
        [core_s, layer_out, gated, looked_up, first_mine, first_other, position],
        scalars=1,
        scratch=[
            pltpu.VMEM((slots, width), BF16),
            pltpu.VMEM((negs, width), BF16),
            pltpu.VMEM((tok_rows, negs), BF16),
            pltpu.VMEM((tok_rows, width), BF16),
            pltpu.VMEM((tok_rows, width), BF16),
        ],
        grant=56 * 1024 * 1024,
    )
    third_in = exchange(third_out, "shard")

    (normed,) = local(norm_kernel, [shaped((tok_rows, width))], [tokens, grad_out_b])
    grad_out_b, w_all, normed, tokens = lax.optimization_barrier(
        (grad_out_b, w_all, normed, tokens)
    )
    visible = history_mask(lengths[0], tok_rows)[None]
    wide_tokens = tokens.astype(F32)
    input_scale = lax.rsqrt(jnp.mean(wide_tokens * wide_tokens, axis=1, keepdims=True) + epsilon)
    normed_s = jnp.broadcast_to(normed[None], (SECTIONS, tok_rows, width))
    pre_act = dot(normed_s, w_all, ((2,), (1,)), ((0,), (0,)))
    activated = jax.nn.silu(pre_act).astype(BF16)
    gate, values, queries, keys = (activated[i * HEADS : (i + 1) * HEADS] for i in range(4))
    scores = dot(queries, keys, ((2,), (2,)), ((0,), (0,))) * DH ** (-0.5)
    score_sig = jax.nn.sigmoid(scores)
    weights = jnp.where(visible, scores * score_sig * (1.0 / MAXLEN), 0.0).astype(BF16)
    joined = dot(weights, values, ((2,), (1,)), ((0,), (0,))).astype(BF16)
    joined_wide = joined.astype(F32)
    middle_scale = lax.rsqrt(
        jnp.sum(joined_wide * joined_wide, axis=(0, 2), keepdims=True) / width + epsilon
    )
    gate_wide = gate.astype(F32)
    w_out_h = w_out.reshape(HEADS, DH, width)
    grad_gated = dot(
        jnp.broadcast_to(grad_out_b[None], (HEADS, tok_rows, width)),
        w_out_h,
        ((2,), (2,)),
        ((0,), (0,)),
    )
    grad_gate = grad_gated * joined_wide * middle_scale
    grad_norm = grad_gated * gate_wide
    grad_joined = middle_scale * grad_norm - joined_wide * middle_scale**3 * (
        jnp.sum(joined_wide * grad_norm, axis=(0, 2), keepdims=True) / width
    )
    grad_joined_b = grad_joined.astype(BF16)
    grad_weights = dot(grad_joined_b, values, ((2,), (2,)), ((0,), (0,)))
    grad_values = dot(weights, grad_joined_b, ((1,), (1,)), ((0,), (0,)))
    slope = score_sig * (1.0 + scores * (1.0 - score_sig))
    grad_scores = jnp.where(
        visible, grad_weights * (1.0 / MAXLEN) * slope * DH ** (-0.5), 0.0
    ).astype(BF16)
    grad_queries = dot(grad_scores, keys, ((2,), (1,)), ((0,), (0,)))
    grad_keys = dot(grad_scores, queries, ((1,), (1,)), ((0,), (0,)))
    grad_act = jnp.concatenate([grad_gate, grad_values, grad_queries, grad_keys], axis=0)
    grad_pre = (grad_act * silu_slope(pre_act)).astype(BF16)
    grad_normed = jnp.sum(dot(grad_pre, w_all, ((2,), (2,)), ((0,), (0,))), axis=0)
    grad_input = input_scale * grad_normed - wide_tokens * input_scale**3 * jnp.mean(
        wide_tokens * grad_normed, axis=1, keepdims=True
    )
    grad_tokens = (grad_out + grad_input).astype(BF16)
    third_in, grad_tokens = lax.optimization_barrier((third_in, grad_tokens))

    neg_row = negative_rows.reshape(1, NEG)
    sent, returned, neg_sum, w_sum = local(
        send_kernel,
        [
            shaped((HALF + SHARED, width)),
            shaped((slots, width)),
            shaped((NEG, width)),
            shaped((WROWS, width), F32),
        ],
        [core_s, third_in, asked_pick, neg_row],
        scalars=1,
    )
    arrived = lax.ppermute(sent, "dp", partners)
    (kept,) = local(
        keep_kernel,
        [shaped((HALF + SHARED, width))],
        [core_s, asked_pick, neg_row, returned, neg_sum, w_sum],
        scalars=1,
    )
    (near_out,) = local(
        near_kernel, [shaped((NEAR, HALF // NEAR + SHARED, width))], [kept, arrived]
    )
    (far_out,) = local(
        far_kernel, [shaped((FAR, PIECE + SHARED, width))], [exchange(near_out, "dp", near)]
    )
    summed, w_rows = local(
        total_kernel,
        [shaped((CHIPS, PIECE, width)), shaped((SHARED, width))],
        [exchange(far_out, "dp", far)],
    )
    mine = exchange(summed, "dp", columns)

    for k in range(4):
        others = lax.ppermute(w_rows, "shard", [(i, i ^ (1 << k)) for i in range(PLANE)])
        w_rows = jnp.concatenate([w_rows, others], axis=0)
    w_other_rows = lax.ppermute(w_rows, "dp", partners)
    (weight_grads,) = local(
        weight_kernel,
        [shaped((width, width), F32)],
        [jnp.stack([core, plane]), w_rows, w_other_rows],
        scalars=1,
    )
    mine, weight_grads = lax.optimization_barrier((mine, weight_grads))
    other = lax.ppermute(mine, "dp", partners)
    item_grads = finish(1 - core, other, item_rows, finish(core, mine, item_rows))
    return (grad_tokens, weight_grads, item_grads)


def solution(mesh):
    in_specs = (
        P(("dp", "shard"), None),
        P(None, "shard"),
        P(),
        P("shard", None),
        P(("dp", "shard"), None),
        P(("dp", "shard"), None),
        P(("dp", "shard")),
        P("shard"),
    )
    out_specs = (P(("dp", "shard"), None), P(), P("shard", None))
    return jax.shard_map(
        shards, mesh=mesh, in_specs=in_specs, out_specs=out_specs, check_vma=False
    )
```

```python
import jax
import jax.numpy as jnp
from jax import lax
from jax.experimental import pallas as pl
from jax.experimental.pallas import tpu as pltpu
from jax.sharding import PartitionSpec as P

D = 512
HEADS = 4
DH = 128
MAXLEN = 192
SECTIONS = 4 * HEADS
PLANE = 16
CAP = 48
NEG = 64
WROWS = 32
CHIPS = 16
NEAR = 4
FAR = 4
HALF = 512
PIECE = 32
SHARED = 16
LANES = 128
BLOCKS = D // LANES
CHAIN_BITS = ((1, 2, 4, 8), (4, 8, 1, 2))
GRANT = 24 * 1024 * 1024
WIDE_GRANT = 56 * 1024 * 1024

epsilon = 1e-06
logit_scale = 64.0
loss_scale = 512.0

F32 = jnp.float32
BF16 = jnp.bfloat16
I32 = jnp.int32


def dot(a, b, contract, batch=((), ())):
    return lax.dot_general(a, b, (contract, batch), preferred_element_type=F32)


def iota(shape, axis):
    return lax.broadcasted_iota(I32, shape, axis)


def one_hot(mask):
    return jnp.where(mask, 1.0, 0.0).astype(BF16)


def silu_slope(values):
    sigmoid = jax.nn.sigmoid(values)
    return sigmoid * (1.0 + values * (1.0 - sigmoid))


def history_mask(lengths_row, rows_count):
    history_ends = jnp.cumsum(lengths_row)
    positions = jnp.arange(rows_count, dtype=jnp.int32)
    history_ids = jnp.sum((positions[:, None] >= history_ends[None, :-1]).astype(jnp.int32), axis=1)
    return (history_ids[:, None] == history_ids[None, :]) & (
        positions[None, :] <= positions[:, None]
    )


def exchange(pieces, axis, groups=None):
    return lax.all_to_all(
        pieces, axis, split_axis=0, concat_axis=0, tiled=True, axis_index_groups=groups
    )


def route_kernel(core_ref, index_ref, w_ref, items_ref, out_ref, pos_ref):
    tok = pos_ref.shape[0]
    first = core_ref[0] == 0
    owners = jnp.broadcast_to(index_ref[0:1, 0:tok].astype(F32), (LANES, tok)).T.astype(I32)
    hits = owners == iota((tok, LANES), 1)
    earlier = one_hot(iota((tok, tok), 1) < iota((tok, tok), 0))
    before = dot(earlier, one_hot(hits), ((1,), (0,)))
    slot = jnp.sum(jnp.where(hits, before, 0.0), axis=1, keepdims=True).astype(I32)
    owners = owners[:, 0:1]
    pos_ref[...] = owners * CAP + slot
    spread = one_hot(owners * LANES + slot == iota((tok, PLANE * LANES), 1))
    asked = jnp.broadcast_to(index_ref[0:1, tok : 2 * tok], (16, tok))
    which = iota((16, tok), 0)
    digits = jnp.where(which == 0, asked >> 5, jnp.where(which == 1, asked & 31, 0))
    requests = dot(digits.astype(F32).astype(BF16), spread, ((1,), (0,))).astype(BF16)
    here = one_hot(iota((items_ref.shape[0], NEG), 0) == index_ref[0:1, 2 * tok :])
    negs = dot(here, items_ref[...], ((0,), (0,)))
    negs = jnp.where(first, negs[0 : NEG // 2], negs[NEG // 2 :])
    scale = lax.rsqrt(jnp.sum(negs * negs, axis=1, keepdims=True) + epsilon)
    negs = (negs * scale).astype(BF16)
    rows = w_ref.shape[0] // 2
    own = w_ref[pl.ds(pl.multiple_of(core_ref[0] * rows, rows), rows), :]
    for j in range(PLANE):
        out_ref[j, 0:rows, :] = own
        for q in range(BLOCKS):
            at = rows + q * (NEG // 2)
            out_ref[j, at : at + NEG // 2, :] = negs[:, q * LANES : (q + 1) * LANES]
        at = rows + BLOCKS * (NEG // 2)
        out_ref[j, at : at + 16, :] = requests[:, j * LANES : (j + 1) * LANES]


def serve_kernel(recv_ref, items_ref, out_ref, pick_ref):
    rows = recv_ref.shape[1] - 16
    count = items_ref.shape[0]
    diagonal = iota((CAP, LANES), 0) == iota((CAP, LANES), 1)
    for j in range(PLANE):
        digits = recv_ref[j, rows : rows + 16, :].astype(F32)
        asked = 32.0 * digits[0:1] + digits[1:2]
        column = jnp.sum(
            jnp.where(diagonal, jnp.broadcast_to(asked, (CAP, LANES)), 0.0), axis=1, keepdims=True
        ).astype(I32)
        pick_ref[j * CAP : (j + 1) * CAP, :] = one_hot(column == iota((CAP, count), 1))
    step = 4
    for j in range(0, PLANE, step):
        served = dot(pick_ref[j * CAP : (j + step) * CAP, :], items_ref[...], ((1,), (0,)))
        served = served.astype(BF16)
        for i in range(step):
            out_ref[j + i] = served[i * CAP : (i + 1) * CAP]


def normalize(tokens_ref, normed_ref):
    step = 128
    for c in range(0, tokens_ref.shape[0], step):
        wide = tokens_ref[c : c + step, :].astype(F32)
        scale = lax.rsqrt(jnp.mean(wide * wide, axis=1, keepdims=True) + epsilon)
        normed_ref[c : c + step, :] = (wide * scale).astype(BF16)


def norm_kernel(core_ref, tokens_ref, mine_ref, other_ref, after_ref, normed_ref, w_all_ref):
    normalize(tokens_ref, normed_ref)
    core = core_ref[0]
    half = w_all_ref.shape[1] // 2
    for ref, part in ((mine_ref, core), (other_ref, 1 - core)):
        at = pl.multiple_of(part * half, half)
        for j in range(SECTIONS):
            w_all_ref[j, pl.ds(at, half), :] = ref[j, 0:half, :]


def forward_kernel(
    core_ref,
    lengths_ref,
    tokens_ref,
    mine_ref,
    other_ref,
    w_out_ref,
    layer_ref,
    gated_ref,
    normed,
    act,
):
    tok, width = tokens_ref.shape
    core = core_ref[0]
    half = width // 2
    step = 128
    normalize(tokens_ref, normed)
    left = normed[:, pl.ds(pl.multiple_of(core * half, half), half)]
    right = normed[:, pl.ds(pl.multiple_of((1 - core) * half, half), half)]
    for j in range(0, SECTIONS, 2):
        w_left = jnp.concatenate([mine_ref[j, 0:half, :], mine_ref[j + 1, 0:half, :]], axis=1)
        w_right = jnp.concatenate([other_ref[j, 0:half, :], other_ref[j + 1, 0:half, :]], axis=1)
        pre = dot(left, w_left, ((1,), (0,))) + dot(right, w_right, ((1,), (0,)))
        pair = (pre * jax.nn.sigmoid(pre)).astype(BF16)
        act[j] = pair[:, 0:DH]
        act[j + 1] = pair[:, DH:]
    end_0 = lengths_ref[0, 0]
    end_1 = end_0 + lengths_ref[0, 1]
    end_2 = end_1 + lengths_ref[0, 2]
    for c in range(0, tok, step):
        seen = c + step
        row = iota((step, 1), 0) + c
        start = jnp.where(row >= end_0, end_0, 0)
        start = jnp.where(row >= end_1, end_1, start)
        start = jnp.where(row >= end_2, end_2, start)
        col = iota((step, seen), 1)
        visible = (col <= row) & (col >= start)
        heads = []
        total = jnp.zeros((step, 1), F32)
        for h in range(HEADS):
            values = act[HEADS + h, 0:seen, :]
            queries = act[2 * HEADS + h, c:seen, :]
            keys = act[3 * HEADS + h, 0:seen, :]
            scores = dot(queries, keys, ((1,), (1,))) * DH ** (-0.5)
            silu = scores * jax.nn.sigmoid(scores) * (1.0 / MAXLEN)
            weights = jnp.where(visible, silu, 0.0).astype(BF16)
            joined = dot(weights, values, ((1,), (0,))).astype(BF16).astype(F32)
            total = total + jnp.sum(joined * joined, axis=1, keepdims=True)
            heads.append(joined)
        scale = lax.rsqrt(total * (1.0 / width) + epsilon)
        out = tokens_ref[c:seen, :].astype(F32)
        for h in range(HEADS):
            gated = (heads[h] * scale * act[h, c:seen, :].astype(F32)).astype(BF16)
            gated_ref[h, c:seen, :] = gated
            out = out + dot(gated, w_out_ref[h * DH : (h + 1) * DH, :], ((1,), (0,)))
        layer_ref[c:seen, :] = out


def loss_kernel(
    core_ref,
    layer_ref,
    gated_ref,
    recv_ref,
    mine_ref,
    other_ref,
    pos_ref,
    out_ref,
    grad_ref,
    grad_b_ref,
    fetched,
    decoys,
    probs,
    unit,
    back,
):
    tok = layer_ref.shape[0]
    part = NEG // 2
    rows = mine_ref.shape[1] - 16 - BLOCKS * part
    for j in range(PLANE):
        fetched[j * CAP : (j + 1) * CAP, :] = recv_ref[j]
        for ref, half in ((mine_ref, core_ref[0]), (other_ref, 1 - core_ref[0])):
            at = pl.multiple_of(j * NEG + half * part, part)
            for q in range(BLOCKS):
                block = ref[j, rows + q * part : rows + (q + 1) * part, :]
                decoys[pl.ds(at, part), q * LANES : (q + 1) * LANES] = block
    step = 128
    for c in range(0, tok, step):
        layer_out = layer_ref[c : c + step, :]
        placed = one_hot(pos_ref[c : c + step, :] == iota((step, PLANE * CAP), 1))
        clicked = dot(placed, fetched[...], ((1,), (0,)))
        out_scale = lax.rsqrt(jnp.sum(layer_out * layer_out, axis=1, keepdims=True) + epsilon)
        unit_b = (layer_out * out_scale).astype(BF16)
        unit[c : c + step, :] = unit_b
        unit_wide = unit_b.astype(F32)
        target_exp = jnp.exp(jnp.sum(unit_wide * clicked, axis=1, keepdims=True) * logit_scale)
        negative_exp = jnp.exp(dot(unit_b, decoys[...], ((1,), (1,))) * logit_scale)
        totals = target_exp + jnp.sum(negative_exp, axis=1, keepdims=True)
        negative_probs = (negative_exp * (loss_scale / totals)).astype(BF16)
        probs[c : c + step, :] = negative_probs
        target_coef = loss_scale * (target_exp / totals - 1.0)
        back[c : c + step, :] = (target_coef * unit_wide).astype(BF16)
        grad_unit = target_coef * clicked + dot(negative_probs, decoys[...], ((1,), (0,)))
        along = jnp.sum(layer_out * grad_unit, axis=1, keepdims=True)
        grad_out = out_scale * grad_unit - layer_out * (out_scale**3 * along)
        grad_ref[c : c + step, :] = grad_out
        grad_b_ref[c : c + step, :] = grad_out.astype(BF16)
    across = jnp.broadcast_to(pos_ref[...].astype(F32), (tok, LANES)).T[0:1, :].astype(I32)
    group = 4
    for j in range(0, PLANE, group):
        slots = group * CAP
        placed_t = one_hot(iota((slots, tok), 0) + j * CAP == across)
        sent = dot(placed_t, back[...], ((1,), (0,))).astype(BF16)
        negs = dot(probs[:, j * NEG : (j + group) * NEG], unit[...], ((0,), (0,))).astype(BF16)
        weights = dot(gated_ref[j // group], grad_b_ref[...], ((0,), (0,))).astype(BF16)
        for i in range(group):
            out_ref[j + i, 0:CAP, :] = sent[i * CAP : (i + 1) * CAP]
            out_ref[j + i, CAP : CAP + NEG, :] = negs[i * NEG : (i + 1) * NEG]
            out_ref[j + i, CAP + NEG :, :] = weights[i * WROWS : (i + 1) * WROWS]


def half_sums(half, pick_ref, neg_row_ref, returned, negs, weights, ref):
    step = 256
    for b in range(0, HALF, step):
        first = pl.multiple_of(half * HALF + b, step)
        here = one_hot(iota((step, NEG), 0) + first == neg_row_ref[...])
        total = dot(pick_ref[:, pl.ds(first, step)], returned[...], ((0,), (0,)))
        total = total + dot(here, negs, ((1,), (0,)))
        ref[b : b + step, :] = total.astype(BF16)
    part = jnp.where(half == 0, weights[0:SHARED], weights[SHARED:])
    ref[HALF:, :] = part.astype(BF16)


def send_kernel(
    core_ref, recv_ref, pick_ref, neg_row_ref, send_ref, returned, negs_ref, weights_ref
):
    negs = jnp.zeros((NEG, D), F32)
    weights = jnp.zeros((WROWS, D), F32)
    for j in range(PLANE):
        returned[j * CAP : (j + 1) * CAP, :] = recv_ref[j, 0:CAP, :]
        negs = negs + recv_ref[j, CAP : CAP + NEG, :].astype(F32)
        weights = weights + recv_ref[j, CAP + NEG :, :].astype(F32)
    negs = negs.astype(BF16)
    negs_ref[...] = negs
    weights_ref[...] = weights
    half_sums(1 - core_ref[0], pick_ref, neg_row_ref, returned, negs, weights, send_ref)


def keep_kernel(
    core_ref, pick_ref, neg_row_ref, returned, negs_ref, weights_ref, keep_ref
):
    negs, weights = negs_ref[...], weights_ref[...]
    half_sums(core_ref[0], pick_ref, neg_row_ref, returned, negs, weights, keep_ref)


def near_kernel(keep_ref, other_ref, out_ref):
    rows = HALF // NEAR
    weights = (keep_ref[HALF:, :].astype(F32) + other_ref[HALF:, :].astype(F32)).astype(BF16)
    for i in range(NEAR):
        at = slice(i * rows, (i + 1) * rows)
        total = keep_ref[at, :].astype(F32) + other_ref[at, :].astype(F32)
        out_ref[i, 0:rows, :] = total.astype(BF16)
        out_ref[i, rows:, :] = weights


def far_kernel(recv_ref, out_ref):
    rows = recv_ref.shape[1] - SHARED
    total = recv_ref[0].astype(F32)
    for i in range(1, NEAR):
        total = total + recv_ref[i].astype(F32)
    total = total.astype(BF16)
    for i in range(FAR):
        out_ref[i, 0:PIECE, :] = total[i * PIECE : (i + 1) * PIECE]
        out_ref[i, PIECE:, :] = total[rows:]


def total_kernel(recv_ref, out_ref, weights_ref):
    total = recv_ref[0].astype(F32)
    for i in range(1, FAR):
        total = total + recv_ref[i].astype(F32)
    total = total.astype(BF16)
    for i in range(CHIPS):
        out_ref[i] = total[0:PIECE]
    weights_ref[...] = total[PIECE:]


def weight_kernel(place_ref, mine_ref, other_ref, out_ref):
    core, plane = place_ref[0], place_ref[1]
    for ref, half in ((mine_ref, core), (other_ref, 1 - core)):
        for n, bits in enumerate(CHAIN_BITS):
            for p in range(PLANE):
                mask = sum(bit for k, bit in enumerate(bits) if p >> k & 1)
                at = (plane ^ mask) * WROWS + half * SHARED + n * (SHARED // 2)
                first = (n * PLANE + p) * (SHARED // 2)
                rows = ref[first : first + SHARED // 2, :].astype(F32)
                out_ref[pl.ds(pl.multiple_of(at, 8), SHARED // 2), :] = rows * (1.0 / loss_scale)


def finish_kernel(half_ref, grads_ref, items_ref, *rest):
    out_ref = rest[-1]
    for i in range(CHIPS):
        first = (i % NEAR) * (HALF // NEAR) + (i // NEAR) * PIECE
        rows = items_ref[first : first + PIECE, :].astype(F32)
        grads = grads_ref[i].astype(F32)
        scale = lax.rsqrt(jnp.sum(rows * rows, axis=1, keepdims=True) + epsilon)
        along = jnp.sum(rows * grads, axis=1, keepdims=True)
        out_ref[first : first + PIECE, :] = (scale * grads - rows * (scale**3 * along)) * (
            1.0 / loss_scale
        )


def finish(half, grads, items, earlier=None):
    count, width = items.shape
    half_block = pl.BlockSpec((HALF, width), lambda i, half_ref: (half_ref[0], 0))
    operands = [half.reshape(1), grads, items]
    in_specs = [pl.BlockSpec(memory_space=pltpu.VMEM), half_block]
    aliases = {}
    if earlier is not None:
        operands.append(earlier)
        in_specs.append(pl.BlockSpec(memory_space=pl.ANY))
        aliases = {3: 0}
    return pl.pallas_call(
        finish_kernel,
        out_shape=jax.ShapeDtypeStruct((count, width), F32),
        grid_spec=pltpu.PrefetchScalarGridSpec(
            num_scalar_prefetch=1, grid=(1,), in_specs=in_specs, out_specs=half_block
        ),
        input_output_aliases=aliases,
        compiler_params=pltpu.CompilerParams(vmem_limit_bytes=GRANT),
        cost_estimate=pl.CostEstimate(flops=0, bytes_accessed=1 << 21, transcendentals=0),
        name="finish",
    )(*operands)


def local(kernel, outs, operands, scalars=0, scratch=(), grant=GRANT):
    spaces = [pltpu.SMEM] * scalars + [pltpu.VMEM] * (len(operands) - scalars)
    moved = sum(v.size * v.dtype.itemsize for v in operands) + sum(
        v.size * v.dtype.itemsize for v in outs
    )
    return pl.pallas_call(
        kernel,
        out_shape=tuple(outs),
        in_specs=[pl.BlockSpec(memory_space=s) for s in spaces],
        out_specs=tuple(pl.BlockSpec(memory_space=pltpu.VMEM) for _ in outs),
        scratch_shapes=list(scratch),
        compiler_params=pltpu.CompilerParams(vmem_limit_bytes=grant),
        cost_estimate=pl.CostEstimate(flops=0, bytes_accessed=moved, transcendentals=0),
    )(*operands)


def shaped(shape, dtype=BF16):
    return jax.ShapeDtypeStruct(shape, dtype)


def shards(tokens, w_proj, w_out, item_rows, lengths, target_owner, target_row, negative_rows):
    tok_rows = tokens.shape[0]
    width = tokens.shape[1]
    item_count = item_rows.shape[0]
    dp = lax.axis_size("dp")
    slots = PLANE * CAP
    negs = PLANE * NEG
    partners = [(i, i ^ 1) for i in range(dp)]
    columns = [[2 * z + c for z in range(CHIPS)] for c in range(2)]
    near = [[2 * (NEAR * h + l) + c for l in range(NEAR)] for h in range(FAR) for c in range(2)]
    far = [[2 * (NEAR * h + l) + c for h in range(FAR)] for l in range(NEAR) for c in range(2)]
    core = lax.rem(lax.axis_index("dp"), 2).astype(I32)
    core_s = core.reshape(1)
    plane = lax.axis_index("shard").astype(I32)

    half_w = width // 2
    index = jnp.concatenate([target_owner[:, 0], target_row, negative_rows]).reshape(1, -1)
    first_out, position = local(
        route_kernel,
        [
            shaped((PLANE, half_w + BLOCKS * NEG // 2 + 16, DH)),
            shaped((tok_rows, 1), I32),
        ],
        [core_s, index, w_proj, item_rows],
        scalars=1,
        grant=WIDE_GRANT,
    )
    first_in = exchange(first_out, "shard")

    rows_wide = item_rows.astype(F32)
    item_scale = lax.rsqrt(jnp.sum(rows_wide * rows_wide, axis=1, keepdims=True) + epsilon)
    unit_items = (rows_wide * item_scale).astype(BF16)
    first_in, unit_items = lax.optimization_barrier((first_in, unit_items))
    served, asked_pick = local(
        serve_kernel,
        [shaped((PLANE, CAP, width)), shaped((slots, item_count))],
        [first_in, unit_items],
        grant=WIDE_GRANT,
    )
    served, first_mine = lax.optimization_barrier((served, first_in))
    looked_up = exchange(served, "shard")
    first_other = lax.ppermute(first_mine, "dp", partners)
    layer_out, gated = local(
        forward_kernel,
        [
            shaped((tok_rows, width), F32),
            shaped((HEADS, tok_rows, DH)),
        ],
        [core_s, lengths, tokens, first_mine, first_other, w_out],
        scalars=2,
        scratch=[
            pltpu.VMEM((tok_rows, width), BF16),
            pltpu.VMEM((SECTIONS, tok_rows, DH), BF16),
        ],
        grant=56 * 1024 * 1024,
    )

    third_out, grad_out, grad_out_b = local(
        loss_kernel,
        [
            shaped((PLANE, CAP + NEG + WROWS, width)),
            shaped((tok_rows, width), F32),
            shaped((tok_rows, width)),
        ],
        [core_s, layer_out, gated, looked_up, first_mine, first_other, position],
        scalars=1,
        scratch=[
            pltpu.VMEM((slots, width), BF16),
            pltpu.VMEM((negs, width), BF16),
            pltpu.VMEM((tok_rows, negs), BF16),
            pltpu.VMEM((tok_rows, width), BF16),
            pltpu.VMEM((tok_rows, width), BF16),
        ],
        grant=56 * 1024 * 1024,
    )
    third_in = exchange(third_out, "shard")

    normed, w_all = local(
        norm_kernel,
        [shaped((tok_rows, width)), shaped((SECTIONS, width, DH))],
        [core_s, tokens, first_mine, first_other, grad_out_b],
        scalars=1,
    )
    grad_out_b, w_all, normed, tokens = lax.optimization_barrier(
        (grad_out_b, w_all, normed, tokens)
    )
    visible = history_mask(lengths[0], tok_rows)[None]
    wide_tokens = tokens.astype(F32)
    input_scale = lax.rsqrt(jnp.mean(wide_tokens * wide_tokens, axis=1, keepdims=True) + epsilon)
    normed_s = jnp.broadcast_to(normed[None], (SECTIONS, tok_rows, width))
    pre_act = dot(normed_s, w_all, ((2,), (1,)), ((0,), (0,)))
    activated = jax.nn.silu(pre_act).astype(BF16)
    gate, values, queries, keys = (activated[i * HEADS : (i + 1) * HEADS] for i in range(4))
    scores = dot(queries, keys, ((2,), (2,)), ((0,), (0,))) * DH ** (-0.5)
    score_sig = jax.nn.sigmoid(scores)
    weights = jnp.where(visible, scores * score_sig * (1.0 / MAXLEN), 0.0).astype(BF16)
    joined = dot(weights, values, ((2,), (1,)), ((0,), (0,))).astype(BF16)
    joined_wide = joined.astype(F32)
    middle_scale = lax.rsqrt(
        jnp.sum(joined_wide * joined_wide, axis=(0, 2), keepdims=True) / width + epsilon
    )
    gate_wide = gate.astype(F32)
    w_out_h = w_out.reshape(HEADS, DH, width)
    grad_gated = dot(
        jnp.broadcast_to(grad_out_b[None], (HEADS, tok_rows, width)),
        w_out_h,
        ((2,), (2,)),
        ((0,), (0,)),
    )
    grad_gate = grad_gated * joined_wide * middle_scale
    grad_norm = grad_gated * gate_wide
    grad_joined = middle_scale * grad_norm - joined_wide * middle_scale**3 * (
        jnp.sum(joined_wide * grad_norm, axis=(0, 2), keepdims=True) / width
    )
    grad_joined_b = grad_joined.astype(BF16)
    grad_weights = dot(grad_joined_b, values, ((2,), (2,)), ((0,), (0,)))
    grad_values = dot(weights, grad_joined_b, ((1,), (1,)), ((0,), (0,)))
    slope = score_sig * (1.0 + scores * (1.0 - score_sig))
    grad_scores = jnp.where(
        visible, grad_weights * (1.0 / MAXLEN) * slope * DH ** (-0.5), 0.0
    ).astype(BF16)
    grad_queries = dot(grad_scores, keys, ((2,), (1,)), ((0,), (0,)))
    grad_keys = dot(grad_scores, queries, ((1,), (1,)), ((0,), (0,)))
    grad_act = jnp.concatenate([grad_gate, grad_values, grad_queries, grad_keys], axis=0)
    grad_pre = (grad_act * silu_slope(pre_act)).astype(BF16)
    grad_normed = jnp.sum(dot(grad_pre, w_all, ((2,), (2,)), ((0,), (0,))), axis=0)
    grad_input = input_scale * grad_normed - wide_tokens * input_scale**3 * jnp.mean(
        wide_tokens * grad_normed, axis=1, keepdims=True
    )
    grad_tokens = (grad_out + grad_input).astype(BF16)
    third_in, grad_tokens = lax.optimization_barrier((third_in, grad_tokens))

    neg_row = negative_rows.reshape(1, NEG)
    sent, returned, neg_sum, w_sum = local(
        send_kernel,
        [
            shaped((HALF + SHARED, width)),
            shaped((slots, width)),
            shaped((NEG, width)),
            shaped((WROWS, width), F32),
        ],
        [core_s, third_in, asked_pick, neg_row],
        scalars=1,
    )
    arrived = lax.ppermute(sent, "dp", partners)
    (kept,) = local(
        keep_kernel,
        [shaped((HALF + SHARED, width))],
        [core_s, asked_pick, neg_row, returned, neg_sum, w_sum],
        scalars=1,
    )
    (near_out,) = local(
        near_kernel, [shaped((NEAR, HALF // NEAR + SHARED, width))], [kept, arrived]
    )
    (far_out,) = local(
        far_kernel, [shaped((FAR, PIECE + SHARED, width))], [exchange(near_out, "dp", near)]
    )
    summed, w_rows = local(
        total_kernel,
        [shaped((CHIPS, PIECE, width)), shaped((SHARED, width))],
        [exchange(far_out, "dp", far)],
    )
    mine = exchange(summed, "dp", columns)

    chains = [w_rows[: SHARED // 2], w_rows[SHARED // 2 :]]
    for k in range(4):
        for n, bits in enumerate(CHAIN_BITS):
            others = lax.ppermute(
                chains[n], "shard", [(i, i ^ bits[k]) for i in range(PLANE)]
            )
            chains[n] = jnp.concatenate([chains[n], others], axis=0)
    w_rows = jnp.concatenate(chains, axis=0)
    mine, w_rows = lax.optimization_barrier((mine, w_rows))
    w_other_rows = lax.ppermute(w_rows, "dp", partners)
    (weight_grads,) = local(
        weight_kernel,
        [shaped((width, width), F32)],
        [jnp.stack([core, plane]), w_rows, w_other_rows],
        scalars=1,
    )
    other = lax.ppermute(mine, "dp", partners)
    item_grads = finish(1 - core, other, item_rows, finish(core, mine, item_rows))
    return (grad_tokens, weight_grads, item_grads)


def solution(mesh):
    in_specs = (
        P(("dp", "shard"), None),
        P(None, "shard"),
        P(),
        P("shard", None),
        P(("dp", "shard"), None),
        P(("dp", "shard"), None),
        P(("dp", "shard")),
        P("shard"),
    )
    out_specs = (P(("dp", "shard"), None), P(), P("shard", None))
    return jax.shard_map(
        shards, mesh=mesh, in_specs=in_specs, out_specs=out_specs, check_vma=False
    )
```

```python
import jax
import jax.numpy as jnp
from jax import lax
from jax.experimental import pallas as pl
from jax.experimental.pallas import tpu as pltpu
from jax.sharding import PartitionSpec as P

D = 512
HEADS = 4
DH = 128
MAXLEN = 192
SECTIONS = 4 * HEADS
PLANE = 16
CAP = 48
NEG = 64
WROWS = 32
CHIPS = 16
NEAR = 4
FAR = 4
HALF = 512
PIECE = 32
SHARED = 16
LANES = 128
BLOCKS = D // LANES
GRANT = 24 * 1024 * 1024
WIDE_GRANT = 56 * 1024 * 1024

epsilon = 1e-06
logit_scale = 64.0
loss_scale = 512.0

F32 = jnp.float32
BF16 = jnp.bfloat16
I32 = jnp.int32


def dot(a, b, contract, batch=((), ())):
    return lax.dot_general(a, b, (contract, batch), preferred_element_type=F32)


def iota(shape, axis):
    return lax.broadcasted_iota(I32, shape, axis)


def one_hot(mask):
    return jnp.where(mask, 1.0, 0.0).astype(BF16)


def silu_slope(values):
    sigmoid = jax.nn.sigmoid(values)
    return sigmoid * (1.0 + values * (1.0 - sigmoid))


def history_mask(lengths_row, rows_count):
    history_ends = jnp.cumsum(lengths_row)
    positions = jnp.arange(rows_count, dtype=jnp.int32)
    history_ids = jnp.sum((positions[:, None] >= history_ends[None, :-1]).astype(jnp.int32), axis=1)
    return (history_ids[:, None] == history_ids[None, :]) & (
        positions[None, :] <= positions[:, None]
    )


def exchange(pieces, axis, groups=None):
    return lax.all_to_all(
        pieces, axis, split_axis=0, concat_axis=0, tiled=True, axis_index_groups=groups
    )


def route_kernel(core_ref, index_ref, w_ref, items_ref, out_ref, pos_ref):
    tok = pos_ref.shape[0]
    first = core_ref[0] == 0
    owners = jnp.broadcast_to(index_ref[0:1, 0:tok].astype(F32), (LANES, tok)).T.astype(I32)
    hits = owners == iota((tok, LANES), 1)
    earlier = one_hot(iota((tok, tok), 1) < iota((tok, tok), 0))
    before = dot(earlier, one_hot(hits), ((1,), (0,)))
    slot = jnp.sum(jnp.where(hits, before, 0.0), axis=1, keepdims=True).astype(I32)
    owners = owners[:, 0:1]
    pos_ref[...] = owners * CAP + slot
    spread = one_hot(owners * LANES + slot == iota((tok, PLANE * LANES), 1))
    asked = jnp.broadcast_to(index_ref[0:1, tok : 2 * tok], (16, tok))
    which = iota((16, tok), 0)
    digits = jnp.where(which == 0, asked >> 5, jnp.where(which == 1, asked & 31, 0))
    requests = dot(digits.astype(F32).astype(BF16), spread, ((1,), (0,))).astype(BF16)
    here = one_hot(iota((items_ref.shape[0], NEG), 0) == index_ref[0:1, 2 * tok :])
    negs = dot(here, items_ref[...], ((0,), (0,)))
    negs = jnp.where(first, negs[0 : NEG // 2], negs[NEG // 2 :])
    scale = lax.rsqrt(jnp.sum(negs * negs, axis=1, keepdims=True) + epsilon)
    negs = (negs * scale).astype(BF16)
    rows = w_ref.shape[0] // 2
    own = w_ref[pl.ds(pl.multiple_of(core_ref[0] * rows, rows), rows), :]
    for j in range(PLANE):
        out_ref[j, 0:rows, :] = own
        for q in range(BLOCKS):
            at = rows + q * (NEG // 2)
            out_ref[j, at : at + NEG // 2, :] = negs[:, q * LANES : (q + 1) * LANES]
        at = rows + BLOCKS * (NEG // 2)
        out_ref[j, at : at + 16, :] = requests[:, j * LANES : (j + 1) * LANES]


def serve_kernel(recv_ref, items_ref, out_ref, pick_ref):
    rows = recv_ref.shape[1] - 16
    count = items_ref.shape[0]
    diagonal = iota((CAP, LANES), 0) == iota((CAP, LANES), 1)
    for j in range(PLANE):
        digits = recv_ref[j, rows : rows + 16, :].astype(F32)
        asked = 32.0 * digits[0:1] + digits[1:2]
        column = jnp.sum(
            jnp.where(diagonal, jnp.broadcast_to(asked, (CAP, LANES)), 0.0), axis=1, keepdims=True
        ).astype(I32)
        pick_ref[j * CAP : (j + 1) * CAP, :] = one_hot(column == iota((CAP, count), 1))
    step = 4
    for j in range(0, PLANE, step):
        served = dot(pick_ref[j * CAP : (j + step) * CAP, :], items_ref[...], ((1,), (0,)))
        served = served.astype(BF16)
        for i in range(step):
            out_ref[j + i] = served[i * CAP : (i + 1) * CAP]


def normalize(tokens_ref, normed_ref):
    step = 128
    for c in range(0, tokens_ref.shape[0], step):
        wide = tokens_ref[c : c + step, :].astype(F32)
        scale = lax.rsqrt(jnp.mean(wide * wide, axis=1, keepdims=True) + epsilon)
        normed_ref[c : c + step, :] = (wide * scale).astype(BF16)


def norm_kernel(core_ref, tokens_ref, mine_ref, other_ref, after_ref, normed_ref, w_all_ref):
    normalize(tokens_ref, normed_ref)
    core = core_ref[0]
    half = w_all_ref.shape[1] // 2
    for ref, part in ((mine_ref, core), (other_ref, 1 - core)):
        at = pl.multiple_of(part * half, half)
        for j in range(SECTIONS):
            w_all_ref[j, pl.ds(at, half), :] = ref[j, 0:half, :]


def forward_kernel(
    core_ref,
    lengths_ref,
    tokens_ref,
    mine_ref,
    other_ref,
    w_out_ref,
    layer_ref,
    gated_ref,
    normed,
    act,
):
    tok, width = tokens_ref.shape
    core = core_ref[0]
    half = width // 2
    step = 128
    normalize(tokens_ref, normed)
    left = normed[:, pl.ds(pl.multiple_of(core * half, half), half)]
    right = normed[:, pl.ds(pl.multiple_of((1 - core) * half, half), half)]
    for j in range(0, SECTIONS, 2):
        w_left = jnp.concatenate([mine_ref[j, 0:half, :], mine_ref[j + 1, 0:half, :]], axis=1)
        w_right = jnp.concatenate([other_ref[j, 0:half, :], other_ref[j + 1, 0:half, :]], axis=1)
        pre = dot(left, w_left, ((1,), (0,))) + dot(right, w_right, ((1,), (0,)))
        pair = (pre * jax.nn.sigmoid(pre)).astype(BF16)
        act[j] = pair[:, 0:DH]
        act[j + 1] = pair[:, DH:]
    end_0 = lengths_ref[0, 0]
    end_1 = end_0 + lengths_ref[0, 1]
    end_2 = end_1 + lengths_ref[0, 2]
    for c in range(0, tok, step):
        seen = c + step
        row = iota((step, 1), 0) + c
        start = jnp.where(row >= end_0, end_0, 0)
        start = jnp.where(row >= end_1, end_1, start)
        start = jnp.where(row >= end_2, end_2, start)
        col = iota((step, seen), 1)
        visible = (col <= row) & (col >= start)
        heads = []
        total = jnp.zeros((step, 1), F32)
        for h in range(HEADS):
            values = act[HEADS + h, 0:seen, :]
            queries = act[2 * HEADS + h, c:seen, :]
            keys = act[3 * HEADS + h, 0:seen, :]
            scores = dot(queries, keys, ((1,), (1,))) * DH ** (-0.5)
            silu = scores * jax.nn.sigmoid(scores) * (1.0 / MAXLEN)
            weights = jnp.where(visible, silu, 0.0).astype(BF16)
            joined = dot(weights, values, ((1,), (0,))).astype(BF16).astype(F32)
            total = total + jnp.sum(joined * joined, axis=1, keepdims=True)
            heads.append(joined)
        scale = lax.rsqrt(total * (1.0 / width) + epsilon)
        out = tokens_ref[c:seen, :].astype(F32)
        for h in range(HEADS):
            gated = (heads[h] * scale * act[h, c:seen, :].astype(F32)).astype(BF16)
            gated_ref[h, c:seen, :] = gated
            out = out + dot(gated, w_out_ref[h * DH : (h + 1) * DH, :], ((1,), (0,)))
        layer_ref[c:seen, :] = out


def loss_kernel(
    core_ref,
    layer_ref,
    gated_ref,
    recv_ref,
    mine_ref,
    other_ref,
    pos_ref,
    out_ref,
    grad_ref,
    grad_b_ref,
    fetched,
    decoys,
    probs,
    unit,
    back,
):
    tok = layer_ref.shape[0]
    part = NEG // 2
    rows = mine_ref.shape[1] - 16 - BLOCKS * part
    for j in range(PLANE):
        fetched[j * CAP : (j + 1) * CAP, :] = recv_ref[j]
        for ref, half in ((mine_ref, core_ref[0]), (other_ref, 1 - core_ref[0])):
            at = pl.multiple_of(j * NEG + half * part, part)
            for q in range(BLOCKS):
                block = ref[j, rows + q * part : rows + (q + 1) * part, :]
                decoys[pl.ds(at, part), q * LANES : (q + 1) * LANES] = block
    step = 128
    for c in range(0, tok, step):
        layer_out = layer_ref[c : c + step, :]
        placed = one_hot(pos_ref[c : c + step, :] == iota((step, PLANE * CAP), 1))
        clicked = dot(placed, fetched[...], ((1,), (0,)))
        out_scale = lax.rsqrt(jnp.sum(layer_out * layer_out, axis=1, keepdims=True) + epsilon)
        unit_b = (layer_out * out_scale).astype(BF16)
        unit[c : c + step, :] = unit_b
        unit_wide = unit_b.astype(F32)
        target_exp = jnp.exp(jnp.sum(unit_wide * clicked, axis=1, keepdims=True) * logit_scale)
        negative_exp = jnp.exp(dot(unit_b, decoys[...], ((1,), (1,))) * logit_scale)
        totals = target_exp + jnp.sum(negative_exp, axis=1, keepdims=True)
        negative_probs = (negative_exp * (loss_scale / totals)).astype(BF16)
        probs[c : c + step, :] = negative_probs
        target_coef = loss_scale * (target_exp / totals - 1.0)
        back[c : c + step, :] = (target_coef * unit_wide).astype(BF16)
        grad_unit = target_coef * clicked + dot(negative_probs, decoys[...], ((1,), (0,)))
        along = jnp.sum(layer_out * grad_unit, axis=1, keepdims=True)
        grad_out = out_scale * grad_unit - layer_out * (out_scale**3 * along)
        grad_ref[c : c + step, :] = grad_out
        grad_b_ref[c : c + step, :] = grad_out.astype(BF16)
    across = jnp.broadcast_to(pos_ref[...].astype(F32), (tok, LANES)).T[0:1, :].astype(I32)
    group = 4
    for j in range(0, PLANE, group):
        slots = group * CAP
        placed_t = one_hot(iota((slots, tok), 0) + j * CAP == across)
        sent = dot(placed_t, back[...], ((1,), (0,))).astype(BF16)
        negs = dot(probs[:, j * NEG : (j + group) * NEG], unit[...], ((0,), (0,))).astype(BF16)
        weights = dot(gated_ref[j // group], grad_b_ref[...], ((0,), (0,))).astype(BF16)
        for i in range(group):
            out_ref[j + i, 0:CAP, :] = sent[i * CAP : (i + 1) * CAP]
            out_ref[j + i, CAP : CAP + NEG, :] = negs[i * NEG : (i + 1) * NEG]
            out_ref[j + i, CAP + NEG :, :] = weights[i * WROWS : (i + 1) * WROWS]


def half_sums(half, pick_ref, neg_row_ref, returned, negs, weights, ref):
    step = 256
    for b in range(0, HALF, step):
        first = pl.multiple_of(half * HALF + b, step)
        here = one_hot(iota((step, NEG), 0) + first == neg_row_ref[...])
        total = dot(pick_ref[:, pl.ds(first, step)], returned[...], ((0,), (0,)))
        total = total + dot(here, negs, ((1,), (0,)))
        ref[b : b + step, :] = total.astype(BF16)
    part = jnp.where(half == 0, weights[0:SHARED], weights[SHARED:])
    ref[HALF:, :] = part.astype(BF16)


def send_kernel(
    core_ref, recv_ref, pick_ref, neg_row_ref, send_ref, returned, negs_ref, weights_ref
):
    negs = jnp.zeros((NEG, D), F32)
    weights = jnp.zeros((WROWS, D), F32)
    for j in range(PLANE):
        returned[j * CAP : (j + 1) * CAP, :] = recv_ref[j, 0:CAP, :]
        negs = negs + recv_ref[j, CAP : CAP + NEG, :].astype(F32)
        weights = weights + recv_ref[j, CAP + NEG :, :].astype(F32)
    negs = negs.astype(BF16)
    negs_ref[...] = negs
    weights_ref[...] = weights
    half_sums(1 - core_ref[0], pick_ref, neg_row_ref, returned, negs, weights, send_ref)


def keep_kernel(
    core_ref, pick_ref, neg_row_ref, returned, negs_ref, weights_ref, keep_ref
):
    negs, weights = negs_ref[...], weights_ref[...]
    half_sums(core_ref[0], pick_ref, neg_row_ref, returned, negs, weights, keep_ref)


def near_kernel(keep_ref, other_ref, out_ref):
    rows = HALF // NEAR
    weights = (keep_ref[HALF:, :].astype(F32) + other_ref[HALF:, :].astype(F32)).astype(BF16)
    for i in range(NEAR):
        at = slice(i * rows, (i + 1) * rows)
        total = keep_ref[at, :].astype(F32) + other_ref[at, :].astype(F32)
        out_ref[i, 0:rows, :] = total.astype(BF16)
        out_ref[i, rows:, :] = weights


def far_kernel(recv_ref, out_ref):
    rows = recv_ref.shape[1] - SHARED
    total = recv_ref[0].astype(F32)
    for i in range(1, NEAR):
        total = total + recv_ref[i].astype(F32)
    total = total.astype(BF16)
    for i in range(FAR):
        out_ref[i, 0:PIECE, :] = total[i * PIECE : (i + 1) * PIECE]
        out_ref[i, PIECE:, :] = total[rows:]


def total_kernel(recv_ref, out_ref, weights_ref):
    total = recv_ref[0].astype(F32)
    for i in range(1, FAR):
        total = total + recv_ref[i].astype(F32)
    total = total.astype(BF16)
    for i in range(CHIPS):
        out_ref[i] = total[0:PIECE]
    weights_ref[...] = total[PIECE:]


def weight_kernel(place_ref, mine_ref, other_ref, out_ref):
    core, plane_y, plane_x = place_ref[0], place_ref[1], place_ref[2]
    for ref, half in ((mine_ref, core), (other_ref, 1 - core)):
        for ky in range(4):
            for kx in range(4):
                owner = ((plane_y - ky) & 3) * 4 + ((plane_x - kx) & 3)
                at = pl.multiple_of(owner * WROWS + half * SHARED, SHARED)
                first = (ky * 4 + kx) * SHARED
                rows = ref[first : first + SHARED, :].astype(F32)
                out_ref[pl.ds(at, SHARED), :] = rows * (1.0 / loss_scale)


def finish_kernel(half_ref, grads_ref, items_ref, *rest):
    out_ref = rest[-1]
    for i in range(CHIPS):
        first = (i % NEAR) * (HALF // NEAR) + (i // NEAR) * PIECE
        rows = items_ref[first : first + PIECE, :].astype(F32)
        grads = grads_ref[i].astype(F32)
        scale = lax.rsqrt(jnp.sum(rows * rows, axis=1, keepdims=True) + epsilon)
        along = jnp.sum(rows * grads, axis=1, keepdims=True)
        out_ref[first : first + PIECE, :] = (scale * grads - rows * (scale**3 * along)) * (
            1.0 / loss_scale
        )


def finish(half, grads, items, earlier=None):
    count, width = items.shape
    half_block = pl.BlockSpec((HALF, width), lambda i, half_ref: (half_ref[0], 0))
    operands = [half.reshape(1), grads, items]
    in_specs = [pl.BlockSpec(memory_space=pltpu.VMEM), half_block]
    aliases = {}
    if earlier is not None:
        operands.append(earlier)
        in_specs.append(pl.BlockSpec(memory_space=pl.ANY))
        aliases = {3: 0}
    return pl.pallas_call(
        finish_kernel,
        out_shape=jax.ShapeDtypeStruct((count, width), F32),
        grid_spec=pltpu.PrefetchScalarGridSpec(
            num_scalar_prefetch=1, grid=(1,), in_specs=in_specs, out_specs=half_block
        ),
        input_output_aliases=aliases,
        compiler_params=pltpu.CompilerParams(vmem_limit_bytes=GRANT),
        cost_estimate=pl.CostEstimate(flops=0, bytes_accessed=1 << 21, transcendentals=0),
        name="finish",
    )(*operands)


def local(kernel, outs, operands, scalars=0, scratch=(), grant=GRANT):
    spaces = [pltpu.SMEM] * scalars + [pltpu.VMEM] * (len(operands) - scalars)
    moved = sum(v.size * v.dtype.itemsize for v in operands) + sum(
        v.size * v.dtype.itemsize for v in outs
    )
    return pl.pallas_call(
        kernel,
        out_shape=tuple(outs),
        in_specs=[pl.BlockSpec(memory_space=s) for s in spaces],
        out_specs=tuple(pl.BlockSpec(memory_space=pltpu.VMEM) for _ in outs),
        scratch_shapes=list(scratch),
        compiler_params=pltpu.CompilerParams(vmem_limit_bytes=grant),
        cost_estimate=pl.CostEstimate(flops=0, bytes_accessed=moved, transcendentals=0),
    )(*operands)


def shaped(shape, dtype=BF16):
    return jax.ShapeDtypeStruct(shape, dtype)


def shards(tokens, w_proj, w_out, item_rows, lengths, target_owner, target_row, negative_rows):
    tok_rows = tokens.shape[0]
    width = tokens.shape[1]
    item_count = item_rows.shape[0]
    dp = lax.axis_size("dp")
    slots = PLANE * CAP
    negs = PLANE * NEG
    partners = [(i, i ^ 1) for i in range(dp)]
    columns = [[2 * z + c for z in range(CHIPS)] for c in range(2)]
    near = [[2 * (NEAR * h + l) + c for l in range(NEAR)] for h in range(FAR) for c in range(2)]
    far = [[2 * (NEAR * h + l) + c for h in range(FAR)] for l in range(NEAR) for c in range(2)]
    core = lax.rem(lax.axis_index("dp"), 2).astype(I32)
    core_s = core.reshape(1)
    plane = lax.axis_index("shard").astype(I32)

    half_w = width // 2
    index = jnp.concatenate([target_owner[:, 0], target_row, negative_rows]).reshape(1, -1)
    first_out, position = local(
        route_kernel,
        [
            shaped((PLANE, half_w + BLOCKS * NEG // 2 + 16, DH)),
            shaped((tok_rows, 1), I32),
        ],
        [core_s, index, w_proj, item_rows],
        scalars=1,
        grant=WIDE_GRANT,
    )
    first_in = exchange(first_out, "shard")

    rows_wide = item_rows.astype(F32)
    item_scale = lax.rsqrt(jnp.sum(rows_wide * rows_wide, axis=1, keepdims=True) + epsilon)
    unit_items = (rows_wide * item_scale).astype(BF16)
    first_in, unit_items = lax.optimization_barrier((first_in, unit_items))
    served, asked_pick = local(
        serve_kernel,
        [shaped((PLANE, CAP, width)), shaped((slots, item_count))],
        [first_in, unit_items],
        grant=WIDE_GRANT,
    )
    served, first_mine = lax.optimization_barrier((served, first_in))
    looked_up = exchange(served, "shard")
    first_other = lax.ppermute(first_mine, "dp", partners)
    layer_out, gated = local(
        forward_kernel,
        [
            shaped((tok_rows, width), F32),
            shaped((HEADS, tok_rows, DH)),
        ],
        [core_s, lengths, tokens, first_mine, first_other, w_out],
        scalars=2,
        scratch=[
            pltpu.VMEM((tok_rows, width), BF16),
            pltpu.VMEM((SECTIONS, tok_rows, DH), BF16),
        ],
        grant=24 * 1024 * 1024,
    )

    third_out, grad_out, grad_out_b = local(
        loss_kernel,
        [
            shaped((PLANE, CAP + NEG + WROWS, width)),
            shaped((tok_rows, width), F32),
            shaped((tok_rows, width)),
        ],
        [core_s, layer_out, gated, looked_up, first_mine, first_other, position],
        scalars=1,
        scratch=[
            pltpu.VMEM((slots, width), BF16),
            pltpu.VMEM((negs, width), BF16),
            pltpu.VMEM((tok_rows, negs), BF16),
            pltpu.VMEM((tok_rows, width), BF16),
            pltpu.VMEM((tok_rows, width), BF16),
        ],
        grant=24 * 1024 * 1024,
    )
    third_in = exchange(third_out, "shard")

    normed, w_all = local(
        norm_kernel,
        [shaped((tok_rows, width)), shaped((SECTIONS, width, DH))],
        [core_s, tokens, first_mine, first_other, grad_out_b],
        scalars=1,
    )
    grad_out_b, w_all, normed, tokens = lax.optimization_barrier(
        (grad_out_b, w_all, normed, tokens)
    )
    visible = history_mask(lengths[0], tok_rows)[None]
    wide_tokens = tokens.astype(F32)
    input_scale = lax.rsqrt(jnp.mean(wide_tokens * wide_tokens, axis=1, keepdims=True) + epsilon)
    normed_s = jnp.broadcast_to(normed[None], (SECTIONS, tok_rows, width))
    pre_act = dot(normed_s, w_all, ((2,), (1,)), ((0,), (0,)))
    activated = jax.nn.silu(pre_act).astype(BF16)
    gate, values, queries, keys = (activated[i * HEADS : (i + 1) * HEADS] for i in range(4))
    scores = dot(queries, keys, ((2,), (2,)), ((0,), (0,))) * DH ** (-0.5)
    score_sig = jax.nn.sigmoid(scores)
    weights = jnp.where(visible, scores * score_sig * (1.0 / MAXLEN), 0.0).astype(BF16)
    joined = dot(weights, values, ((2,), (1,)), ((0,), (0,))).astype(BF16)
    joined_wide = joined.astype(F32)
    middle_scale = lax.rsqrt(
        jnp.sum(joined_wide * joined_wide, axis=(0, 2), keepdims=True) / width + epsilon
    )
    gate_wide = gate.astype(F32)
    w_out_h = w_out.reshape(HEADS, DH, width)
    grad_gated = dot(
        jnp.broadcast_to(grad_out_b[None], (HEADS, tok_rows, width)),
        w_out_h,
        ((2,), (2,)),
        ((0,), (0,)),
    )
    grad_gate = grad_gated * joined_wide * middle_scale
    grad_norm = grad_gated * gate_wide
    grad_joined = middle_scale * grad_norm - joined_wide * middle_scale**3 * (
        jnp.sum(joined_wide * grad_norm, axis=(0, 2), keepdims=True) / width
    )
    grad_joined_b = grad_joined.astype(BF16)
    grad_weights = dot(grad_joined_b, values, ((2,), (2,)), ((0,), (0,)))
    grad_values = dot(weights, grad_joined_b, ((1,), (1,)), ((0,), (0,)))
    slope = score_sig * (1.0 + scores * (1.0 - score_sig))
    grad_scores = jnp.where(
        visible, grad_weights * (1.0 / MAXLEN) * slope * DH ** (-0.5), 0.0
    ).astype(BF16)
    grad_queries = dot(grad_scores, keys, ((2,), (1,)), ((0,), (0,)))
    grad_keys = dot(grad_scores, queries, ((1,), (1,)), ((0,), (0,)))
    grad_act = jnp.concatenate([grad_gate, grad_values, grad_queries, grad_keys], axis=0)
    grad_pre = (grad_act * silu_slope(pre_act)).astype(BF16)
    grad_normed = jnp.sum(dot(grad_pre, w_all, ((2,), (2,)), ((0,), (0,))), axis=0)
    grad_input = input_scale * grad_normed - wide_tokens * input_scale**3 * jnp.mean(
        wide_tokens * grad_normed, axis=1, keepdims=True
    )
    grad_tokens = (grad_out + grad_input).astype(BF16)
    third_in, grad_tokens = lax.optimization_barrier((third_in, grad_tokens))

    neg_row = negative_rows.reshape(1, NEG)
    sent, returned, neg_sum, w_sum = local(
        send_kernel,
        [
            shaped((HALF + SHARED, width)),
            shaped((slots, width)),
            shaped((NEG, width)),
            shaped((WROWS, width), F32),
        ],
        [core_s, third_in, asked_pick, neg_row],
        scalars=1,
    )
    arrived = lax.ppermute(sent, "dp", partners)
    (kept,) = local(
        keep_kernel,
        [shaped((HALF + SHARED, width))],
        [core_s, asked_pick, neg_row, returned, neg_sum, w_sum],
        scalars=1,
    )
    (near_out,) = local(
        near_kernel, [shaped((NEAR, HALF // NEAR + SHARED, width))], [kept, arrived]
    )
    (far_out,) = local(
        far_kernel, [shaped((FAR, PIECE + SHARED, width))], [exchange(near_out, "dp", near)]
    )
    summed, w_rows = local(
        total_kernel,
        [shaped((CHIPS, PIECE, width)), shaped((SHARED, width))],
        [exchange(far_out, "dp", far)],
    )
    mine = exchange(summed, "dp", columns)

    def turned(rows, step_y, step_x):
        moves = [
            (y * 4 + x, (y + step_y) % 4 * 4 + (x + step_x) % 4) for y in range(4) for x in range(4)
        ]
        return lax.ppermute(rows, "shard", moves)

    w_rows = jnp.concatenate([w_rows] + [turned(w_rows, 0, k) for k in (1, 2, 3)], axis=0)
    w_rows = jnp.concatenate([w_rows] + [turned(w_rows, k, 0) for k in (1, 2, 3)], axis=0)
    w_other_rows = lax.ppermute(w_rows, "dp", partners)
    other = lax.ppermute(mine, "dp", partners)
    item_grads = finish(1 - core, other, item_rows, finish(core, mine, item_rows))
    w_rows, w_other_rows, item_grads = lax.optimization_barrier((w_rows, w_other_rows, item_grads))
    (weight_grads,) = local(
        weight_kernel,
        [shaped((width, width), F32)],
        [jnp.stack([core, plane >> 2, plane & 3]), w_rows, w_other_rows],
        scalars=1,
    )
    return (grad_tokens, weight_grads, item_grads)


def solution(mesh):
    in_specs = (
        P(("dp", "shard"), None),
        P(None, "shard"),
        P(),
        P("shard", None),
        P(("dp", "shard"), None),
        P(("dp", "shard"), None),
        P(("dp", "shard")),
        P("shard"),
    )
    out_specs = (P(("dp", "shard"), None), P(), P("shard", None))
    return jax.shard_map(
        shards, mesh=mesh, in_specs=in_specs, out_specs=out_specs, check_vma=False
    )
```
